128 devices in a mesh: wake: 16 (over y_hi, x, core), grid: 8 (over z, y_lo).
Axes of the slice: x: 4, y: 4 (y_hi: 2, y_lo: 2; y = y_hi * 2 + y_lo), z: 4, core: 2. Of those that a mesh axis runs over, the one named last changes fastest.
Arguments:
- flow: float32 [5, 256, 131072], P(None, 'wake', 'grid'), may hold values from -6 to 6
- section_map: int32 [256, 131072], P('wake', 'grid'), may hold values from 0 to 2
- viscosity: float32 [3, 5], replicated, may hold values from 0.12 to 0.24
- particle_position: float32 [3, 32768], P(None, ('wake', 'grid')), may hold values from 0 to 1
- particle_strength: float32 [3, 32768], P(None, ('wake', 'grid')), may hold values from -0.6 to 0.6
- particle_core: float32 [32768], P(('wake', 'grid')), may hold values from 0.08 to 0.16
- shed_counts: int32 [16], replicated, may hold values from 512 to 2048, as said below
- node_position: float32 [3, 131072], P(None, ('wake', 'grid')), may hold values from 0 to 1
- node_block: int32 [131072, 1], P(('wake', 'grid')), may hold values from 0 to 15; in each aligned block of 1024 rows (0 to 1023, 1024 to 2047, ...) at most 128 rows name the same one
Outputs:
- flow_out: float32 [5, 256, 131072], P(None, 'wake', 'grid')
- particle_velocity: float32 [3, 32768], P(None, ('wake', 'grid'))
- particle_stretching: float32 [3, 32768], P(None, ('wake', 'grid'))
The draws below stay inside these ranges and needn't reach their ends.
Inputs may be any that keep to these rules, and one draw needn't show every extreme that they name: `shed_counts`: at least one block holds 2048 live particles. `node_block`: among the 1024 nodes of one device (aligned blocks of nodes), at most 128 name any one block, and some block is named by exactly 128.
All inputs are finite; a program needn't handle non-finite values.
Results may differ from the reference program's by a relative error of at most 0.0003.
Values sent between devices are 32-bit elements; how exact they have to be, the bound alone decides.
A program may use at most 192 MiB of HBM per device.

```python
import math
import jax
import jax.numpy as jnp
import numpy as np
from jax import lax

NSEC = 3
CY = 16
CZ = 16384
NODE_Z = 64
PB = 2048
SWEEPS = 3
STOPS = 8
NPART = 32768
NODE_DEV = 1024
NODES = 131072
CAP = 128
GY = 256
GZ = 131072
N_WAKE = 16
N_GRID = 8


def draw_shed_counts(key, part):
    first = jax.random.fold_in(key, 11)
    second = jax.random.fold_in(key, 23)
    counts = jax.random.randint(first, (N_WAKE,), PB // 4, PB + 1)
    full = jax.random.randint(second, (), 0, N_WAKE)
    return jnp.where(jnp.arange(N_WAKE) == full, PB, counts).astype(jnp.int32)


def set_ends(values, stream_key, low, top_value):
    longest = values.shape.index(max(values.shape))
    spots = []
    for shift in (0, 1):
        where = [jax.random.randint(jax.random.fold_in(stream_key, axis), (), 0, length) for axis, length in enumerate(values.shape)]
        where[longest] = (where[longest] + shift) % values.shape[longest]
        spots.append(tuple(where))
    return values.at[spots[0]].set(low).at[spots[1]].set(top_value)


def block_scale(key, shape, shards, least, largest):
    def one(axis_at, parts):
        draws = jax.random.uniform(jax.random.fold_in(jax.random.fold_in(key, 6), axis_at), (parts,), jnp.float32, least / len(shards), largest / len(shards))
        return jnp.repeat(jnp.exp(draws), shape[axis_at] // parts).reshape((-1,) + (1,) * (len(shape) - axis_at - 1))

    loudness = one(*shards[0])
    for cut in shards[1:]:
        loudness = loudness * one(*cut)
    return loudness


def cumulative_ranks(amount, lean):
    portions = [(1 << 20) // math.isqrt(grade ** lean) + 1 for grade in range(1, amount + 1)]
    deviation = 1 + sum(portions) // (1 << 30)
    return np.cumsum(np.array([max(1, weight // deviation) for weight in portions]))


def ranked_ids(rng, dims, number_of, slope):
    table = cumulative_ranks(number_of, slope)
    lot = jax.random.randint(jax.random.fold_in(rng, 1), dims, 0, int(table[number_of - 1]))
    standing = jnp.searchsorted(jnp.asarray(table, jnp.int32), lot, side="right")
    return jax.random.permutation(jax.random.fold_in(rng, 2), number_of)[standing].astype(jnp.int32)


def assign_block(rng, own, number, rows, count, top, reach, skew):
    ranking = jax.random.permutation(rng, count)
    packed, usual = shares(count, rows * top, reach, skew, True), shares(count, rows * top, reach, skew, False)
    places = jnp.arange(count)

    def named(lengths, offset_by):
        used = int((lengths > 0).sum())
        fixed = max(1, used // 4)
        moved = fixed + (places - fixed + offset_by * (used - fixed)) % max(1, count - fixed)
        return jnp.zeros((count,), jnp.int32).at[ranking[jnp.where(places < fixed, places, moved)]].set(jnp.asarray(lengths, jnp.int32))

    lengths = jnp.where(number % 4 == 0, named(packed, number // 4), named(usual, number - number // 4 - 1))
    mixed = jax.random.permutation(jax.random.fold_in(own, 3), count)
    donor, receiver = mixed[0:count // 2 * 2:2], mixed[1:count // 2 * 2:2]
    slack = jnp.minimum(lengths[donor] - 1, reach - lengths[receiver]) // 2
    slack = jnp.where((donor == ranking[0]) | (receiver == ranking[0]) | (lengths[receiver] == 0), 0, jnp.maximum(slack, 0))
    moved = jax.random.randint(jax.random.fold_in(own, 4), (count // 2,), 0, 1 << 20) % (slack + 1)
    lengths = lengths.at[donor].add(-moved).at[receiver].add(moved)
    items = jnp.searchsorted(jnp.cumsum(lengths), jnp.arange(rows * top), side="right").astype(jnp.int32)
    listing = items.reshape(top, rows).T
    listing = listing[jax.random.permutation(jax.random.fold_in(own, 1), rows)]
    offset_by = jax.random.randint(jax.random.fold_in(own, 2), (rows, 1), 0, top)
    return jnp.take_along_axis(listing, (jnp.arange(top)[None, :] + offset_by) % top, axis=1)


def shares(amount, total, limit, slope, full):
    portions = [(1 << 20) // math.isqrt(rank ** slope) + 1 for rank in range(1, amount + 1)]
    largest = limit if full else min(limit, max(-(-total // amount), total * portions[0] // sum(portions)))
    least = 1 if total - largest >= amount - 1 else 0
    given, surplus = [largest] + [least] * (amount - 1), total - largest - least * (amount - 1)
    while surplus > 0:
        movable = [i for i in range(1, amount) if given[i] < largest] or [i for i in range(1, amount) if given[i] < limit]
        whole, budget = sum([portions[i] for i in movable]), surplus
        for i in movable:
            more = min(limit - given[i], max(1, budget * portions[i] // whole), surplus)
            given[i] = given[i] + more
            surplus = surplus - more
    return np.array(given)


def bell_draw(own_key, extent, width, reach, split=(), kind=jnp.bfloat16):
    level = block_scale(own_key, extent, split, -0.22, 0.18) if split else 1.0
    values = jax.random.normal(own_key, extent, jnp.float32) * width * level
    return jnp.minimum(jnp.maximum(values, -reach), reach).astype(kind)


def setup_inputs(seed: int = 0) -> dict:
    streams_of = jax.random.split(jax.random.key(seed), 10)
    flow = bell_draw(streams_of[0], (5, GY, GZ), 1.0, 6.0, ((1, 16), (2, 8)), jnp.float32)
    section_map = set_ends(ranked_ids(streams_of[1], (GY, GZ), NSEC, 2), jax.random.fold_in(streams_of[1], 3), 0, NSEC - 1).astype(jnp.int32)
    viscosity = jnp.clip(jnp.exp(jax.random.uniform(streams_of[2], (NSEC, 5), jnp.float32, math.log(0.12), math.log(0.24))), 0.12, 0.24)
    particle_position = jnp.clip(1.0 * jax.random.uniform(streams_of[3], (3, NPART), jnp.float32) ** block_scale(streams_of[3], (3, NPART), ((1, 128),), -0.2, 0.2), 0.0, 1.0)
    particle_strength = bell_draw(streams_of[4], (3, NPART), 0.1, 0.6, ((1, 128),), jnp.float32)
    particle_core = jnp.clip(jnp.exp(math.log(0.16) - 0.6931472 * jax.random.uniform(streams_of[5], (NPART,), jnp.float32) ** block_scale(streams_of[5], (NPART,), ((0, 128),), -0.2, 0.2)), 0.08, 0.16)
    shed_counts = draw_shed_counts(jax.random.fold_in(streams_of[9], 71), 0)
    node_position = jnp.clip(1.0 * jax.random.uniform(streams_of[7], (3, NODES), jnp.float32) ** block_scale(streams_of[7], (3, NODES), ((1, 128),), -0.2, 0.2), 0.0, 1.0)
    node_block_keys = jax.random.split(jax.random.fold_in(streams_of[8], 1), NODES // NODE_DEV)
    node_block_turns = jax.random.permutation(jax.random.fold_in(streams_of[8], 3), NODES // NODE_DEV)
    node_block = jax.vmap(lambda own, number: assign_block(jax.random.fold_in(streams_of[8], 2), own, number, NODE_DEV, N_WAKE, 1, CAP, 2))(node_block_keys, node_block_turns).reshape((NODES, 1))
    return dict(flow=flow, section_map=section_map, viscosity=viscosity, particle_position=particle_position, particle_strength=particle_strength, particle_core=particle_core, shed_counts=shed_counts, node_position=node_position, node_block=node_block)


inverse_four_pi = 1.0 / (4.0 * math.pi)


def cross_three(first, second):
    return (first[1] * second[2] - first[2] * second[1],
            first[2] * second[0] - first[0] * second[2],
            first[0] * second[1] - first[1] * second[0])


def particle_rates(place, spin, core, live, source, source_live):
    delta = [place[component][:, None] - source[component][None, :] for component in range(3)]
    spread = 0.5 * (core[:, None] * core[:, None] + source[6][None, :] * source[6][None, :])
    distance = delta[0] * delta[0] + delta[1] * delta[1] + delta[2] * delta[2] + spread
    weight = jnp.where(source_live[None, :], distance ** -1.5, 0.0)
    steep = 3.0 * weight / distance
    source_spin = [source[3 + component][None, :] for component in range(3)]
    curl = cross_three(delta, source_spin)
    along = spin[0][:, None] * delta[0] + spin[1][:, None] * delta[1] + spin[2][:, None] * delta[2]
    velocity = jnp.stack([jnp.sum(weight * curl[component], axis=1) for component in range(3)])
    spin_sum = [jnp.sum(weight * source_spin[component], axis=1) for component in range(3)]
    bent = jnp.stack([jnp.sum(steep * along * curl[component], axis=1) for component in range(3)])
    turned = jnp.stack(cross_three(spin, spin_sum))
    factor = jnp.where(live, -inverse_four_pi, 0.0)[None, :]
    return velocity * factor, (turned - bent) * factor


def node_rates(points, source, source_live):
    delta = [points[component][:, None] - source[component][None, :] for component in range(3)]
    distance = delta[0] * delta[0] + delta[1] * delta[1] + delta[2] * delta[2] + source[6][None, :] * source[6][None, :]
    weight = jnp.where(source_live[None, :], distance ** -1.5, 0.0)
    source_spin = [source[3 + component][None, :] for component in range(3)]
    curl = cross_three(delta, source_spin)
    return jnp.stack([jnp.sum(weight * curl[component], axis=1) for component in range(3)]) * (-inverse_four_pi)


def reference(flow, section_map, viscosity, particle_position, particle_strength, particle_core, shed_counts, node_position, node_block):
    slots = jnp.arange(PB, dtype=jnp.int32)
    place_blocks = particle_position.reshape(3, N_WAKE, PB)
    spin_blocks = particle_strength.reshape(3, N_WAKE, PB)
    core_blocks = particle_core.reshape(N_WAKE, PB)

    def block_source(number):
        return jnp.concatenate([place_blocks[:, number], spin_blocks[:, number], core_blocks[number][None, :]], axis=0)

    def wake_block(number):
        live = slots < shed_counts[number]

        def stop(turn, totals):
            source_number = (number + turn - STOPS // 2) % N_WAKE
            velocity, stretch = particle_rates(place_blocks[:, number], spin_blocks[:, number], core_blocks[number], live,
                                               block_source(source_number), slots < shed_counts[source_number])
            return (totals[0] + velocity, totals[1] + stretch)

        zeros = jnp.zeros((3, PB), jnp.float32)
        return lax.fori_loop(0, STOPS, stop, (zeros, zeros))

    velocity, stretch = lax.map(wake_block, jnp.arange(N_WAKE, dtype=jnp.int32))
    particle_velocity = velocity.transpose(1, 0, 2).reshape(3, NPART)
    particle_stretching = stretch.transpose(1, 0, 2).reshape(3, NPART)

    node_groups = node_position.reshape(3, NODES // NODE_DEV, NODE_DEV).transpose(1, 0, 2)
    block_groups = node_block[:, 0].reshape(NODES // NODE_DEV, NODE_DEV)

    def node_group(arrays):
        points, targets = arrays

        def one_block(number, total):
            result = node_rates(points, block_source(number), slots < shed_counts[number])
            return total + jnp.where((targets == number)[None, :], result, 0.0)

        return lax.fori_loop(0, N_WAKE, one_block, jnp.zeros((3, NODE_DEV), jnp.float32))

    node_velocity = lax.map(node_group, (node_groups, block_groups)).transpose(1, 0, 2).reshape(3, NODES)

    node_index = jnp.arange(NODES, dtype=jnp.int32)
    device = node_index // NODE_DEV
    local = node_index % NODE_DEV
    rows = (device // N_GRID) * CY + local // NODE_Z
    columns = (device % N_GRID) * CZ + (local % NODE_Z) * (CZ // NODE_Z)
    field = flow.at[1:4, rows, columns].set(node_velocity)

    def one_field(arrays):
        current, rates = arrays
        diffusion = jnp.zeros(section_map.shape, jnp.float32)
        for number in range(NSEC):
            diffusion = diffusion + jnp.where(section_map == number, rates[number], 0.0)
        for sweep in range(SWEEPS):
            padded = jnp.pad(current, ((1, 1), (1, 1)))
            beside = padded[2:, 1:-1] + padded[:-2, 1:-1] + padded[1:-1, 2:] + padded[1:-1, :-2]
            current = current + diffusion * (beside - 4.0 * current)
        return current

    flow_out = lax.map(one_field, (field, viscosity.T))
    return flow_out, particle_velocity, particle_stretching
```

```python
import math

import jax
import jax.numpy as jnp
from jax import lax
from jax.experimental import pallas as pl
from jax.experimental.pallas import tpu as pltpu
from jax.sharding import PartitionSpec as P

PB = 2048
NW = 16
NG = 8
CHUNK = 512
UNROLL = 4
PAIRED = 2
TILE = 64
SWEEPS = 3
BF = jnp.bfloat16
F32 = jnp.float32
MESH = pl.DeviceIdType.MESH
SCALE = -1.0 / (4.0 * math.pi)
WHOLE = pl.BlockSpec(memory_space=pltpu.VMEM)


def split_three(value):
    high = value.astype(BF).astype(F32)
    rest = value - high
    middle = rest.astype(BF).astype(F32)
    return high, middle, rest - middle


def dot_nt(first, second):
    return lax.dot_general(first, second, (((1,), (1,)), ((), ())), preferred_element_type=F32)


def cross_rows(first, second):
    return [
        first[1] * second[2] - first[2] * second[1],
        first[2] * second[0] - first[0] * second[2],
        first[0] * second[1] - first[1] * second[0],
    ]


def target_rows(place, weight, halved):
    ones = jnp.ones_like(weight)
    none = jnp.zeros_like(weight)
    parts = split_three(jnp.concatenate([-2.0 * row for row in place] + [none, none, weight, none, none], axis=0))
    unit = jnp.concatenate([none] * 3 + [none if halved else ones, ones if halved else none] + [none] * 3, axis=0)
    high, middle, low = parts
    return jnp.concatenate([high + unit, middle, low, high + unit, middle, high + unit], axis=0).astype(BF)


def source_rows(rows, live):
    place = rows[0:3]
    square = place[0] * place[0] + place[1] * place[1] + place[2] * place[2]
    core = rows[6] * rows[6]
    half = square + 0.5 * core
    ones = jnp.ones_like(square)
    none = jnp.zeros_like(square)
    high, middle, low = split_three(
        jnp.concatenate(list(place) + [square + core, half, ones, none, none], axis=0)
    )
    distance = jnp.concatenate([high, high, high, middle, middle, low], axis=0).astype(BF)
    spin = [jnp.where(live, rows[3 + c], 0.0) for c in range(3)]
    moment = jnp.concatenate(spin + cross_rows(place, spin) + [none, none], axis=0)
    return distance, moment, half


def gather_kernel(
    place, spin, core, node_place, node_block, gathered, points, slot_out, amounts,
    send_one, recv_one, send_two, recv_two, send_three, recv_three,
):
    wake = lax.axis_index("wake")
    grid = lax.axis_index("grid")
    side = lax.rem(wake, 2)
    pair = wake // 2
    sibling = wake + 1 - 2 * side
    lanes = pl.ds(pl.multiple_of(grid * 256, 256), 256)
    mine = gathered.at[pair, side, :, lanes]

    barrier = pltpu.get_barrier_semaphore()
    for turn in range(1, NG):
        pl.semaphore_signal(
            barrier, inc=1, device_id={"wake": wake, "grid": lax.rem(grid + turn, NG)}, device_id_type=MESH
        )
        pl.semaphore_signal(
            barrier, inc=1, device_id={"wake": lax.rem(wake + 2 * turn, NW), "grid": grid}, device_id_type=MESH
        )
    pl.semaphore_signal(barrier, inc=1, device_id={"wake": sibling, "grid": grid}, device_id_type=MESH)
    mine[...] = jnp.concatenate(
        [place[...], spin[...], core[...], jnp.zeros((1, 256), F32)], axis=0
    )
    pl.semaphore_wait(barrier, 2 * NG - 1)

    first = []
    for turn in range(1, NG):
        copy = pltpu.make_async_remote_copy(
            src_ref=mine,
            dst_ref=mine,
            send_sem=send_one.at[turn - 1],
            recv_sem=recv_one.at[turn - 1],
            device_id={"wake": wake, "grid": lax.rem(grid + turn, NG)},
            device_id_type=MESH,
        )
        copy.start()
        first.append(copy)

    names = node_block[...]
    spots = [node_place[c : c + 1, :] - 0.5 for c in range(3)]
    weight = spots[0] * spots[0] + spots[1] * spots[1] + spots[2] * spots[2]
    rows = target_rows(spots, weight, False)
    members = jnp.where(lax.broadcasted_iota(jnp.int32, (NW, 1024), 0) == names, 1.0, 0.0)
    triangle = jnp.where(
        lax.broadcasted_iota(jnp.int32, (128, 128), 0) <= lax.broadcasted_iota(jnp.int32, (128, 128), 1),
        1.0,
        0.0,
    ).astype(BF)
    pieces = jnp.concatenate([members[:, 128 * k : 128 * (k + 1)] for k in range(8)], axis=0)
    running = jnp.dot(pieces.astype(BF), triangle, preferred_element_type=F32)
    before = jnp.zeros((NW, 1), F32)
    ranks = []
    for k in range(8):
        part = running[NW * k : NW * (k + 1)]
        ranks.append(part + before)
        before = before + part[:, 127:128]
    rank = jnp.sum(members * jnp.concatenate(ranks, axis=1), axis=0, keepdims=True) - 1.0
    slot = names * 128 + rank.astype(jnp.int32)
    slot_out[...] = slot
    amounts[...] = jnp.broadcast_to(before, (NW, 128)).astype(jnp.int32)

    for copy in first:
        copy.wait_recv()
    second = []
    for turn in range(1, NG):
        copy = pltpu.make_async_remote_copy(
            src_ref=gathered.at[pair, side],
            dst_ref=gathered.at[pair, side],
            send_sem=send_two.at[turn - 1],
            recv_sem=recv_two.at[turn - 1],
            device_id={"wake": lax.rem(wake + 2 * turn, NW), "grid": grid},
            device_id_type=MESH,
        )
        copy.start()
        second.append(copy)

    def place_nodes(part, carry):
        start = pl.multiple_of(part * 256, 256)
        chosen = jnp.where(
            lax.broadcasted_iota(jnp.int32, (256, 1024), 0) + part * 256 == slot, 1.0, 0.0
        ).astype(BF)
        points[pl.ds(start, 256), :] = dot_nt(chosen, rows).astype(BF)
        return carry

    lax.fori_loop(0, 8, place_nodes, 0)

    for copy in second:
        copy.wait_recv()
    third = pltpu.make_async_remote_copy(
        src_ref=gathered.at[:, side],
        dst_ref=gathered.at[:, side],
        send_sem=send_three.at[0],
        recv_sem=recv_three.at[0],
        device_id={"wake": sibling, "grid": grid},
        device_id_type=MESH,
    )
    third.start()
    for copy in first + second:
        copy.wait_send()
    third.wait()


def gather_particles(place, spin, core, node_place, node_block):
    return pl.pallas_call(
        gather_kernel,
        out_shape=[
            jax.ShapeDtypeStruct((NW // 2, 2, 8, PB), F32),
            jax.ShapeDtypeStruct((NW * 128, 48), BF),
            jax.ShapeDtypeStruct((1, 1024), jnp.int32),
            jax.ShapeDtypeStruct((NW, 128), jnp.int32),
        ],
        in_specs=[WHOLE] * 5,
        out_specs=[WHOLE] * 4,
        scratch_shapes=[
            pltpu.SemaphoreType.DMA((NG - 1,)),
            pltpu.SemaphoreType.DMA((NG - 1,)),
            pltpu.SemaphoreType.DMA((NG - 1,)),
            pltpu.SemaphoreType.DMA((NG - 1,)),
            pltpu.SemaphoreType.DMA((1,)),
            pltpu.SemaphoreType.DMA((1,)),
        ],
        compiler_params=pltpu.CompilerParams(
            collective_id=0, has_side_effects=True, vmem_limit_bytes=32 << 20
        ),
        cost_estimate=pl.CostEstimate(flops=1 << 28, bytes_accessed=4 << 20, transcendentals=0),
    )(place, spin, core, node_place, node_block)


def build_source(counts, gathered, block, start, size):
    tile = gathered[block // 2, lax.rem(block, 2), :, pl.ds(start, size)]
    live = start + lax.broadcasted_iota(jnp.int32, (1, size), 1) < counts[block]
    source = [tile[c : c + 1] - 0.5 for c in range(3)] + [tile[c : c + 1] for c in range(3, 7)]
    distance, moment, half = source_rows(source, live)
    return distance, moment, source, half


def node_kernel(counts, amounts, gathered, points, slot, node_place, node_out, distance_rows, moment_rows, total):
    def build(block, carry):
        def step(chunk, inner):
            start = pl.multiple_of(chunk * CHUNK, CHUNK)
            distance, moment, _, _ = build_source(counts, gathered, block, start, CHUNK)
            high, middle, low = split_three(moment)
            distance_rows[block, :, pl.ds(start, CHUNK)] = distance
            moment_rows[block, :, pl.ds(start, CHUNK)] = jnp.concatenate(
                [high, middle, low, jnp.zeros_like(low)], axis=0
            ).astype(BF)
            return inner

        return lax.fori_loop(0, pl.cdiv(counts[block], CHUNK), step, carry)

    lax.fori_loop(0, NW, build, 0)
    total[...] = jnp.zeros_like(total)

    def count_items(block, amount):
        return amount + pl.cdiv(amounts[block, 0], TILE) * pl.cdiv(counts[block], CHUNK)

    items = lax.fori_loop(0, NW, count_items, 0)

    def advance(block, part, chunk):
        safe = jnp.minimum(block, NW - 1)
        parts = pl.cdiv(amounts[safe, 0], TILE)
        chunks = pl.cdiv(counts[safe], CHUNK)
        end = chunk + 1 >= chunks
        last = end & (part + 1 >= parts)
        return (
            jnp.where(last, block + 1, block),
            jnp.where(last, 0, jnp.where(end, part + 1, part)),
            jnp.where(end, 0, chunk + 1),
        )

    def skip(block):
        def empty(at):
            return (at < NW) & (amounts[jnp.minimum(at, NW - 1), 0] == 0)

        return lax.while_loop(empty, lambda at: at + 1, block)

    def run(turn, carry):
        block, part, chunk = carry
        added = []
        for _ in range(UNROLL):
            block = skip(block)
            safe = jnp.minimum(block, NW - 1)
            row = jnp.where(block < NW, safe * 2 + part, 2 * NW)
            start = pl.multiple_of(chunk * CHUNK, CHUNK)
            point = points[pl.ds(pl.multiple_of(jnp.minimum(row, 2 * NW - 1) * TILE, TILE), TILE), :]
            distance = distance_rows[safe, :, pl.ds(start, CHUNK)]
            columns = moment_rows[safe, :, pl.ds(start, CHUNK)]
            root = lax.rsqrt(jnp.dot(point, distance, preferred_element_type=F32))
            third = root * root * root
            high = third.astype(BF)
            low = (third - high.astype(F32)).astype(BF)
            gain = dot_nt(jnp.concatenate([high, low], axis=0), columns)
            added.append((row, gain[0:TILE] + gain[TILE : 2 * TILE]))
            block, part, chunk = advance(block, part, chunk)
        for row, gain in added:
            where = pl.ds(pl.multiple_of(row * TILE, TILE), TILE)
            total[where, :] += gain
        return block, part, chunk

    lax.fori_loop(0, pl.cdiv(items, UNROLL), run, (0, 0, 0))

    slots = jnp.transpose(jnp.broadcast_to(slot[...].astype(F32), (8, 1024)))[:, 0:1].astype(jnp.int32)
    found = jnp.zeros((1024, 32), F32)
    for block in range(NW):
        gained = total[128 * block : 128 * (block + 1), :]
        gained = gained[:, 0:8] + gained[:, 8:16] + gained[:, 16:24]
        used = lax.broadcasted_iota(jnp.int32, (128, 8), 0) < amounts[block, 0]
        high, middle, low = split_three(jnp.where(used, gained, 0.0))
        stacked = jnp.concatenate([high, middle, low, jnp.zeros_like(low)], axis=1).astype(BF)
        chosen = jnp.where(
            lax.broadcasted_iota(jnp.int32, (1024, 128), 1) + block * 128 == slots, 1.0, 0.0
        ).astype(BF)
        found = found + jnp.dot(chosen, stacked, preferred_element_type=F32)
    found = jnp.transpose(jnp.concatenate([found, jnp.zeros((1024, 96), F32)], axis=1))
    found = found[0:8] + found[8:16] + found[16:24]
    spots = [node_place[c : c + 1, :] - 0.5 for c in range(3)]
    moved = cross_rows(spots, [found[c : c + 1] for c in range(3)])
    for c in range(3):
        node_out[c : c + 1, :] = (moved[c] - found[3 + c : 4 + c]) * SCALE


SCALAR = pl.BlockSpec(memory_space=pltpu.SMEM)


def node_rates(counts, amounts, gathered, points, slot, node_place):
    return pl.pallas_call(
        node_kernel,
        out_shape=jax.ShapeDtypeStruct((3, 1024), F32),
        in_specs=[SCALAR, SCALAR, WHOLE, WHOLE, WHOLE, WHOLE],
        out_specs=WHOLE,
        scratch_shapes=[
            pltpu.VMEM((NW, 48, PB), BF),
            pltpu.VMEM((NW, 32, PB), BF),
            pltpu.VMEM((33 * TILE, 32), F32),
        ],
        compiler_params=pltpu.CompilerParams(vmem_limit_bytes=40 << 20),
        cost_estimate=pl.CostEstimate(flops=1 << 33, bytes_accessed=2 << 20, transcendentals=3 << 20),
    )(counts, amounts, gathered, points, slot, node_place)


def pair_kernel(counts, gathered, velocity_out, stretch_out, total):
    wake = lax.axis_index("wake")
    grid = lax.axis_index("grid")
    own = gathered[wake // 2, lax.rem(wake, 2), :, pl.ds(pl.multiple_of(grid * 256, 256), 256)]
    place = [own[c : c + 1] - 0.5 for c in range(3)]
    spin = [own[3 + c : 4 + c] for c in range(3)]
    weight = (
        place[0] * place[0] + place[1] * place[1] + place[2] * place[2] + 0.5 * own[6:7] * own[6:7]
    )
    rows = lax.broadcasted_iota(jnp.int32, (256, 256), 0)
    lanes = lax.broadcasted_iota(jnp.int32, (256, 256), 1)
    identity = jnp.where(rows == lanes, 1.0, 0.0).astype(BF)
    targets = dot_nt(identity, target_rows(place, weight, True)).astype(BF)
    total[...] = jnp.zeros_like(total)

    def count_items(turn, amount):
        return amount + pl.cdiv(counts[lax.rem(wake + turn + NW - 4, NW)], CHUNK)

    items = lax.fori_loop(0, NW // 2, count_items, 0)

    def run(step, carry):
        turn, chunk = carry
        gain = None
        for _ in range(PAIRED):
            block = lax.rem(wake + jnp.minimum(turn, NW // 2 - 1) + NW - 4, NW)
            start = pl.multiple_of(chunk * CHUNK, CHUNK)
            distance, moment, source, half = build_source(counts, gathered, block, start, CHUNK)
            moment = jnp.where(turn < NW // 2, moment, 0.0)
            parts = [split_three(moment)]
            for factor in (source[0], source[1], source[2], half):
                parts.append(split_three(moment * factor))
            columns = [parts[k][level] for level in range(3) for k in range(5)]
            columns = jnp.concatenate(columns + [jnp.zeros_like(moment)], axis=0).astype(BF)
            for cut in range(0, CHUNK, 256):
                squared = jnp.dot(targets, distance[:, cut : cut + 256], preferred_element_type=F32)
                root = lax.rsqrt(squared)
                second = root * root
                fifth = second * second * root
                high = fifth.astype(BF)
                low = (fifth - high.astype(F32)).astype(BF)
                added = dot_nt(jnp.concatenate([high, low], axis=0), columns[:, cut : cut + 256])
                gain = added if gain is None else gain + added
            end = chunk + 1 >= pl.cdiv(counts[block], CHUNK)
            turn = jnp.where(end, turn + 1, turn)
            chunk = jnp.where(end, 0, chunk + 1)
        total[...] += gain
        return turn, chunk

    lax.fori_loop(0, pl.cdiv(items, PAIRED), run, (0, 0))

    sums = jnp.transpose(total[0:256, :] + total[256:512, :])
    sums = sums[0:40] + sums[40:80] + sums[80:120]
    plain = [sums[k : k + 1] for k in range(6)]
    turned = [[sums[8 + 8 * c + k : 9 + 8 * c + k] for k in range(6)] for c in range(3)]
    heavy = [sums[32 + k : 33 + k] for k in range(6)]
    mixed = [
        weight * plain[k]
        + heavy[k]
        - 2.0 * (place[0] * turned[0][k] + place[1] * turned[1][k] + place[2] * turned[2][k])
        for k in range(6)
    ]
    live = grid * 256 + lax.broadcasted_iota(jnp.int32, (1, 256), 1) < counts[wake]
    factor = jnp.where(live, SCALE, 0.0)
    swept = cross_rows(place, mixed[0:3])
    bent_own = cross_rows(place, plain[0:3])
    along = spin[0] * place[0] + spin[1] * place[1] + spin[2] * place[2]
    pulled = [spin[0] * turned[0][k] + spin[1] * turned[1][k] + spin[2] * turned[2][k] for k in range(6)]
    bent_far = cross_rows(place, pulled[0:3])
    lifted = cross_rows(spin, mixed[0:3])
    for c in range(3):
        velocity_out[c : c + 1, :] = (swept[c] - mixed[3 + c]) * factor
        bent = along * (bent_own[c] - plain[3 + c]) - (bent_far[c] - pulled[3 + c])
        stretch_out[c : c + 1, :] = (lifted[c] - 3.0 * bent) * factor


def pair_rates(counts, gathered):
    return pl.pallas_call(
        pair_kernel,
        out_shape=[jax.ShapeDtypeStruct((3, 256), F32)] * 2,
        in_specs=[SCALAR, WHOLE],
        out_specs=[WHOLE] * 2,
        scratch_shapes=[pltpu.VMEM((512, 128), F32)],
        compiler_params=pltpu.CompilerParams(vmem_limit_bytes=32 << 20),
        cost_estimate=pl.CostEstimate(flops=1 << 34, bytes_accessed=2 << 20, transcendentals=3 << 20),
    )(counts, gathered)


SPAN = 1280
WIDE = 16640
BUFFER = WIDE + 256


def sweep_kernel(
    flow, sections, viscosity, below, above, left, right, nodes, out,
    rows_in, kind, first, second, rates, rows_out, sem_in, sem_out,
):
    fields = 5
    incoming = [
        pltpu.make_async_copy(flow.at[f], rows_in.at[f, pl.ds(0, 16), pl.ds(256, 16384)], sem_in.at[f])
        for f in range(fields)
    ]
    for copy in incoming:
        copy.start()
    kind[0:16, 256:16640] = sections[...].astype(F32) + 1.0
    kind[16:19, 256:16640] = below[5]
    kind[19:21, 256:16640] = jnp.zeros((2, 16384), F32)
    kind[21:24, 256:16640] = above[5]
    kind[:, 128:256] = left[5]
    kind[:, 16640:16768] = right[5]
    steps = WIDE // SPAN
    lane = lax.broadcasted_iota(jnp.int32, (8, 128), 1)

    def neighbours(wide):
        across = (pltpu.roll(wide, 1, 1) + pltpu.roll(wide, SPAN + 255, 1))[:, 128 : SPAN + 128]
        mid = wide[:, 128 : SPAN + 128]
        return mid, across + (pltpu.roll(mid, 1, 0) + pltpu.roll(mid, 23, 0))

    outgoing = []
    for f in (0, 4, 1, 2, 3):
        incoming[f].wait()
        rows_in[f, 16:19, 256:16640] = below[f]
        rows_in[f, 19:21, 256:16640] = jnp.zeros((2, 16384), F32)
        rows_in[f, 21:24, 256:16640] = above[f]
        rows_in[f, :, 128:256] = left[f]
        rows_in[f, :, 16640:16768] = right[f]

        if f in (1, 2, 3):
            for k in range(65):
                start = 256 + 256 * k
                for tile in range(3):
                    where = (f, pl.ds(8 * tile, 8), pl.ds(start, 128))
                    column = jnp.broadcast_to(nodes[f - 1, 8 * tile : 8 * tile + 8, k : k + 1], (8, 128))
                    rows_in[where] = jnp.where(lane == 0, column, rows_in[where])

        def sweep_first(step, carry):
            start = pl.multiple_of(step * SPAN, 128)
            inner = pl.ds(pl.multiple_of(start + 128, 128), SPAN)
            mid, beside = neighbours(rows_in[f, :, pl.ds(start, SPAN + 256)])
            name = kind[:, inner]
            rate = jnp.where(
                name == 1.0,
                viscosity[0, f],
                jnp.where(name == 2.0, viscosity[1, f], jnp.where(name == 3.0, viscosity[2, f], 0.0)),
            )
            rates[:, inner] = rate
            first[:, inner] = mid + rate * (beside - 4.0 * mid)
            return carry

        def sweep_second(step, carry):
            start = pl.multiple_of(step * SPAN, 128)
            inner = pl.ds(pl.multiple_of(start + 128, 128), SPAN)
            mid, beside = neighbours(first[:, pl.ds(start, SPAN + 256)])
            second[:, inner] = mid + rates[:, inner] * (beside - 4.0 * mid)
            return carry

        def sweep_third(step, carry):
            start = pl.multiple_of(step * SPAN, 128)
            inner = pl.ds(pl.multiple_of(start + 128, 128), SPAN)
            mid, beside = neighbours(second[:, pl.ds(start, SPAN + 256)])
            rows_out[f, :, inner] = (mid + rates[:, inner] * (beside - 4.0 * mid))[0:16]
            return carry

        lax.fori_loop(0, steps, sweep_first, 0)
        lax.fori_loop(0, steps, sweep_second, 0)
        lax.fori_loop(0, steps, sweep_third, 0)
        copy = pltpu.make_async_copy(
            rows_out.at[f, :, pl.ds(256, 16384)], out.at[f], sem_out.at[f]
        )
        copy.start()
        outgoing.append(copy)
    for copy in outgoing:
        copy.wait()


def sweep_fields(flow, sections, viscosity, below, above, left, right, nodes):
    return pl.pallas_call(
        sweep_kernel,
        out_shape=jax.ShapeDtypeStruct((5, 16, 16384), F32),
        in_specs=[pl.BlockSpec(memory_space=pl.ANY), WHOLE, SCALAR] + [WHOLE] * 5,
        out_specs=pl.BlockSpec(memory_space=pl.ANY),
        scratch_shapes=[
            pltpu.VMEM((5, 24, BUFFER), F32),
            pltpu.VMEM((24, BUFFER), F32),
            pltpu.VMEM((24, BUFFER), F32),
            pltpu.VMEM((24, BUFFER), F32),
            pltpu.VMEM((24, BUFFER), F32),
            pltpu.VMEM((5, 16, BUFFER), F32),
            pltpu.SemaphoreType.DMA((5,)),
            pltpu.SemaphoreType.DMA((5,)),
        ],
        compiler_params=pltpu.CompilerParams(vmem_limit_bytes=56 << 20),
        cost_estimate=pl.CostEstimate(flops=1 << 25, bytes_accessed=14 << 20, transcendentals=0),
    )(flow, sections, viscosity, below, above, left, right, nodes)


def shift(value, wake_by, grid_by):
    pairs = []
    for wake in range(NW):
        for grid in range(NG):
            to_wake, to_grid = wake + wake_by, grid + grid_by
            if 0 <= to_wake < NW and 0 <= to_grid < NG:
                pairs.append((wake * NG + grid, to_wake * NG + to_grid))
    return lax.ppermute(value, ("wake", "grid"), pairs)


def on_device(
    flow,
    section_map,
    viscosity,
    particle_position,
    particle_strength,
    particle_core,
    shed_counts,
    node_position,
    node_block,
):
    named = section_map.astype(F32)[None] + 1.0
    below = shift(jnp.concatenate([flow[:, 0:3], named[:, 0:3]], axis=0), -1, 0)
    above = shift(jnp.concatenate([flow[:, 13:16], named[:, 13:16]], axis=0), 1, 0)

    def side(lanes):
        own = jnp.concatenate([flow[:, :, lanes], named[:, :, lanes]], axis=0)
        gap = jnp.zeros((6, 2, 128), F32)
        return jnp.concatenate([own, below[:, :, lanes], gap, above[:, :, lanes]], axis=1)

    right = shift(side(slice(0, 128)), 0, -1)
    left = shift(side(slice(16256, 16384)), 0, 1)

    gathered, points, slot, amounts = gather_particles(
        particle_position, particle_strength, particle_core[None], node_position, node_block.reshape(1, 1024)
    )
    moved = node_rates(shed_counts, amounts[:, 0:1], gathered, points, slot, node_position)
    own = moved.reshape(3, 16, 64)
    corner = own[:, :, 0]
    lower = shift(own[:, 0:3], -1, 0)
    upper = shift(own[:, 13:16], 1, 0)
    beside = shift(corner, 0, -1)
    beside_lower = shift(corner[:, 0:3], -1, -1)
    beside_upper = shift(corner[:, 13:16], 1, -1)
    gap = jnp.zeros((3, 2, 65), F32)

    def joined(rows, column):
        return jnp.concatenate([rows, column[:, :, None]], axis=2)

    nodes = jnp.concatenate(
        [joined(own, beside), joined(lower, beside_lower), gap, joined(upper, beside_upper)], axis=1
    )
    nodes = jnp.pad(nodes, ((0, 0), (0, 0), (0, 63)))
    velocity, stretch = pair_rates(shed_counts, gathered)
    field = sweep_fields(flow, section_map, viscosity, below, above, left, right, nodes)
    return (field, velocity, stretch)


def solution(mesh):
    return jax.shard_map(
        on_device,
        mesh=mesh,
        in_specs=(
            P(None, "wake", "grid"),
            P("wake", "grid"),
            P(),
            P(None, ("wake", "grid")),
            P(None, ("wake", "grid")),
            P(("wake", "grid")),
            P(),
            P(None, ("wake", "grid")),
            P(("wake", "grid"), None),
        ),
        out_specs=(P(None, "wake", "grid"), P(None, ("wake", "grid")), P(None, ("wake", "grid"))),
        check_vma=False,
    )
```

```python
import math

import jax
import jax.numpy as jnp
from jax import lax
from jax.experimental import pallas as pl
from jax.experimental.pallas import tpu as pltpu
from jax.sharding import PartitionSpec as P

PB = 2048
NW = 16
NG = 8
CHUNK = 512
BF = jnp.bfloat16
F32 = jnp.float32
MESH = pl.DeviceIdType.MESH
SCALE = -1.0 / (4.0 * math.pi)
WHOLE = pl.BlockSpec(memory_space=pltpu.VMEM)


def split_three(value):
    high = value.astype(BF).astype(F32)
    rest = value - high
    middle = rest.astype(BF).astype(F32)
    return high, middle, rest - middle


def dot_nt(first, second):
    return lax.dot_general(first, second, (((1,), (1,)), ((), ())), preferred_element_type=F32)


def cross_rows(first, second):
    return [
        first[1] * second[2] - first[2] * second[1],
        first[2] * second[0] - first[0] * second[2],
        first[0] * second[1] - first[1] * second[0],
    ]


def target_rows(place, weight, halved):
    ones = jnp.ones_like(weight)
    none = jnp.zeros_like(weight)
    parts = split_three(jnp.concatenate([-2.0 * row for row in place] + [none, none, weight, none, none], axis=0))
    unit = jnp.concatenate([none] * 3 + [none if halved else ones, ones if halved else none] + [none] * 3, axis=0)
    high, middle, low = parts
    return jnp.concatenate([high + unit, middle, low, high + unit, middle, high + unit], axis=0).astype(BF)


def source_rows(rows, live):
    place = rows[0:3]
    square = place[0] * place[0] + place[1] * place[1] + place[2] * place[2]
    core = rows[6] * rows[6]
    half = square + 0.5 * core
    ones = jnp.ones_like(square)
    none = jnp.zeros_like(square)
    high, middle, low = split_three(
        jnp.concatenate(list(place) + [square + core, half, ones, none, none], axis=0)
    )
    distance = jnp.concatenate([high, high, high, middle, middle, low], axis=0).astype(BF)
    spin = [jnp.where(live, rows[3 + c], 0.0) for c in range(3)]
    moment = jnp.concatenate(spin + cross_rows(place, spin) + [none, none], axis=0)
    return distance, moment, half


def source_columns(moment, factors):
    parts = [split_three(moment)] + [split_three(moment * factor) for factor in factors]
    columns = [part[level] for level in range(3) for part in parts]
    return columns


def centred(rows):
    return [rows[c : c + 1] - 0.5 for c in range(3)]


def square_sum(place):
    return place[0] * place[0] + place[1] * place[1] + place[2] * place[2]


def gather_kernel(
    counts, place_in, spin_in, core_in, node_place_in, node_block_in, flow, sections,
    velocity_out, stretch_out, own_nodes, far_nodes, rows_halo, left_halo, right_halo,
    kind_rows, kind_left, kind_right,
    gathered, share, node_place, node_block, points, targets_ref, total, node_total, answers,
    sem_in, send_one, recv_one, send_two, recv_two, send_three, recv_three,
    send_halo, recv_halo, send_node, recv_node,
):
    wake = lax.axis_index("wake")
    grid = lax.axis_index("grid")
    side = lax.rem(wake, 2)
    pair = wake // 2
    lanes = pl.ds(pl.multiple_of(grid * 256, 256), 256)
    mine = gathered.at[pair, side, :, lanes]

    def device(wake_by, grid_by):
        return {"wake": lax.rem(wake + wake_by + NW, NW), "grid": lax.rem(grid + grid_by + NG, NG)}

    loads = [
        pltpu.make_async_copy(source, target, sem_in.at[k])
        for k, (source, target) in enumerate(
            [
                (place_in, share.at[0]),
                (spin_in, share.at[1]),
                (core_in, share.at[2, pl.ds(0, 1)]),
                (node_place_in, node_place),
                (node_block_in, node_block),
            ]
        )
    ]
    for load in loads:
        load.start()

    peers = [(0, turn) for turn in range(1, NG)] + [(2 * turn, 0) for turn in range(1, NG)]
    peers += [(1, 0), (-1, 0), (1, 1), (1, -1), (-1, 1), (-1, -1)]
    barrier = pltpu.get_barrier_semaphore()
    for peer in peers:
        pl.semaphore_signal(barrier, inc=1, device_id=device(*peer), device_id_type=MESH)
    for load in loads:
        load.wait()
    mine[...] = jnp.concatenate(
        [share[0], share[1], share[2, 0:1], jnp.zeros((1, 256), F32)], axis=0
    )
    pl.semaphore_wait(barrier, len(peers))

    def send(source, target, sends, recvs, slot, peer):
        copy = pltpu.make_async_remote_copy(
            src_ref=source,
            dst_ref=target,
            send_sem=sends.at[slot],
            recv_sem=recvs.at[slot],
            device_id=device(*peer),
            device_id_type=MESH,
        )
        copy.start()
        return copy

    first = [send(mine, mine, send_one, recv_one, turn - 1, (0, turn)) for turn in range(1, NG)]

    names = node_block[...]
    spots = centred(node_place)
    rows = target_rows(spots, square_sum(spots), False)
    members = jnp.where(lax.broadcasted_iota(jnp.int32, (NW, 1024), 0) == names, 1.0, 0.0)
    triangle = jnp.where(
        lax.broadcasted_iota(jnp.int32, (128, 128), 0) <= lax.broadcasted_iota(jnp.int32, (128, 128), 1),
        1.0,
        0.0,
    ).astype(BF)
    pieces = jnp.concatenate([members[:, 128 * k : 128 * (k + 1)] for k in range(8)], axis=0)
    running = jnp.dot(pieces.astype(BF), triangle, preferred_element_type=F32)
    before = jnp.zeros((NW, 1), F32)
    ranks = []
    for k in range(8):
        part = running[NW * k : NW * (k + 1)]
        ranks.append(part + before)
        before = before + part[:, 127:128]
    rank = jnp.sum(members * jnp.concatenate(ranks, axis=1), axis=0, keepdims=True) - 1.0
    slot = names * 128 + rank.astype(jnp.int32)

    own = mine[...]
    place = centred(own)
    weight = square_sum(place) + 0.5 * own[6:7] * own[6:7]
    identity = jnp.where(
        lax.broadcasted_iota(jnp.int32, (256, 256), 0) == lax.broadcasted_iota(jnp.int32, (256, 256), 1),
        1.0,
        0.0,
    ).astype(BF)
    targets_ref[...] = dot_nt(identity, target_rows(place, weight, True)).astype(BF)
    total[...] = jnp.zeros_like(total)

    for copy in first:
        copy.wait_recv()
    block_here = gathered.at[pair, side]
    second = [
        send(block_here, block_here, send_two, recv_two, turn - 1, (2 * turn, 0)) for turn in range(1, NG)
    ]

    top, bottom = pl.ds(0, 3), pl.ds(13, 3)
    low_rows, high_rows = pl.ds(0, 3), pl.ds(5, 3)
    begin, finish = pl.ds(0, 128), pl.ds(16256, 128)
    middle, before_lanes, after_lanes = pl.ds(256, 16384), pl.ds(128, 128), pl.ds(16640, 128)
    everything, every = pl.ds(0, 16384), pl.ds(0, 16)
    plan = [
        ((-1, 0), top, everything, 0, low_rows, middle),
        ((1, 0), bottom, everything, 0, high_rows, middle),
        ((0, -1), every, begin, 2, every, begin),
        ((0, 1), every, finish, 1, every, begin),
        ((-1, -1), top, begin, 0, low_rows, after_lanes),
        ((-1, 1), top, finish, 0, low_rows, before_lanes),
        ((1, -1), bottom, begin, 0, high_rows, after_lanes),
        ((1, 1), bottom, finish, 0, high_rows, before_lanes),
    ]
    halos = []
    for k, (peer, from_rows, from_lanes, which, to_rows, to_lanes) in enumerate(plan):
        target = (rows_halo, left_halo, right_halo)[which]
        halos.append(
            send(
                flow.at[:, from_rows, from_lanes], target.at[:, to_rows, to_lanes],
                send_halo, recv_halo, 2 * k, peer,
            )
        )
        target = (kind_rows, kind_left, kind_right)[which]
        halos.append(
            send(
                sections.at[from_rows, from_lanes], target.at[to_rows, to_lanes],
                send_halo, recv_halo, 2 * k + 1, peer,
            )
        )

    def place_nodes(part, carry):
        start = pl.multiple_of(part * 256, 256)
        chosen = jnp.where(
            lax.broadcasted_iota(jnp.int32, (256, 1024), 0) + part * 256 == slot, 1.0, 0.0
        ).astype(BF)
        points[pl.ds(start, 256), :] = dot_nt(chosen, rows).astype(BF)
        return carry

    lax.fori_loop(0, 8, place_nodes, 0)

    def load_source(block, start):
        tile = gathered[block // 2, lax.rem(block, 2), :, pl.ds(start, CHUNK)]
        live = start + lax.broadcasted_iota(jnp.int32, (1, CHUNK), 1) < counts[block]
        source = centred(tile) + [tile[c : c + 1] for c in range(3, 7)]
        distance, moment, half = source_rows(source, live)
        return distance, moment, source[0:3] + [half]

    def node_slots(block):
        return pl.ds(pl.multiple_of(block * 128, 128), 128)

    def split_two(value):
        high = value.astype(BF)
        return high, (value - high.astype(F32)).astype(BF)

    def near(offset):
        block = lax.rem(wake + offset + NW, NW)
        looking = jnp.concatenate([targets_ref[...], points[node_slots(block), :]], axis=0)

        def run(step, gained):
            distance, moment, factors = load_source(block, pl.multiple_of(step * CHUNK, CHUNK))
            columns = source_columns(moment, factors)
            columns = jnp.concatenate(columns + [jnp.zeros_like(moment)], axis=0).astype(BF)
            for cut in range(0, CHUNK, 256):
                root = lax.rsqrt(
                    jnp.dot(looking, distance[:, cut : cut + 256], preferred_element_type=F32)
                )
                second_power = root * root
                third = second_power * root
                fifth = third[0:256] * second_power[0:256]
                high, low = split_two(fifth)
                high_node, low_node = split_two(third[256:384])
                added = dot_nt(
                    jnp.concatenate([high, low, high_node, low_node], axis=0), columns[:, cut : cut + 256]
                )
                gained = added if gained is None else gained + added
            return gained

        gained = None
        for step in range(PB // CHUNK):
            gained = run(step, gained)
        total[...] += gained[0:256] + gained[256:512]
        sums = gained[512:640] + gained[640:768]
        node_total[node_slots(block), :] = sums[:, 0:8] + sums[:, 40:48] + sums[:, 80:88]

    def far(offset):
        block = lax.rem(wake + offset + NW, NW)
        looking = points[node_slots(block), :]
        gained = None
        for step in range(PB // CHUNK):
            distance, moment, _ = load_source(block, pl.multiple_of(step * CHUNK, CHUNK))
            columns = source_columns(moment, [])
            columns = jnp.concatenate(columns + [jnp.zeros_like(moment)], axis=0).astype(BF)
            root = lax.rsqrt(jnp.dot(looking, distance, preferred_element_type=F32))
            high, low = split_two(root * root * root)
            added = dot_nt(jnp.concatenate([high, low], axis=0), columns)
            gained = added if gained is None else gained + added
        sums = gained[0:128] + gained[128:256]
        node_total[node_slots(block), :] = sums[:, 0:8] + sums[:, 8:16] + sums[:, 16:24]

    def loop(function, start):
        def body(turn, carry):
            function(start + 2 * turn)
            return carry

        lax.fori_loop(0, NW // 4, body, 0)

    for copy in second:
        copy.wait_recv()
    third_copy = send(
        gathered.at[:, side], gathered.at[:, side], send_three, recv_three, 0, (1 - 2 * side, 0)
    )
    loop(near, -4)
    loop(far, 4)
    third_copy.wait_recv()
    loop(far, 5)
    loop(near, -3)

    answers[...] = jnp.zeros_like(answers)

    def return_nodes(part, carry):
        start = pl.multiple_of(part * 256, 256)
        slot_rows = lax.broadcasted_iota(jnp.int32, (256, 1024), 0) + part * 256
        chosen = jnp.where(slot_rows == slot, 1.0, 0.0).astype(BF)
        named = jnp.sum(jnp.where(slot_rows == slot, 1.0, 0.0), axis=1, keepdims=True) > 0.0
        gained = jnp.where(named, node_total[pl.ds(start, 256), :], 0.0)
        high, mid, low = split_three(gained)
        stacked = jnp.concatenate([high, mid, low, jnp.zeros_like(low)], axis=1).astype(BF)
        answers[...] += lax.dot_general(
            stacked, chosen, (((0,), (0,)), ((), ())), preferred_element_type=F32
        )
        return carry

    lax.fori_loop(0, 8, return_nodes, 0)
    found = answers[0:8] + answers[8:16] + answers[16:24]
    moved = cross_rows(spots, [found[c : c + 1] for c in range(3)])
    for c in range(3):
        result = (moved[c] - found[3 + c : 4 + c]) * SCALE
        even = jnp.concatenate([result[:, 128 * k : 128 * (k + 1)] for k in range(8)], axis=0)
        odd = pltpu.roll(even, 64, 1)
        own_nodes[c] = jnp.concatenate(
            [(even, odd)[r % 2][r // 2 : r // 2 + 1] for r in range(16)], axis=0
        )
    shared = [
        send(own_nodes, far_nodes.at[k], send_node, recv_node, k, peer)
        for k, peer in enumerate([(0, -1), (-1, 0), (1, 0), (-1, -1), (1, -1)])
    ]

    spin = [own[3 + c : 4 + c] for c in range(3)]
    sums = jnp.transpose(total[...])
    sums = sums[0:40] + sums[40:80] + sums[80:120]
    plain = [sums[k : k + 1] for k in range(6)]
    turned = [[sums[8 + 8 * c + k : 9 + 8 * c + k] for k in range(6)] for c in range(3)]
    heavy = [sums[32 + k : 33 + k] for k in range(6)]
    mixed = [
        weight * plain[k]
        + heavy[k]
        - 2.0 * (place[0] * turned[0][k] + place[1] * turned[1][k] + place[2] * turned[2][k])
        for k in range(6)
    ]
    live = grid * 256 + lax.broadcasted_iota(jnp.int32, (1, 256), 1) < counts[wake]
    factor = jnp.where(live, SCALE, 0.0)
    swept = cross_rows(place, mixed[0:3])
    bent_own = cross_rows(place, plain[0:3])
    along = spin[0] * place[0] + spin[1] * place[1] + spin[2] * place[2]
    pulled = [spin[0] * turned[0][k] + spin[1] * turned[1][k] + spin[2] * turned[2][k] for k in range(6)]
    bent_far = cross_rows(place, pulled[0:3])
    lifted = cross_rows(spin, mixed[0:3])
    for c in range(3):
        velocity_out[c : c + 1, :] = (swept[c] - mixed[3 + c]) * factor
        bent = along * (bent_own[c] - plain[3 + c]) - (bent_far[c] - pulled[3 + c])
        stretch_out[c : c + 1, :] = (lifted[c] - 3.0 * bent) * factor

    for copy in shared + halos:
        copy.wait()
    for copy in first + second + [third_copy]:
        copy.wait_send()


ANY = pl.BlockSpec(memory_space=pl.ANY)
SCALAR = pl.BlockSpec(memory_space=pltpu.SMEM)


def gather_and_sum(counts, place, spin, core, node_place, node_block, flow, sections):
    dma = pltpu.SemaphoreType.DMA
    return pl.pallas_call(
        gather_kernel,
        out_shape=[
            jax.ShapeDtypeStruct((3, 256), F32),
            jax.ShapeDtypeStruct((3, 256), F32),
            jax.ShapeDtypeStruct((3, 16, 128), F32),
            jax.ShapeDtypeStruct((5, 3, 16, 128), F32),
            jax.ShapeDtypeStruct((5, 8, BUFFER), F32),
            jax.ShapeDtypeStruct((5, 16, 128), F32),
            jax.ShapeDtypeStruct((5, 16, 128), F32),
            jax.ShapeDtypeStruct((8, BUFFER), jnp.int32),
            jax.ShapeDtypeStruct((16, 128), jnp.int32),
            jax.ShapeDtypeStruct((16, 128), jnp.int32),
        ],
        in_specs=[SCALAR] + [ANY] * 7,
        out_specs=[WHOLE] * 4 + [ANY] * 6,
        scratch_shapes=[
            pltpu.VMEM((NW // 2, 2, 8, PB), F32),
            pltpu.VMEM((3, 3, 256), F32),
            pltpu.VMEM((3, 1024), F32),
            pltpu.VMEM((1, 1024), jnp.int32),
            pltpu.VMEM((NW * 128, 48), BF),
            pltpu.VMEM((256, 48), BF),
            pltpu.VMEM((256, 128), F32),
            pltpu.VMEM((NW * 128, 8), F32),
            pltpu.VMEM((32, 1024), F32),
            dma((5,)),
            dma((NG - 1,)),
            dma((NG - 1,)),
            dma((NG - 1,)),
            dma((NG - 1,)),
            dma((1,)),
            dma((1,)),
            dma((16,)),
            dma((16,)),
            dma((5,)),
            dma((5,)),
        ],
        compiler_params=pltpu.CompilerParams(
            collective_id=0, has_side_effects=True, vmem_limit_bytes=40 << 20
        ),
    )(counts, place, spin, core, node_place, node_block, flow, sections)


TILES = 13
STEPS = 10
BUFFER = 16640 + 256


def sweep_kernel(
    flow, sections, viscosity, rows_halo, left_halo, right_halo, kind_rows, kind_left, kind_right,
    own_nodes, far_nodes, velocity, stretch, out, velocity_out, stretch_out,
    rows_in, kind, first, second, rates, rows_out, nodes, sem_in, sem_out,
):
    fields = 5
    wake = lax.axis_index("wake")
    grid = lax.axis_index("grid")
    own_rows, halo_rows = pl.ds(0, 16), pl.ds(16, 8)
    middle, before, after = pl.ds(256, 16384), pl.ds(128, 128), pl.ds(16640, 128)
    kinds = [
        pltpu.make_async_copy(source, target, sem_in.at[4 * fields + k])
        for k, (source, target) in enumerate(
            [
                (sections, kind.at[own_rows, middle]),
                (kind_rows, kind.at[halo_rows, :]),
                (kind_left, kind.at[own_rows, before]),
                (kind_right, kind.at[own_rows, after]),
            ]
        )
    ]
    incoming = [
        [
            pltpu.make_async_copy(source, target, sem_in.at[4 * f + k])
            for k, (source, target) in enumerate(
                [
                    (flow.at[f], rows_in.at[f, own_rows, middle]),
                    (rows_halo.at[f], rows_in.at[f, halo_rows, :]),
                    (left_halo.at[f], rows_in.at[f, own_rows, before]),
                    (right_halo.at[f], rows_in.at[f, own_rows, after]),
                ]
            )
        ]
        for f in range(fields)
    ]
    for copy in kinds + [copy for f in ORDER for copy in incoming[f]]:
        copy.start()
    velocity_out[...] = velocity[...]
    stretch_out[...] = stretch[...]

    lane = lax.broadcasted_iota(jnp.int32, (24, 128), 1)
    row = lax.broadcasted_iota(jnp.int32, (24, 128), 0)
    is_first, is_last = lane == 0, lane == 127
    inside_rows = ((row < 20) | (wake > 0)) & ((row < 16) | (row >= 20) | (wake < NW - 1))
    lane8 = lax.broadcasted_iota(jnp.int32, (8, 128), 1)
    row8 = lax.broadcasted_iota(jnp.int32, (8, 128), 0)

    for c in range(3):
        def with_next(rows, column):
            return jnp.where(lane8 == 64, jnp.broadcast_to(column, (8, 128)), rows)

        halo = jnp.where(row8 < 4, far_nodes[1, c, 0:8], far_nodes[2, c, 8:16])
        halo_next = jnp.where(row8 < 4, far_nodes[3, c, 0:8], far_nodes[4, c, 8:16])
        parts = [
            with_next(own_nodes[c, 0:8], far_nodes[0, c, 0:8, 0:1]),
            with_next(own_nodes[c, 8:16], far_nodes[0, c, 8:16, 0:1]),
            with_next(halo, halo_next[:, 0:1]),
        ]
        nodes[c] = jnp.where(inside_rows, jnp.concatenate(parts, axis=0), 0.0)

    for copy in kinds:
        copy.wait()

    tile_lanes = lambda t: pl.ds(pl.multiple_of(t * 128, 128), 128)

    outgoing = []
    for f in ORDER:
        for copy in incoming[f]:
            copy.wait()
        rows_in[f, 16:24, 256:16640] = jnp.where(
            inside_rows[16:24, 0:1], rows_in[f, 16:24, 256:16640], 0.0
        )
        for start, edge in ((128, grid == 0), (16640, grid == NG - 1)):
            keep = inside_rows & jnp.logical_not(edge)
            rows_in[f, :, start : start + 128] = jnp.where(keep, rows_in[f, :, start : start + 128], 0.0)
        if f in (1, 2, 3):
            for k in range(65):
                start = 256 + 256 * k
                column = jnp.broadcast_to(nodes[f - 1, :, k : k + 1], (24, 128))
                if k == 64:
                    column = jnp.where(grid == NG - 1, 0.0, column)
                rows_in[f, :, start : start + 128] = jnp.where(
                    is_first, column, rows_in[f, :, start : start + 128]
                )

        def sweep(load, finish):
            def body(step, carry):
                last_right, here, right, left = carry
                for k in range(TILES):
                    t = step * TILES + k + 1
                    following = load(t + 1)
                    next_right = pltpu.roll(following, 1, 1)
                    next_left = pltpu.roll(following, 127, 1)
                    across = jnp.where(is_first, last_right, right) + jnp.where(is_last, next_left, left)
                    along = pltpu.roll(here, 1, 0) + pltpu.roll(here, 23, 0)
                    finish(t, here, across + along)
                    last_right, here, right, left = right, following, next_right, next_left
                return last_right, here, right, left

            start = load(1)
            lax.fori_loop(
                0, STEPS, body, (pltpu.roll(load(0), 1, 1), start, pltpu.roll(start, 1, 1), pltpu.roll(start, 127, 1))
            )

        def finish_first(t, here, beside):
            name = kind[:, tile_lanes(t)]
            rate = jnp.where(
                name == 0, viscosity[0, f], jnp.where(name == 1, viscosity[1, f], viscosity[2, f])
            )
            keep = inside_rows & jnp.logical_not(((t == 1) & (grid == 0)) | ((t == 130) & (grid == NG - 1)))
            rate = jnp.where(keep, rate, 0.0)
            rates[:, tile_lanes(t)] = rate
            first[:, tile_lanes(t)] = here + rate * (beside - 4.0 * here)

        def finish_second(t, here, beside):
            second[:, tile_lanes(t)] = here + rates[:, tile_lanes(t)] * (beside - 4.0 * here)

        def finish_third(t, here, beside):
            rows_out[f, :, tile_lanes(t)] = (here + rates[:, tile_lanes(t)] * (beside - 4.0 * here))[0:16]

        sweep(lambda t: rows_in[f, :, tile_lanes(t)], finish_first)
        sweep(lambda t: first[:, tile_lanes(t)], finish_second)
        sweep(lambda t: second[:, tile_lanes(t)], finish_third)
        copy = pltpu.make_async_copy(rows_out.at[f, :, middle], out.at[f], sem_out.at[f])
        copy.start()
        outgoing.append(copy)
    for copy in outgoing:
        copy.wait()


ORDER = (0, 4, 1, 2, 3)


def sweep_fields(*arrays):
    dma = pltpu.SemaphoreType.DMA
    return pl.pallas_call(
        sweep_kernel,
        out_shape=[
            jax.ShapeDtypeStruct((5, 16, 16384), F32),
            jax.ShapeDtypeStruct((3, 256), F32),
            jax.ShapeDtypeStruct((3, 256), F32),
        ],
        in_specs=[ANY, ANY, SCALAR] + [ANY] * 6 + [WHOLE] * 4,
        out_specs=[ANY, WHOLE, WHOLE],
        scratch_shapes=[
            pltpu.VMEM((5, 24, BUFFER), F32),
            pltpu.VMEM((24, BUFFER), jnp.int32),
            pltpu.VMEM((24, BUFFER), F32),
            pltpu.VMEM((24, BUFFER), F32),
            pltpu.VMEM((24, BUFFER), F32),
            pltpu.VMEM((5, 16, BUFFER), F32),
            pltpu.VMEM((3, 24, 128), F32),
            dma((24,)),
            dma((5,)),
        ],
        compiler_params=pltpu.CompilerParams(vmem_limit_bytes=56 << 20),
    )(*arrays)


def on_device(
    flow,
    section_map,
    viscosity,
    particle_position,
    particle_strength,
    particle_core,
    shed_counts,
    node_position,
    node_block,
):
    (
        velocity, stretch, own_nodes, far_nodes, rows_halo, left_halo, right_halo, kind_rows, kind_left, kind_right,
    ) = gather_and_sum(
        shed_counts,
        particle_position,
        particle_strength,
        particle_core.reshape(1, 256),
        node_position,
        node_block.reshape(1, 1024),
        flow,
        section_map,
    )
    field, velocity, stretch = sweep_fields(
        flow, section_map, viscosity, rows_halo, left_halo, right_halo, kind_rows, kind_left, kind_right,
        own_nodes, far_nodes, velocity, stretch,
    )
    return (field, velocity, stretch)


def solution(mesh):
    return jax.shard_map(
        on_device,
        mesh=mesh,
        in_specs=(
            P(None, "wake", "grid"),
            P("wake", "grid"),
            P(),
            P(None, ("wake", "grid")),
            P(None, ("wake", "grid")),
            P(("wake", "grid")),
            P(),
            P(None, ("wake", "grid")),
            P(("wake", "grid"), None),
        ),
        out_specs=(P(None, "wake", "grid"), P(None, ("wake", "grid")), P(None, ("wake", "grid"))),
        check_vma=False,
    )
```

```python
import math

import jax
import jax.numpy as jnp
from jax import lax
from jax.experimental import pallas as pl
from jax.experimental.pallas import tpu as pltpu
from jax.sharding import PartitionSpec as P

PB = 2048
NW = 16
NG = 8
CHUNK = 512
LIMIT = 64 << 20
BF = jnp.bfloat16
F32 = jnp.float32
MESH = pl.DeviceIdType.MESH
SCALE = -1.0 / (4.0 * math.pi)
WHOLE = pl.BlockSpec(memory_space=pltpu.VMEM)


def split_three(value):
    high = value.astype(BF).astype(F32)
    rest = value - high
    middle = rest.astype(BF).astype(F32)
    return high, middle, rest - middle


def dot_nt(first, second):
    return lax.dot_general(first, second, (((1,), (1,)), ((), ())), preferred_element_type=F32)


def cross_rows(first, second):
    return [
        first[1] * second[2] - first[2] * second[1],
        first[2] * second[0] - first[0] * second[2],
        first[0] * second[1] - first[1] * second[0],
    ]


def target_rows(place, weight, halved):
    ones = jnp.ones_like(weight)
    none = jnp.zeros_like(weight)
    parts = split_three(jnp.concatenate([-2.0 * row for row in place] + [none, none, weight, none, none], axis=0))
    unit = jnp.concatenate([none] * 3 + [none if halved else ones, ones if halved else none] + [none] * 3, axis=0)
    high, middle, low = parts
    return jnp.concatenate([high + unit, middle, low, high + unit, middle, high + unit], axis=0).astype(BF)


def source_rows(rows, live):
    place = rows[0:3]
    square = place[0] * place[0] + place[1] * place[1] + place[2] * place[2]
    core = rows[6] * rows[6]
    half = square + 0.5 * core
    ones = jnp.ones_like(square)
    none = jnp.zeros_like(square)
    high, middle, low = split_three(
        jnp.concatenate(list(place) + [square + core, half, ones, none, none], axis=0)
    )
    distance = jnp.concatenate([high, high, high, middle, middle, low], axis=0).astype(BF)
    spin = [jnp.where(live, rows[3 + c], 0.0) for c in range(3)]
    moment = jnp.concatenate(spin + cross_rows(place, spin) + [none, none], axis=0)
    return distance, moment, half


def source_columns(moment, factors):
    parts = [split_three(moment)] + [split_three(moment * factor) for factor in factors]
    columns = [part[level] for level in range(3) for part in parts]
    return columns


def centred(rows):
    return [rows[c : c + 1] - 0.5 for c in range(3)]


def square_sum(place):
    return place[0] * place[0] + place[1] * place[1] + place[2] * place[2]


def gather_kernel(
    counts, place_in, spin_in, core_in, node_place_in, node_block_in, flow, sections,
    velocity_out, stretch_out, own_nodes, far_nodes, rows_halo, left_halo, right_halo,
    kind_rows, kind_left, kind_right,
    gathered, share, node_place, node_block, points, targets_ref, total, node_total, answers,
    sem_in, send_one, recv_one, send_two, recv_two, send_three, recv_three,
    send_halo, recv_halo, send_node, recv_node,
):
    wake = lax.axis_index("wake")
    grid = lax.axis_index("grid")
    side = lax.rem(wake, 2)
    pair = wake // 2
    lanes = pl.ds(pl.multiple_of(grid * 256, 256), 256)
    mine = gathered.at[pair, side, :, lanes]

    def device(wake_by, grid_by):
        return {"wake": lax.rem(wake + wake_by + NW, NW), "grid": lax.rem(grid + grid_by + NG, NG)}

    loads = [
        pltpu.make_async_copy(source, target, sem_in.at[k])
        for k, (source, target) in enumerate(
            [
                (place_in, share.at[0]),
                (spin_in, share.at[1]),
                (core_in, share.at[2, pl.ds(0, 1)]),
                (node_place_in, node_place),
                (node_block_in, node_block),
            ]
        )
    ]
    for load in loads:
        load.start()

    peers = [(0, turn) for turn in range(1, NG)] + [(2 * turn, 0) for turn in range(1, NG)]
    peers += [(1, 0), (-1, 0), (1, 1), (1, -1), (-1, 1), (-1, -1)]
    barrier = pltpu.get_barrier_semaphore()
    for peer in peers:
        pl.semaphore_signal(barrier, inc=1, device_id=device(*peer), device_id_type=MESH)
    for load in loads:
        load.wait()
    mine[...] = jnp.concatenate(
        [share[0], share[1], share[2, 0:1], jnp.zeros((1, 256), F32)], axis=0
    )
    pl.semaphore_wait(barrier, len(peers))

    def describe(source, target, sends, recvs, slot, peer):
        return pltpu.make_async_remote_copy(
            src_ref=source,
            dst_ref=target,
            send_sem=sends.at[slot],
            recv_sem=recvs.at[slot],
            device_id=device(*peer),
            device_id_type=MESH,
        )

    def send(*arguments):
        copy = describe(*arguments)
        copy.start()
        return copy

    first = [send(mine, mine, send_one, recv_one, turn - 1, (0, turn)) for turn in range(1, NG)]

    names = node_block[...]
    spots = centred(node_place)
    rows = target_rows(spots, square_sum(spots), False)
    members = jnp.where(lax.broadcasted_iota(jnp.int32, (NW, 1024), 0) == names, 1.0, 0.0)
    triangle = jnp.where(
        lax.broadcasted_iota(jnp.int32, (128, 128), 0) <= lax.broadcasted_iota(jnp.int32, (128, 128), 1),
        1.0,
        0.0,
    ).astype(BF)
    pieces = jnp.concatenate([members[:, 128 * k : 128 * (k + 1)] for k in range(8)], axis=0)
    running = jnp.dot(pieces.astype(BF), triangle, preferred_element_type=F32)
    before = jnp.zeros((NW, 1), F32)
    ranks = []
    for k in range(8):
        part = running[NW * k : NW * (k + 1)]
        ranks.append(part + before)
        before = before + part[:, 127:128]
    rank = jnp.sum(members * jnp.concatenate(ranks, axis=1), axis=0, keepdims=True) - 1.0
    slot = names * 128 + rank.astype(jnp.int32)

    own = mine[...]
    place = centred(own)
    weight = square_sum(place) + 0.5 * own[6:7] * own[6:7]
    identity = jnp.where(
        lax.broadcasted_iota(jnp.int32, (256, 256), 0) == lax.broadcasted_iota(jnp.int32, (256, 256), 1),
        1.0,
        0.0,
    ).astype(BF)
    targets_ref[...] = dot_nt(identity, target_rows(place, weight, True)).astype(BF)
    total[...] = jnp.zeros_like(total)

    for copy in first:
        copy.wait_recv()
    block_here = gathered.at[pair, side]
    second = [
        send(block_here, block_here, send_two, recv_two, turn - 1, (2 * turn, 0)) for turn in range(1, NG)
    ]

    top, bottom = pl.ds(0, 3), pl.ds(13, 3)
    low_rows, high_rows = pl.ds(0, 3), pl.ds(5, 3)
    begin, finish = pl.ds(0, 128), pl.ds(16256, 128)
    middle, before_lanes, after_lanes = pl.ds(256, 16384), pl.ds(128, 128), pl.ds(16640, 128)
    everything, every = pl.ds(0, 16384), pl.ds(0, 16)
    plan = [
        ((-1, 0), top, everything, 0, low_rows, middle),
        ((1, 0), bottom, everything, 0, high_rows, middle),
        ((0, -1), every, begin, 2, every, begin),
        ((0, 1), every, finish, 1, every, begin),
        ((-1, -1), top, begin, 0, low_rows, after_lanes),
        ((-1, 1), top, finish, 0, low_rows, before_lanes),
        ((1, -1), bottom, begin, 0, high_rows, after_lanes),
        ((1, 1), bottom, finish, 0, high_rows, before_lanes),
    ]
    halos = []
    for k, (peer, from_rows, from_lanes, which, to_rows, to_lanes) in enumerate(plan):
        for part, (source, targets) in enumerate(
            [
                (flow.at[:, from_rows, from_lanes], (rows_halo, left_halo, right_halo)),
                (sections.at[from_rows, from_lanes], (kind_rows, kind_left, kind_right)),
            ]
        ):
            target = targets[which].at[:, to_rows, to_lanes] if part == 0 else targets[which].at[to_rows, to_lanes]
            halos.append((peer, describe(source, target, send_halo, recv_halo, 2 * k + part, peer)))

    def within(wake_by, grid_by):
        to_wake, to_grid = wake + wake_by, grid + grid_by
        return (to_wake >= 0) & (to_wake < NW) & (to_grid >= 0) & (to_grid < NG)

    def start_halos():
        for peer, copy in halos:
            pl.when(within(*peer))(copy.start)

    def finish_halos():
        for peer, copy in halos:
            pl.when(within(*peer))(copy.wait_send)
            pl.when(within(-peer[0], -peer[1]))(copy.wait_recv)

    def place_nodes(part, carry):
        start = pl.multiple_of(part * 256, 256)
        chosen = jnp.where(
            lax.broadcasted_iota(jnp.int32, (256, 1024), 0) + part * 256 == slot, 1.0, 0.0
        ).astype(BF)
        points[pl.ds(start, 256), :] = dot_nt(chosen, rows).astype(BF)
        return carry

    lax.fori_loop(0, 8, place_nodes, 0)

    def load_source(block, start):
        tile = gathered[block // 2, lax.rem(block, 2), :, pl.ds(start, CHUNK)]
        live = start + lax.broadcasted_iota(jnp.int32, (1, CHUNK), 1) < counts[block]
        source = centred(tile) + [tile[c : c + 1] for c in range(3, 7)]
        distance, moment, half = source_rows(source, live)
        return distance, moment, source[0:3] + [half]

    def node_slots(block):
        return pl.ds(pl.multiple_of(block * 128, 128), 128)

    def split_two(value):
        high = value.astype(BF)
        return high, (value - high.astype(F32)).astype(BF)

    def near(offset, with_nodes=True):
        block = lax.rem(wake + offset + NW, NW)
        looking = targets_ref[...]
        if with_nodes:
            looking = jnp.concatenate([looking, points[node_slots(block), :]], axis=0)

        def run(step, gained):
            distance, moment, factors = load_source(block, pl.multiple_of(step * CHUNK, CHUNK))
            columns = source_columns(moment, factors)
            columns = jnp.concatenate(columns + [jnp.zeros_like(moment)], axis=0).astype(BF)
            for cut in range(0, CHUNK, 256):
                root = lax.rsqrt(
                    jnp.dot(looking, distance[:, cut : cut + 256], preferred_element_type=F32)
                )
                second_power = root * root
                third = second_power * root
                fifth = third[0:256] * second_power[0:256]
                weights = split_two(fifth)
                if with_nodes:
                    weights += split_two(third[256:384])
                added = dot_nt(jnp.concatenate(weights, axis=0), columns[:, cut : cut + 256])
                gained = added if gained is None else gained + added
            return gained

        gained = None
        for step in range(PB // CHUNK):
            gained = run(step, gained)
        total[...] += gained[0:256] + gained[256:512]
        if not with_nodes:
            return
        sums = gained[512:640] + gained[640:768]
        node_total[node_slots(block), :] = sums[:, 0:8] + sums[:, 40:48] + sums[:, 80:88]

    def far(offset):
        block = lax.rem(wake + offset + NW, NW)
        looking = points[node_slots(block), :]
        gained = None
        for step in range(PB // CHUNK):
            distance, moment, _ = load_source(block, pl.multiple_of(step * CHUNK, CHUNK))
            columns = source_columns(moment, [])
            columns = jnp.concatenate(columns + [jnp.zeros_like(moment)], axis=0).astype(BF)
            root = lax.rsqrt(jnp.dot(looking, distance, preferred_element_type=F32))
            high, low = split_two(root * root * root)
            added = dot_nt(jnp.concatenate([high, low], axis=0), columns)
            gained = added if gained is None else gained + added
        sums = gained[0:128] + gained[128:256]
        node_total[node_slots(block), :] = sums[:, 0:8] + sums[:, 8:16] + sums[:, 16:24]

    def loop(function, offsets):
        def body(turn, carry):
            function(offsets(turn))
            return carry

        return lambda amount: lax.fori_loop(0, amount, body, 0)

    near(0)
    for copy in second:
        copy.wait_recv()
    third_copy = send(
        gathered.at[:, side], gathered.at[:, side], send_three, recv_three, 0, (1 - 2 * side, 0)
    )
    start_halos()
    loop(near, lambda turn: 2 * turn - 4 + 2 * (turn // 2))(3)
    loop(far, lambda turn: 2 * turn + 4)(4)
    third_copy.wait_recv()
    loop(far, lambda turn: 2 * turn + 1)(6)
    loop(near, lambda turn: 2 * turn - 3)(2)

    answers[...] = jnp.zeros_like(answers)

    def return_nodes(part, carry):
        start = pl.multiple_of(part * 256, 256)
        slot_rows = lax.broadcasted_iota(jnp.int32, (256, 1024), 0) + part * 256
        chosen = jnp.where(slot_rows == slot, 1.0, 0.0).astype(BF)
        named = jnp.sum(jnp.where(slot_rows == slot, 1.0, 0.0), axis=1, keepdims=True) > 0.0
        gained = jnp.where(named, node_total[pl.ds(start, 256), :], 0.0)
        high, mid, low = split_three(gained)
        stacked = jnp.concatenate([high, mid, low, jnp.zeros_like(low)], axis=1).astype(BF)
        answers[...] += lax.dot_general(
            stacked, chosen, (((0,), (0,)), ((), ())), preferred_element_type=F32
        )
        return carry

    lax.fori_loop(0, 8, return_nodes, 0)
    found = answers[0:8] + answers[8:16] + answers[16:24]
    moved = cross_rows(spots, [found[c : c + 1] for c in range(3)])
    for c in range(3):
        result = (moved[c] - found[3 + c : 4 + c]) * SCALE
        even = jnp.concatenate([result[:, 128 * k : 128 * (k + 1)] for k in range(8)], axis=0)
        odd = pltpu.roll(even, 64, 1)
        own_nodes[c] = jnp.concatenate(
            [(even, odd)[r % 2][r // 2 : r // 2 + 1] for r in range(16)], axis=0
        )
    shared = [
        send(own_nodes, far_nodes.at[k], send_node, recv_node, k, peer)
        for k, peer in enumerate([(0, -1), (-1, 0), (1, 0), (-1, -1), (1, -1)])
    ]

    loop(lambda offset: near(offset, False), lambda turn: 2 * turn + 1)(2)

    spin = [own[3 + c : 4 + c] for c in range(3)]
    sums = jnp.transpose(total[...])
    sums = sums[0:40] + sums[40:80] + sums[80:120]
    plain = [sums[k : k + 1] for k in range(6)]
    turned = [[sums[8 + 8 * c + k : 9 + 8 * c + k] for k in range(6)] for c in range(3)]
    heavy = [sums[32 + k : 33 + k] for k in range(6)]
    mixed = [
        weight * plain[k]
        + heavy[k]
        - 2.0 * (place[0] * turned[0][k] + place[1] * turned[1][k] + place[2] * turned[2][k])
        for k in range(6)
    ]
    live = grid * 256 + lax.broadcasted_iota(jnp.int32, (1, 256), 1) < counts[wake]
    factor = jnp.where(live, SCALE, 0.0)
    swept = cross_rows(place, mixed[0:3])
    bent_own = cross_rows(place, plain[0:3])
    along = spin[0] * place[0] + spin[1] * place[1] + spin[2] * place[2]
    pulled = [spin[0] * turned[0][k] + spin[1] * turned[1][k] + spin[2] * turned[2][k] for k in range(6)]
    bent_far = cross_rows(place, pulled[0:3])
    lifted = cross_rows(spin, mixed[0:3])
    for c in range(3):
        velocity_out[c : c + 1, :] = (swept[c] - mixed[3 + c]) * factor
        bent = along * (bent_own[c] - plain[3 + c]) - (bent_far[c] - pulled[3 + c])
        stretch_out[c : c + 1, :] = (lifted[c] - 3.0 * bent) * factor

    for copy in shared:
        copy.wait()
    finish_halos()
    for copy in first + second + [third_copy]:
        copy.wait_send()


ANY = pl.BlockSpec(memory_space=pltpu.HBM)
SCALAR = pl.BlockSpec(memory_space=pltpu.SMEM)


def gather_and_sum(counts, place, spin, core, node_place, node_block, flow, sections):
    dma = pltpu.SemaphoreType.DMA
    return pl.pallas_call(
        gather_kernel,
        out_shape=[
            jax.ShapeDtypeStruct((3, 256), F32),
            jax.ShapeDtypeStruct((3, 256), F32),
            jax.ShapeDtypeStruct((3, 16, 128), F32),
            jax.ShapeDtypeStruct((5, 3, 16, 128), F32),
            jax.ShapeDtypeStruct((5, 8, BUFFER), F32),
            jax.ShapeDtypeStruct((5, 16, 128), F32),
            jax.ShapeDtypeStruct((5, 16, 128), F32),
            jax.ShapeDtypeStruct((8, BUFFER), jnp.int32),
            jax.ShapeDtypeStruct((16, 128), jnp.int32),
            jax.ShapeDtypeStruct((16, 128), jnp.int32),
        ],
        in_specs=[SCALAR] + [ANY] * 7,
        out_specs=[WHOLE] * 4 + [ANY] * 6,
        scratch_shapes=[
            pltpu.VMEM((NW // 2, 2, 8, PB), F32),
            pltpu.VMEM((3, 3, 256), F32),
            pltpu.VMEM((3, 1024), F32),
            pltpu.VMEM((1, 1024), jnp.int32),
            pltpu.VMEM((NW * 128, 48), BF),
            pltpu.VMEM((256, 48), BF),
            pltpu.VMEM((256, 128), F32),
            pltpu.VMEM((NW * 128, 8), F32),
            pltpu.VMEM((32, 1024), F32),
            dma((5,)),
            dma((NG - 1,)),
            dma((NG - 1,)),
            dma((NG - 1,)),
            dma((NG - 1,)),
            dma((1,)),
            dma((1,)),
            dma((16,)),
            dma((16,)),
            dma((5,)),
            dma((5,)),
        ],
        compiler_params=pltpu.CompilerParams(
            collective_id=0, has_side_effects=True, vmem_limit_bytes=LIMIT
        ),
    )(counts, place, spin, core, node_place, node_block, flow, sections)


TILES = 130
STEPS = 130 // TILES
BUFFER = 16640 + 256


def sweep_kernel(
    flow, sections, viscosity, rows_halo, left_halo, right_halo, kind_rows, kind_left, kind_right,
    own_nodes, far_nodes, velocity, stretch, out, velocity_out, stretch_out,
    rows_in, kind, first, second, rates, rows_out, nodes, sem_in, sem_out,
):
    fields = 5
    wake = lax.axis_index("wake")
    grid = lax.axis_index("grid")
    own_rows, halo_rows = pl.ds(0, 16), pl.ds(16, 8)
    middle, before, after = pl.ds(256, 16384), pl.ds(128, 128), pl.ds(16640, 128)
    kinds = [
        pltpu.make_async_copy(source, target, sem_in.at[4 * fields + k])
        for k, (source, target) in enumerate(
            [
                (sections, kind.at[own_rows, middle]),
                (kind_rows, kind.at[halo_rows, :]),
                (kind_left, kind.at[own_rows, before]),
                (kind_right, kind.at[own_rows, after]),
            ]
        )
    ]
    def incoming(f):
        return [
            pltpu.make_async_copy(source, target, sem_in.at[4 * f + k])
            for k, (source, target) in enumerate(
                [
                    (flow.at[f], rows_in.at[f, own_rows, middle]),
                    (rows_halo.at[f], rows_in.at[f, halo_rows, :]),
                    (left_halo.at[f], rows_in.at[f, own_rows, before]),
                    (right_halo.at[f], rows_in.at[f, own_rows, after]),
                ]
            )
        ]

    def outgoing(f):
        return pltpu.make_async_copy(rows_out.at[f, :, middle], out.at[f], sem_out.at[f])

    for copy in kinds + incoming(0):
        copy.start()
    velocity_out[...] = velocity[...]
    stretch_out[...] = stretch[...]

    lane = lax.broadcasted_iota(jnp.int32, (24, 128), 1)
    row = lax.broadcasted_iota(jnp.int32, (24, 128), 0)
    is_first, is_last = lane == 0, lane == 127
    inside_rows = ((row < 20) | (wake > 0)) & ((row < 16) | (row >= 20) | (wake < NW - 1))
    lane8 = lax.broadcasted_iota(jnp.int32, (8, 128), 1)
    row8 = lax.broadcasted_iota(jnp.int32, (8, 128), 0)

    for c in range(3):
        def with_next(rows, column):
            return jnp.where(lane8 == 64, jnp.broadcast_to(column, (8, 128)), rows)

        halo = jnp.where(row8 < 4, far_nodes[1, c, 0:8], far_nodes[2, c, 8:16])
        halo_next = jnp.where(row8 < 4, far_nodes[3, c, 0:8], far_nodes[4, c, 8:16])
        parts = [
            with_next(own_nodes[c, 0:8], far_nodes[0, c, 0:8, 0:1]),
            with_next(own_nodes[c, 8:16], far_nodes[0, c, 8:16, 0:1]),
            with_next(halo, halo_next[:, 0:1]),
        ]
        nodes[c] = jnp.where(inside_rows, jnp.concatenate(parts, axis=0), 0.0)

    for copy in kinds:
        copy.wait()

    tile_lanes = lambda t: pl.ds(pl.multiple_of(t * 128, 128), 128)

    def field(f, done):
        for copy in incoming(f):
            copy.wait()

        @pl.when(f + 1 < fields)
        def _():
            for copy in incoming(f + 1):
                copy.start()

        rows_in[f, 16:24, 256:16640] = jnp.where(
            inside_rows[16:24, 0:1], rows_in[f, 16:24, 256:16640], 0.0
        )
        for start, edge in ((128, grid == 0), (16640, grid == NG - 1)):
            keep = inside_rows & jnp.logical_not(edge)
            rows_in[f, :, start : start + 128] = jnp.where(keep, rows_in[f, :, start : start + 128], 0.0)
        @pl.when((f >= 1) & (f <= 3))
        def _():
            given = nodes[jnp.clip(f - 1, 0, 2)]
            for k in range(65):
                start = 256 + 256 * k
                column = jnp.broadcast_to(given[:, k : k + 1], (24, 128))
                if k == 64:
                    column = jnp.where(grid == NG - 1, 0.0, column)
                rows_in[f, :, start : start + 128] = jnp.where(
                    is_first, column, rows_in[f, :, start : start + 128]
                )

        def sweep(load, finish):
            def body(step, carry):
                last_right, here, right, left = carry
                for k in range(TILES):
                    t = step * TILES + k + 1
                    following = load(t + 1)
                    next_right = pltpu.roll(following, 1, 1)
                    next_left = pltpu.roll(following, 127, 1)
                    across = jnp.where(is_first, last_right, right) + jnp.where(is_last, next_left, left)
                    along = pltpu.roll(here, 1, 0) + pltpu.roll(here, 23, 0)
                    finish(t, here, across + along)
                    last_right, here, right, left = right, following, next_right, next_left
                return last_right, here, right, left

            start = load(1)
            lax.fori_loop(
                0, STEPS, body, (pltpu.roll(load(0), 1, 1), start, pltpu.roll(start, 1, 1), pltpu.roll(start, 127, 1))
            )

        def finish_first(t, here, beside):
            name = kind[:, tile_lanes(t)]
            rate = jnp.where(
                name == 0, viscosity[0, f], jnp.where(name == 1, viscosity[1, f], viscosity[2, f])
            )
            keep = inside_rows & jnp.logical_not(((t == 1) & (grid == 0)) | ((t == 130) & (grid == NG - 1)))
            rate = jnp.where(keep, rate, 0.0)
            rates[:, tile_lanes(t)] = rate
            first[:, tile_lanes(t)] = here + rate * (beside - 4.0 * here)

        def finish_second(t, here, beside):
            second[:, tile_lanes(t)] = here + rates[:, tile_lanes(t)] * (beside - 4.0 * here)

        def finish_third(t, here, beside):
            rows_out[f, :, tile_lanes(t)] = (here + rates[:, tile_lanes(t)] * (beside - 4.0 * here))[0:16]

        sweep(lambda t: rows_in[f, :, tile_lanes(t)], finish_first)
        sweep(lambda t: first[:, tile_lanes(t)], finish_second)
        sweep(lambda t: second[:, tile_lanes(t)], finish_third)
        outgoing(f).start()
        return done

    lax.fori_loop(0, fields, field, 0)
    for f in range(fields):
        outgoing(f).wait()


def sweep_fields(*arrays):
    dma = pltpu.SemaphoreType.DMA
    return pl.pallas_call(
        sweep_kernel,
        out_shape=[
            jax.ShapeDtypeStruct((5, 16, 16384), F32),
            jax.ShapeDtypeStruct((3, 256), F32),
            jax.ShapeDtypeStruct((3, 256), F32),
        ],
        in_specs=[ANY, ANY, SCALAR] + [ANY] * 6 + [WHOLE] * 4,
        out_specs=[ANY, WHOLE, WHOLE],
        scratch_shapes=[
            pltpu.VMEM((5, 24, BUFFER), F32),
            pltpu.VMEM((24, BUFFER), jnp.int32),
            pltpu.VMEM((24, BUFFER), F32),
            pltpu.VMEM((24, BUFFER), F32),
            pltpu.VMEM((24, BUFFER), F32),
            pltpu.VMEM((5, 16, BUFFER), F32),
            pltpu.VMEM((3, 24, 128), F32),
            dma((24,)),
            dma((5,)),
        ],
        compiler_params=pltpu.CompilerParams(vmem_limit_bytes=LIMIT),
    )(*arrays)


def on_device(
    flow,
    section_map,
    viscosity,
    particle_position,
    particle_strength,
    particle_core,
    shed_counts,
    node_position,
    node_block,
):
    (
        velocity, stretch, own_nodes, far_nodes, rows_halo, left_halo, right_halo, kind_rows, kind_left, kind_right,
    ) = gather_and_sum(
        shed_counts,
        particle_position,
        particle_strength,
        particle_core.reshape(1, 256),
        node_position,
        node_block.reshape(1, 1024),
        flow,
        section_map,
    )
    field, velocity, stretch = sweep_fields(
        flow, section_map, viscosity, rows_halo, left_halo, right_halo, kind_rows, kind_left, kind_right,
        own_nodes, far_nodes, velocity, stretch,
    )
    return (field, velocity, stretch)


def solution(mesh):
    return jax.shard_map(
        on_device,
        mesh=mesh,
        in_specs=(
            P(None, "wake", "grid"),
            P("wake", "grid"),
            P(),
            P(None, ("wake", "grid")),
            P(None, ("wake", "grid")),
            P(("wake", "grid")),
            P(),
            P(None, ("wake", "grid")),
            P(("wake", "grid"), None),
        ),
        out_specs=(P(None, "wake", "grid"), P(None, ("wake", "grid")), P(None, ("wake", "grid"))),
        check_vma=False,
    )
```

```python
import math

import jax
import jax.numpy as jnp
from jax import lax
from jax.experimental import pallas as pl
from jax.experimental.pallas import tpu as pltpu
from jax.sharding import PartitionSpec as P

PB = 2048
NW = 16
NG = 8
CHUNK = 512
LIMIT = 64 << 20
BF = jnp.bfloat16
F32 = jnp.float32
MESH = pl.DeviceIdType.MESH
SCALE = -1.0 / (4.0 * math.pi)
WHOLE = pl.BlockSpec(memory_space=pltpu.VMEM)


def split_three(value):
    high = value.astype(BF).astype(F32)
    rest = value - high
    middle = rest.astype(BF).astype(F32)
    return high, middle, rest - middle


def dot_nt(first, second):
    return lax.dot_general(first, second, (((1,), (1,)), ((), ())), preferred_element_type=F32)


def cross_rows(first, second):
    return [
        first[1] * second[2] - first[2] * second[1],
        first[2] * second[0] - first[0] * second[2],
        first[0] * second[1] - first[1] * second[0],
    ]


def target_rows(place, weight, halved):
    ones = jnp.ones_like(weight)
    none = jnp.zeros_like(weight)
    parts = split_three(jnp.concatenate([weight, none, none] + [-2.0 * row for row in place] + [none, none], axis=0))
    unit = jnp.concatenate([none] * 6 + [none if halved else ones, ones if halved else none], axis=0)
    high, middle, low = parts
    return jnp.concatenate([high + unit, middle, low, high + unit, middle, high + unit], axis=0).astype(BF)


def source_columns(moment, factors):
    parts = [split_three(moment)] + [split_three(moment * factor) for factor in factors]
    columns = [part[level] for level in range(3) for part in parts]
    return columns


def centred(rows, centre):
    return [rows[c : c + 1] - centre[c][:, 0 : rows.shape[1]] for c in range(3)]


def square_sum(place):
    return place[0] * place[0] + place[1] * place[1] + place[2] * place[2]


def gather_kernel(
    counts, place_in, spin_in, core_in, node_place_in, node_block_in, flow, sections,
    velocity_out, stretch_out, own_nodes, far_nodes, rows_halo, left_halo, right_halo,
    kind_rows, kind_left, kind_right,
    gathered, share, node_place, node_block, points, targets_ref, total, node_total,
    sem_in, send_one, recv_one, send_two, recv_two, send_three, recv_three,
    send_halo, recv_halo, send_node, recv_node,
):
    wake = lax.axis_index("wake")
    grid = lax.axis_index("grid")
    side = lax.rem(wake, 2)
    pair = wake // 2
    lanes = pl.ds(pl.multiple_of(grid * 256, 256), 256)
    mine = gathered.at[pair, side, :, lanes]

    def device(wake_by, grid_by):
        return {"wake": lax.rem(wake + wake_by + NW, NW), "grid": lax.rem(grid + grid_by + NG, NG)}

    loads = [
        pltpu.make_async_copy(source, target, sem_in.at[k])
        for k, (source, target) in enumerate(
            [
                (place_in, share.at[0]),
                (spin_in, share.at[1]),
                (core_in, share.at[2, pl.ds(0, 1)]),
                (node_place_in, node_place),
                (node_block_in, node_block),
            ]
        )
    ]
    for load in loads:
        load.start()

    peers = [(0, turn) for turn in range(1, NG)] + [(2 * turn, 0) for turn in range(1, NG)]
    peers += [(1, 0), (-1, 0), (1, 1), (1, -1), (-1, 1), (-1, -1)]
    barrier = pltpu.get_barrier_semaphore()
    for peer in peers:
        pl.semaphore_signal(barrier, inc=1, device_id=device(*peer), device_id_type=MESH)
    for load in loads:
        load.wait()
    own_live = grid * 256 + lax.broadcasted_iota(jnp.int32, (1, 256), 1) < counts[wake]
    squared_core = share[2, 0:1] * share[2, 0:1]
    mine[...] = jnp.concatenate(
        [jnp.where(own_live, share[1], 0.0), share[0], squared_core, 0.5 * squared_core], axis=0
    )
    pl.semaphore_wait(barrier, len(peers))

    def describe(source, target, sends, recvs, slot, peer):
        return pltpu.make_async_remote_copy(
            src_ref=source,
            dst_ref=target,
            send_sem=sends.at[slot],
            recv_sem=recvs.at[slot],
            device_id=device(*peer),
            device_id_type=MESH,
        )

    def send(*arguments):
        copy = describe(*arguments)
        copy.start()
        return copy

    own = mine[...]
    centre = [
        jnp.broadcast_to(jnp.sum(own[3 + c : 4 + c], axis=1, keepdims=True) * (1.0 / 256.0), (1, 1024))
        for c in range(3)
    ]
    first = [send(mine, mine, send_one, recv_one, turn - 1, (0, turn)) for turn in range(1, NG)]

    names = node_block[...]
    spots = centred(node_place, centre)
    rows = target_rows(spots, square_sum(spots), False)
    members = jnp.where(lax.broadcasted_iota(jnp.int32, (NW, 1024), 0) == names, 1.0, 0.0)
    triangle = jnp.where(
        lax.broadcasted_iota(jnp.int32, (128, 128), 0) <= lax.broadcasted_iota(jnp.int32, (128, 128), 1),
        1.0,
        0.0,
    ).astype(BF)
    pieces = jnp.concatenate([members[:, 128 * k : 128 * (k + 1)] for k in range(8)], axis=0)
    running = jnp.dot(pieces.astype(BF), triangle, preferred_element_type=F32)
    before = jnp.zeros((NW, 1), F32)
    ranks = []
    for k in range(8):
        part = running[NW * k : NW * (k + 1)]
        ranks.append(part + before)
        before = before + part[:, 127:128]
    rank = jnp.sum(members * jnp.concatenate(ranks, axis=1), axis=0, keepdims=True) - 1.0
    slot = names * 128 + rank.astype(jnp.int32)
    slot_eight = lax.broadcasted_iota(jnp.int32, (128, 8), 0).astype(F32)

    place = centred(own[3:6], centre)
    weight = square_sum(place) + own[7:8]
    identity = jnp.where(
        lax.broadcasted_iota(jnp.int32, (256, 256), 0) == lax.broadcasted_iota(jnp.int32, (256, 256), 1),
        1.0,
        0.0,
    ).astype(BF)
    targets_ref[...] = dot_nt(identity, target_rows(place, weight, True)).astype(BF)
    total[...] = jnp.zeros_like(total)

    for copy in first:
        copy.wait_recv()
    block_here = gathered.at[pair, side]
    second = [
        send(block_here, block_here, send_two, recv_two, turn - 1, (2 * turn, 0)) for turn in range(1, NG)
    ]

    top, bottom = pl.ds(0, 3), pl.ds(13, 3)
    low_rows, high_rows = pl.ds(0, 3), pl.ds(5, 3)
    begin, finish = pl.ds(0, 128), pl.ds(16256, 128)
    middle, before_lanes, after_lanes = pl.ds(256, 16384), pl.ds(128, 128), pl.ds(16640, 128)
    everything, every = pl.ds(0, 16384), pl.ds(0, 16)
    plan = [
        ((-1, 0), top, everything, 0, low_rows, middle),
        ((1, 0), bottom, everything, 0, high_rows, middle),
        ((0, -1), every, begin, 2, every, begin),
        ((0, 1), every, finish, 1, every, begin),
        ((-1, -1), top, begin, 0, low_rows, after_lanes),
        ((-1, 1), top, finish, 0, low_rows, before_lanes),
        ((1, -1), bottom, begin, 0, high_rows, after_lanes),
        ((1, 1), bottom, finish, 0, high_rows, before_lanes),
    ]
    halos = []
    for k, (peer, from_rows, from_lanes, which, to_rows, to_lanes) in enumerate(plan):
        for part, (source, targets) in enumerate(
            [
                (flow.at[:, from_rows, from_lanes], (rows_halo, left_halo, right_halo)),
                (sections.at[from_rows, from_lanes], (kind_rows, kind_left, kind_right)),
            ]
        ):
            target = targets[which].at[:, to_rows, to_lanes] if part == 0 else targets[which].at[to_rows, to_lanes]
            halos.append((peer, describe(source, target, send_halo, recv_halo, 2 * k + part, peer)))

    def within(wake_by, grid_by):
        to_wake, to_grid = wake + wake_by, grid + grid_by
        return (to_wake >= 0) & (to_wake < NW) & (to_grid >= 0) & (to_grid < NG)

    def start_halos():
        for peer, copy in halos:
            pl.when(within(*peer))(copy.start)

    def finish_halos():
        for peer, copy in halos:
            pl.when(within(*peer))(copy.wait_send)
            pl.when(within(-peer[0], -peer[1]))(copy.wait_recv)

    for part in range(8):
        chosen = jnp.where(
            lax.broadcasted_iota(jnp.int32, (256, 1024), 0) + part * 256 == slot, 1.0, 0.0
        ).astype(BF)
        points[256 * part : 256 * (part + 1), :] = dot_nt(chosen, rows).astype(BF)

    line = lax.broadcasted_iota(jnp.int32, (8, CHUNK), 0)
    is_place = (line >= 3) & (line < 6)
    shift = jnp.zeros((8, CHUNK), F32)
    for c in range(3):
        shift = jnp.where(line == 3 + c, jnp.broadcast_to(centre[c][:, 0:CHUNK], (8, CHUNK)), shift)

    def load_source(block, start):
        tile = gathered[block // 2, lax.rem(block, 2), :, pl.ds(start, CHUNK)] - shift
        summed = jnp.where(is_place, tile * tile, 0.0)
        for step in (4, 2, 1):
            summed = summed + pltpu.roll(summed, step, 0)
        full = tile + jnp.where(line >= 6, summed, 0.0)
        high, middle, low = split_three(jnp.where(line == 0, 1.0, full))
        distance = jnp.concatenate([high, high, high, middle, middle, low], axis=0).astype(BF)
        down_one, down_two = pltpu.roll(tile, 1, 0), pltpu.roll(tile, 2, 0)
        place_next = jnp.where(line == 5, down_two, pltpu.roll(tile, 7, 0))
        place_last = jnp.where(line == 3, pltpu.roll(tile, 6, 0), down_one)
        spin_next = jnp.where(line == 5, pltpu.roll(tile, 5, 0), down_two)
        spin_last = jnp.where(line == 3, down_one, pltpu.roll(tile, 4, 0))
        crossed = place_next * spin_last - place_last * spin_next
        moment = jnp.where(line < 3, tile, jnp.where(line < 6, crossed, 0.0))
        return distance, moment, [full[k : k + 1] for k in (3, 4, 5, 7)]

    def node_slots(block):
        return pl.ds(pl.multiple_of(block * 128, 128), 128)

    def split_two(value):
        high = value.astype(BF)
        return high, (value - high.astype(F32)).astype(BF)

    def near(offset, with_nodes=True):
        block = lax.rem(wake + offset + NW, NW)
        looking = targets_ref[...]
        if with_nodes:
            looking = jnp.concatenate([looking, points[node_slots(block), :]], axis=0)

        def run(step, gained):
            distance, moment, factors = load_source(block, pl.multiple_of(step * CHUNK, CHUNK))
            columns = source_columns(moment, factors)
            columns = jnp.concatenate(columns + [jnp.zeros_like(moment)], axis=0).astype(BF)
            for cut in range(0, CHUNK, 256):
                root = lax.rsqrt(
                    jnp.dot(looking, distance[:, cut : cut + 256], preferred_element_type=F32)
                )
                second_power = root * root
                third = second_power * root
                fifth = third[0:256] * second_power[0:256]
                weights = split_two(fifth)
                if with_nodes:
                    weights += split_two(third[256:384])
                added = dot_nt(jnp.concatenate(weights, axis=0), columns[:, cut : cut + 256])
                gained = added if gained is None else gained + added
            return gained

        gained = None
        for step in range(PB // CHUNK):
            gained = run(step, gained)
        total[...] += gained[0:256] + gained[256:512]
        if not with_nodes:
            return
        sums = gained[512:640] + gained[640:768]
        node_total[node_slots(block), :] = sums[:, 0:8] + sums[:, 40:48] + sums[:, 80:88]

    def far(offset):
        block = lax.rem(wake + offset + NW, NW)
        looking = points[node_slots(block), :]
        gained = None
        for step in range(PB // CHUNK):
            distance, moment, _ = load_source(block, pl.multiple_of(step * CHUNK, CHUNK))
            columns = source_columns(moment, [])
            columns = jnp.concatenate(columns + [jnp.zeros_like(moment)], axis=0).astype(BF)
            root = lax.rsqrt(jnp.dot(looking, distance, preferred_element_type=F32))
            high, low = split_two(root * root * root)
            added = dot_nt(jnp.concatenate([high, low], axis=0), columns)
            gained = added if gained is None else gained + added
        sums = gained[0:128] + gained[128:256]
        node_total[node_slots(block), :] = sums[:, 0:8] + sums[:, 8:16] + sums[:, 16:24]

    def loop(function, offsets):
        def body(turn, carry):
            function(offsets(turn))
            return carry

        return lambda amount: lax.fori_loop(0, amount, body, 0)

    near(0)
    for copy in second:
        copy.wait_recv()
    third_copy = send(
        gathered.at[:, side], gathered.at[:, side], send_three, recv_three, 0, (1 - 2 * side, 0)
    )
    start_halos()
    loop(near, lambda turn: 2 * turn - 4 + 2 * (turn // 2))(3)
    loop(lambda offset: [far(offset + 2 * k) for k in range(4)], lambda turn: 4 + turn)(1)
    third_copy.wait_recv()
    loop(lambda offset: [far(offset + 2 * k) for k in range(3)], lambda turn: 6 * turn + 1)(2)
    loop(near, lambda turn: 2 * turn - 3)(2)

    answers = None
    for part in range(8):
        slot_rows = lax.broadcasted_iota(jnp.int32, (256, 1024), 0) + part * 256
        chosen = jnp.where(slot_rows == slot, 1.0, 0.0).astype(BF)
        gained = jnp.concatenate(
            [
                jnp.where(
                    slot_eight < before[block : block + 1],
                    node_total[128 * block : 128 * (block + 1), :],
                    0.0,
                )
                for block in (2 * part, 2 * part + 1)
            ],
            axis=0,
        )
        high, mid, low = split_three(gained)
        stacked = jnp.concatenate([high, mid, low, jnp.zeros_like(low)], axis=1).astype(BF)
        added = lax.dot_general(stacked, chosen, (((0,), (0,)), ((), ())), preferred_element_type=F32)
        answers = added if answers is None else answers + added
    found = answers[0:8] + answers[8:16] + answers[16:24]
    moved = cross_rows(spots, [found[c : c + 1] for c in range(3)])
    for c in range(3):
        result = (moved[c] - found[3 + c : 4 + c]) * SCALE
        even = jnp.concatenate([result[:, 128 * k : 128 * (k + 1)] for k in range(8)], axis=0)
        odd = pltpu.roll(even, 64, 1)
        own_nodes[c] = jnp.concatenate(
            [(even, odd)[r % 2][r // 2 : r // 2 + 1] for r in range(16)], axis=0
        )
    shared = [
        send(own_nodes, far_nodes.at[k], send_node, recv_node, k, peer)
        for k, peer in enumerate([(0, -1), (-1, 0), (1, 0), (-1, -1), (1, -1)])
    ]

    loop(lambda offset: near(offset, False), lambda turn: 2 * turn + 1)(2)

    spin = [own[c : c + 1] for c in range(3)]
    sums = jnp.transpose(total[...])
    sums = sums[0:40] + sums[40:80] + sums[80:120]
    plain = [sums[k : k + 1] for k in range(6)]
    turned = [[sums[8 + 8 * c + k : 9 + 8 * c + k] for k in range(6)] for c in range(3)]
    heavy = [sums[32 + k : 33 + k] for k in range(6)]
    mixed = [
        weight * plain[k]
        + heavy[k]
        - 2.0 * (place[0] * turned[0][k] + place[1] * turned[1][k] + place[2] * turned[2][k])
        for k in range(6)
    ]
    live = grid * 256 + lax.broadcasted_iota(jnp.int32, (1, 256), 1) < counts[wake]
    factor = jnp.where(live, SCALE, 0.0)
    swept = cross_rows(place, mixed[0:3])
    bent_own = cross_rows(place, plain[0:3])
    along = spin[0] * place[0] + spin[1] * place[1] + spin[2] * place[2]
    pulled = [spin[0] * turned[0][k] + spin[1] * turned[1][k] + spin[2] * turned[2][k] for k in range(6)]
    bent_far = cross_rows(place, pulled[0:3])
    lifted = cross_rows(spin, mixed[0:3])
    for c in range(3):
        velocity_out[c : c + 1, :] = (swept[c] - mixed[3 + c]) * factor
        bent = along * (bent_own[c] - plain[3 + c]) - (bent_far[c] - pulled[3 + c])
        stretch_out[c : c + 1, :] = (lifted[c] - 3.0 * bent) * factor

    for copy in shared:
        copy.wait()
    finish_halos()
    for copy in first + second + [third_copy]:
        copy.wait_send()


ANY = pl.BlockSpec(memory_space=pltpu.HBM)
SCALAR = pl.BlockSpec(memory_space=pltpu.SMEM)


def gather_and_sum(counts, place, spin, core, node_place, node_block, flow, sections):
    dma = pltpu.SemaphoreType.DMA
    return pl.pallas_call(
        gather_kernel,
        out_shape=[
            jax.ShapeDtypeStruct((3, 256), F32),
            jax.ShapeDtypeStruct((3, 256), F32),
            jax.ShapeDtypeStruct((3, 16, 128), F32),
            jax.ShapeDtypeStruct((5, 3, 16, 128), F32),
            jax.ShapeDtypeStruct((5, 8, BUFFER), F32),
            jax.ShapeDtypeStruct((5, 16, 128), F32),
            jax.ShapeDtypeStruct((5, 16, 128), F32),
            jax.ShapeDtypeStruct((8, BUFFER), jnp.int32),
            jax.ShapeDtypeStruct((16, 128), jnp.int32),
            jax.ShapeDtypeStruct((16, 128), jnp.int32),
        ],
        in_specs=[SCALAR] + [ANY] * 7,
        out_specs=[WHOLE] * 4 + [ANY] * 6,
        scratch_shapes=[
            pltpu.VMEM((NW // 2, 2, 8, PB), F32),
            pltpu.VMEM((3, 3, 256), F32),
            pltpu.VMEM((3, 1024), F32),
            pltpu.VMEM((1, 1024), jnp.int32),
            pltpu.VMEM((NW * 128, 48), BF),
            pltpu.VMEM((256, 48), BF),
            pltpu.VMEM((256, 128), F32),
            pltpu.VMEM((NW * 128, 8), F32),
            dma((5,)),
            dma((NG - 1,)),
            dma((NG - 1,)),
            dma((NG - 1,)),
            dma((NG - 1,)),
            dma((1,)),
            dma((1,)),
            dma((16,)),
            dma((16,)),
            dma((5,)),
            dma((5,)),
        ],
        compiler_params=pltpu.CompilerParams(
            collective_id=0, has_side_effects=True, vmem_limit_bytes=LIMIT
        ),
    )(counts, place, spin, core, node_place, node_block, flow, sections)


TILES = 130
STEPS = 130 // TILES
BUFFER = 16640 + 256


def sweep_kernel(
    flow, sections, viscosity, rows_halo, left_halo, right_halo, kind_rows, kind_left, kind_right,
    own_nodes, far_nodes, velocity, stretch, out, velocity_out, stretch_out,
    rows_in, kind, first, second, rates, rows_out, nodes, sem_in, sem_out,
):
    fields = 5
    wake = lax.axis_index("wake")
    grid = lax.axis_index("grid")
    own_rows, halo_rows = pl.ds(0, 16), pl.ds(16, 8)
    middle, before, after = pl.ds(256, 16384), pl.ds(128, 128), pl.ds(16640, 128)
    kinds = [
        pltpu.make_async_copy(source, target, sem_in.at[4 * fields + k])
        for k, (source, target) in enumerate(
            [
                (sections, kind.at[own_rows, middle]),
                (kind_rows, kind.at[halo_rows, :]),
                (kind_left, kind.at[own_rows, before]),
                (kind_right, kind.at[own_rows, after]),
            ]
        )
    ]
    def incoming(f):
        return [
            pltpu.make_async_copy(source, target, sem_in.at[4 * f + k])
            for k, (source, target) in enumerate(
                [
                    (flow.at[f], rows_in.at[f, own_rows, middle]),
                    (rows_halo.at[f], rows_in.at[f, halo_rows, :]),
                    (left_halo.at[f], rows_in.at[f, own_rows, before]),
                    (right_halo.at[f], rows_in.at[f, own_rows, after]),
                ]
            )
        ]

    def outgoing(f):
        return pltpu.make_async_copy(rows_out.at[f, :, middle], out.at[f], sem_out.at[f])

    for copy in kinds + incoming(0):
        copy.start()
    velocity_out[...] = velocity[...]
    stretch_out[...] = stretch[...]

    lane = lax.broadcasted_iota(jnp.int32, (24, 128), 1)
    row = lax.broadcasted_iota(jnp.int32, (24, 128), 0)
    is_first, is_last = lane == 0, lane == 127
    inside_rows = ((row < 20) | (wake > 0)) & ((row < 16) | (row >= 20) | (wake < NW - 1))
    lane8 = lax.broadcasted_iota(jnp.int32, (8, 128), 1)
    row8 = lax.broadcasted_iota(jnp.int32, (8, 128), 0)

    for c in range(3):
        def with_next(rows, column):
            return jnp.where(lane8 == 64, jnp.broadcast_to(column, (8, 128)), rows)

        halo = jnp.where(row8 < 4, far_nodes[1, c, 0:8], far_nodes[2, c, 8:16])
        halo_next = jnp.where(row8 < 4, far_nodes[3, c, 0:8], far_nodes[4, c, 8:16])
        parts = [
            with_next(own_nodes[c, 0:8], far_nodes[0, c, 0:8, 0:1]),
            with_next(own_nodes[c, 8:16], far_nodes[0, c, 8:16, 0:1]),
            with_next(halo, halo_next[:, 0:1]),
        ]
        nodes[c] = jnp.where(inside_rows, jnp.concatenate(parts, axis=0), 0.0)

    for copy in kinds:
        copy.wait()

    tile_lanes = lambda t: pl.ds(pl.multiple_of(t * 128, 128), 128)

    def field(f, done):
        for copy in incoming(f):
            copy.wait()

        @pl.when(f + 1 < fields)
        def _():
            for copy in incoming(f + 1):
                copy.start()

        rows_in[f, 16:24, 256:16640] = jnp.where(
            inside_rows[16:24, 0:1], rows_in[f, 16:24, 256:16640], 0.0
        )
        for start, edge in ((128, grid == 0), (16640, grid == NG - 1)):
            keep = inside_rows & jnp.logical_not(edge)
            rows_in[f, :, start : start + 128] = jnp.where(keep, rows_in[f, :, start : start + 128], 0.0)
        @pl.when((f >= 1) & (f <= 3))
        def _():
            given = nodes[jnp.clip(f - 1, 0, 2)]
            for k in range(65):
                start = 256 + 256 * k
                column = jnp.broadcast_to(given[:, k : k + 1], (24, 128))
                if k == 64:
                    column = jnp.where(grid == NG - 1, 0.0, column)
                rows_in[f, :, start : start + 128] = jnp.where(
                    is_first, column, rows_in[f, :, start : start + 128]
                )

        def sweep(load, finish):
            def body(step, carry):
                last_right, here, right, left = carry
                for k in range(TILES):
                    t = step * TILES + k + 1
                    following = load(t + 1)
                    next_right = pltpu.roll(following, 1, 1)
                    next_left = pltpu.roll(following, 127, 1)
                    across = jnp.where(is_first, last_right, right) + jnp.where(is_last, next_left, left)
                    along = pltpu.roll(here, 1, 0) + pltpu.roll(here, 23, 0)
                    finish(t, here, across + along)
                    last_right, here, right, left = right, following, next_right, next_left
                return last_right, here, right, left

            start = load(1)
            lax.fori_loop(
                0, STEPS, body, (pltpu.roll(load(0), 1, 1), start, pltpu.roll(start, 1, 1), pltpu.roll(start, 127, 1))
            )

        def finish_first(t, here, beside):
            name = kind[:, tile_lanes(t)]
            rate = jnp.where(
                name == 0, viscosity[0, f], jnp.where(name == 1, viscosity[1, f], viscosity[2, f])
            )
            keep = inside_rows & jnp.logical_not(((t == 1) & (grid == 0)) | ((t == 130) & (grid == NG - 1)))
            rate = jnp.where(keep, rate, 0.0)
            rates[:, tile_lanes(t)] = rate
            first[:, tile_lanes(t)] = here + rate * (beside - 4.0 * here)

        def finish_second(t, here, beside):
            second[:, tile_lanes(t)] = here + rates[:, tile_lanes(t)] * (beside - 4.0 * here)

        def finish_third(t, here, beside):
            rows_out[f, :, tile_lanes(t)] = (here + rates[:, tile_lanes(t)] * (beside - 4.0 * here))[0:16]

        sweep(lambda t: rows_in[f, :, tile_lanes(t)], finish_first)
        sweep(lambda t: first[:, tile_lanes(t)], finish_second)
        sweep(lambda t: second[:, tile_lanes(t)], finish_third)
        outgoing(f).start()
        return done

    lax.fori_loop(0, fields, field, 0)
    for f in range(fields):
        outgoing(f).wait()


def sweep_fields(*arrays):
    dma = pltpu.SemaphoreType.DMA
    return pl.pallas_call(
        sweep_kernel,
        out_shape=[
            jax.ShapeDtypeStruct((5, 16, 16384), F32),
            jax.ShapeDtypeStruct((3, 256), F32),
            jax.ShapeDtypeStruct((3, 256), F32),
        ],
        in_specs=[ANY, ANY, SCALAR] + [ANY] * 6 + [WHOLE] * 4,
        out_specs=[ANY, WHOLE, WHOLE],
        scratch_shapes=[
            pltpu.VMEM((5, 24, BUFFER), F32),
            pltpu.VMEM((24, BUFFER), jnp.int32),
            pltpu.VMEM((24, BUFFER), F32),
            pltpu.VMEM((24, BUFFER), F32),
            pltpu.VMEM((24, BUFFER), F32),
            pltpu.VMEM((5, 16, BUFFER), F32),
            pltpu.VMEM((3, 24, 128), F32),
            dma((24,)),
            dma((5,)),
        ],
        compiler_params=pltpu.CompilerParams(vmem_limit_bytes=LIMIT),
    )(*arrays)


def on_device(
    flow,
    section_map,
    viscosity,
    particle_position,
    particle_strength,
    particle_core,
    shed_counts,
    node_position,
    node_block,
):
    (
        velocity, stretch, own_nodes, far_nodes, rows_halo, left_halo, right_halo, kind_rows, kind_left, kind_right,
    ) = gather_and_sum(
        shed_counts,
        particle_position,
        particle_strength,
        particle_core.reshape(1, 256),
        node_position,
        node_block.reshape(1, 1024),
        flow,
        section_map,
    )
    field, velocity, stretch = sweep_fields(
        flow, section_map, viscosity, rows_halo, left_halo, right_halo, kind_rows, kind_left, kind_right,
        own_nodes, far_nodes, velocity, stretch,
    )
    return (field, velocity, stretch)


def solution(mesh):
    return jax.shard_map(
        on_device,
        mesh=mesh,
        in_specs=(
            P(None, "wake", "grid"),
            P("wake", "grid"),
            P(),
            P(None, ("wake", "grid")),
            P(None, ("wake", "grid")),
            P(("wake", "grid")),
            P(),
            P(None, ("wake", "grid")),
            P(("wake", "grid"), None),
        ),
        out_specs=(P(None, "wake", "grid"), P(None, ("wake", "grid")), P(None, ("wake", "grid"))),
        check_vma=False,
    )
```

```python
import math

import jax
import jax.numpy as jnp
from jax import lax
from jax.experimental import pallas as pl
from jax.experimental.pallas import tpu as pltpu
from jax.sharding import PartitionSpec as P

PB = 2048
NW = 16
NG = 8
CHUNK = 512
LIMIT = 64 << 20
BF = jnp.bfloat16
F32 = jnp.float32
MESH = pl.DeviceIdType.MESH
SCALE = -1.0 / (4.0 * math.pi)
WHOLE = pl.BlockSpec(memory_space=pltpu.VMEM)


def split_three(value):
    high = value.astype(BF).astype(F32)
    rest = value - high
    middle = rest.astype(BF).astype(F32)
    return high, middle, rest - middle


def dot_nt(first, second):
    return lax.dot_general(first, second, (((1,), (1,)), ((), ())), preferred_element_type=F32)


def cross_rows(first, second):
    return [
        first[1] * second[2] - first[2] * second[1],
        first[2] * second[0] - first[0] * second[2],
        first[0] * second[1] - first[1] * second[0],
    ]


def target_rows(place, weight, halved):
    ones = jnp.ones_like(weight)
    none = jnp.zeros_like(weight)
    parts = split_three(jnp.concatenate([weight, none, none] + [-2.0 * row for row in place] + [none, none], axis=0))
    unit = jnp.concatenate([none] * 6 + [none if halved else ones, ones if halved else none], axis=0)
    high, middle, low = parts
    return jnp.concatenate([high + unit, middle, low, high + unit, middle, high + unit], axis=0).astype(BF)


def source_columns(moment, factors):
    parts = [split_three(moment)] + [split_three(moment * factor) for factor in factors]
    columns = [part[level] for level in range(3) for part in parts]
    return columns


def centred(rows, centre):
    return [rows[c : c + 1] - centre[c][:, 0 : rows.shape[1]] for c in range(3)]


def square_sum(place):
    return place[0] * place[0] + place[1] * place[1] + place[2] * place[2]


def gather_kernel(
    counts, place_in, spin_in, core_in, node_place_in, node_block_in, flow, sections,
    velocity_out, stretch_out, own_nodes, far_nodes, rows_halo, left_halo, right_halo,
    kind_rows, kind_left, kind_right,
    gathered, share, node_place, node_block, points, targets_ref, total, node_total,
    sem_in, send_one, recv_one, send_two, recv_two, send_three, recv_three,
    send_halo, recv_halo, send_node, recv_node,
):
    wake = lax.axis_index("wake")
    grid = lax.axis_index("grid")
    side = lax.rem(wake, 2)
    pair = wake // 2
    lanes = pl.ds(pl.multiple_of(grid * 256, 256), 256)
    mine = gathered.at[pair, side, :, lanes]

    def device(wake_by, grid_by):
        return {"wake": lax.rem(wake + wake_by + NW, NW), "grid": lax.rem(grid + grid_by + NG, NG)}

    loads = [
        pltpu.make_async_copy(source, target, sem_in.at[k])
        for k, (source, target) in enumerate(
            [
                (place_in, share.at[0]),
                (spin_in, share.at[1]),
                (core_in, share.at[2, pl.ds(0, 1)]),
                (node_place_in, node_place),
                (node_block_in, node_block),
            ]
        )
    ]
    for load in loads:
        load.start()

    peers = [(0, turn) for turn in range(1, NG)] + [(2 * turn, 0) for turn in range(1, NG)]
    peers += [(1, 0), (-1, 0), (1, 1), (1, -1), (-1, 1), (-1, -1)]
    barrier = pltpu.get_barrier_semaphore()
    for peer in peers:
        pl.semaphore_signal(barrier, inc=1, device_id=device(*peer), device_id_type=MESH)
    for load in loads:
        load.wait()
    own_live = grid * 256 + lax.broadcasted_iota(jnp.int32, (1, 256), 1) < counts[wake]
    squared_core = share[2, 0:1] * share[2, 0:1]
    mine[...] = jnp.concatenate(
        [jnp.where(own_live, share[1], 0.0), share[0], squared_core, 0.5 * squared_core], axis=0
    )
    pl.semaphore_wait(barrier, len(peers))

    def describe(source, target, sends, recvs, slot, peer):
        return pltpu.make_async_remote_copy(
            src_ref=source,
            dst_ref=target,
            send_sem=sends.at[slot],
            recv_sem=recvs.at[slot],
            device_id=device(*peer),
            device_id_type=MESH,
        )

    def send(*arguments):
        copy = describe(*arguments)
        copy.start()
        return copy

    own = mine[...]
    centre = [
        jnp.broadcast_to(jnp.sum(own[3 + c : 4 + c], axis=1, keepdims=True) * (1.0 / 256.0), (1, 1024))
        for c in range(3)
    ]
    first = [send(mine, mine, send_one, recv_one, turn - 1, (0, turn)) for turn in range(1, NG)]

    names = node_block[...]
    spots = centred(node_place, centre)
    rows = target_rows(spots, square_sum(spots), False)
    members = jnp.where(lax.broadcasted_iota(jnp.int32, (NW, 1024), 0) == names, 1.0, 0.0)
    triangle = jnp.where(
        lax.broadcasted_iota(jnp.int32, (128, 128), 0) <= lax.broadcasted_iota(jnp.int32, (128, 128), 1),
        1.0,
        0.0,
    ).astype(BF)
    pieces = jnp.concatenate([members[:, 128 * k : 128 * (k + 1)] for k in range(8)], axis=0)
    running = jnp.dot(pieces.astype(BF), triangle, preferred_element_type=F32)
    before = jnp.zeros((NW, 1), F32)
    ranks = []
    for k in range(8):
        part = running[NW * k : NW * (k + 1)]
        ranks.append(part + before)
        before = before + part[:, 127:128]
    rank = jnp.sum(members * jnp.concatenate(ranks, axis=1), axis=0, keepdims=True) - 1.0
    slot = names * 128 + rank.astype(jnp.int32)
    slot_eight = lax.broadcasted_iota(jnp.int32, (128, 8), 0).astype(F32)

    place = centred(own[3:6], centre)
    weight = square_sum(place) + own[7:8]
    identity = jnp.where(
        lax.broadcasted_iota(jnp.int32, (256, 256), 0) == lax.broadcasted_iota(jnp.int32, (256, 256), 1),
        1.0,
        0.0,
    ).astype(BF)
    targets_ref[...] = dot_nt(identity, target_rows(place, weight, True)).astype(BF)
    total[...] = jnp.zeros_like(total)

    for copy in first:
        copy.wait_recv()
    block_here = gathered.at[pair, side]
    second = [
        send(block_here, block_here, send_two, recv_two, turn - 1, (2 * turn, 0)) for turn in (1, 2, 7, 3, 4, 5, 6)
    ]

    top, bottom = pl.ds(0, 3), pl.ds(13, 3)
    low_rows, high_rows = pl.ds(0, 3), pl.ds(5, 3)
    begin, finish = pl.ds(0, 128), pl.ds(16256, 128)
    middle, before_lanes, after_lanes = pl.ds(256, 16384), pl.ds(128, 128), pl.ds(16640, 128)
    everything, every = pl.ds(0, 16384), pl.ds(0, 16)
    plan = [
        ((-1, 0), top, everything, 0, low_rows, middle),
        ((1, 0), bottom, everything, 0, high_rows, middle),
        ((0, -1), every, begin, 2, every, begin),
        ((0, 1), every, finish, 1, every, begin),
        ((-1, -1), top, begin, 0, low_rows, after_lanes),
        ((-1, 1), top, finish, 0, low_rows, before_lanes),
        ((1, -1), bottom, begin, 0, high_rows, after_lanes),
        ((1, 1), bottom, finish, 0, high_rows, before_lanes),
    ]
    halos = []
    for k, (peer, from_rows, from_lanes, which, to_rows, to_lanes) in enumerate(plan):
        for part, (source, targets) in enumerate(
            [
                (flow.at[:, from_rows, from_lanes], (rows_halo, left_halo, right_halo)),
                (sections.at[from_rows, from_lanes], (kind_rows, kind_left, kind_right)),
            ]
        ):
            target = targets[which].at[:, to_rows, to_lanes] if part == 0 else targets[which].at[to_rows, to_lanes]
            halos.append((peer, describe(source, target, send_halo, recv_halo, 2 * k + part, peer)))

    def within(wake_by, grid_by):
        to_wake, to_grid = wake + wake_by, grid + grid_by
        return (to_wake >= 0) & (to_wake < NW) & (to_grid >= 0) & (to_grid < NG)

    def start_halos():
        for peer, copy in halos:
            pl.when(within(*peer))(copy.start)

    def finish_halos():
        for peer, copy in halos:
            pl.when(within(*peer))(copy.wait_send)
            pl.when(within(-peer[0], -peer[1]))(copy.wait_recv)

    for part in range(8):
        chosen = jnp.where(
            lax.broadcasted_iota(jnp.int32, (256, 1024), 0) + part * 256 == slot, 1.0, 0.0
        ).astype(BF)
        points[256 * part : 256 * (part + 1), :] = dot_nt(chosen, rows).astype(BF)

    line = lax.broadcasted_iota(jnp.int32, (8, CHUNK), 0)
    is_place = (line >= 3) & (line < 6)
    shift = jnp.zeros((8, CHUNK), F32)
    for c in range(3):
        shift = jnp.where(line == 3 + c, jnp.broadcast_to(centre[c][:, 0:CHUNK], (8, CHUNK)), shift)

    def load_source(block, start):
        tile = gathered[block // 2, lax.rem(block, 2), :, pl.ds(start, CHUNK)] - shift
        summed = jnp.where(is_place, tile * tile, 0.0)
        for step in (4, 2, 1):
            summed = summed + pltpu.roll(summed, step, 0)
        full = tile + jnp.where(line >= 6, summed, 0.0)
        high, middle, low = split_three(jnp.where(line == 0, 1.0, full))
        distance = jnp.concatenate([high, high, high, middle, middle, low], axis=0).astype(BF)
        down_one, down_two = pltpu.roll(tile, 1, 0), pltpu.roll(tile, 2, 0)
        place_next = jnp.where(line == 5, down_two, pltpu.roll(tile, 7, 0))
        place_last = jnp.where(line == 3, pltpu.roll(tile, 6, 0), down_one)
        spin_next = jnp.where(line == 5, pltpu.roll(tile, 5, 0), down_two)
        spin_last = jnp.where(line == 3, down_one, pltpu.roll(tile, 4, 0))
        crossed = place_next * spin_last - place_last * spin_next
        moment = jnp.where(line < 3, tile, jnp.where(line < 6, crossed, 0.0))
        return distance, moment, [full[k : k + 1] for k in (3, 4, 5, 7)]

    def node_slots(block):
        return pl.ds(pl.multiple_of(block * 128, 128), 128)

    def split_two(value):
        high = value.astype(BF)
        return high, (value - high.astype(F32)).astype(BF)

    def near(offset, with_nodes=True):
        block = lax.rem(wake + offset + NW, NW)
        looking = targets_ref[...]
        if with_nodes:
            looking = jnp.concatenate([looking, points[node_slots(block), :]], axis=0)

        def run(step, gained):
            distance, moment, factors = load_source(block, pl.multiple_of(step * CHUNK, CHUNK))
            columns = source_columns(moment, factors)
            columns = jnp.concatenate(columns + [jnp.zeros_like(moment)], axis=0).astype(BF)
            for cut in range(0, CHUNK, CHUNK):
                root = lax.rsqrt(
                    jnp.dot(looking, distance[:, cut : cut + CHUNK], preferred_element_type=F32)
                )
                second_power = root * root
                third = second_power * root
                fifth = third[0:256] * second_power[0:256]
                weights = split_two(fifth)
                if with_nodes:
                    weights += split_two(third[256:384])
                added = dot_nt(jnp.concatenate(weights, axis=0), columns[:, cut : cut + CHUNK])
                gained = added if gained is None else gained + added
            return gained

        gained = None
        for step in range(PB // CHUNK):
            gained = run(step, gained)
        total[...] += gained[0:256] + gained[256:512]
        if not with_nodes:
            return
        sums = gained[512:640] + gained[640:768]
        node_total[node_slots(block), :] = sums[:, 0:8] + sums[:, 40:48] + sums[:, 80:88]

    def far(offset):
        block = lax.rem(wake + offset + NW, NW)
        looking = points[node_slots(block), :]
        gained = None
        for step in range(PB // CHUNK):
            distance, moment, _ = load_source(block, pl.multiple_of(step * CHUNK, CHUNK))
            columns = source_columns(moment, [])
            columns = jnp.concatenate(columns + [jnp.zeros_like(moment)], axis=0).astype(BF)
            root = lax.rsqrt(jnp.dot(looking, distance, preferred_element_type=F32))
            high, low = split_two(root * root * root)
            added = dot_nt(jnp.concatenate([high, low], axis=0), columns)
            gained = added if gained is None else gained + added
        sums = gained[0:128] + gained[128:256]
        node_total[node_slots(block), :] = sums[:, 0:8] + sums[:, 8:16] + sums[:, 16:24]

    def loop(function, offsets):
        def body(turn, carry):
            function(offsets(turn))
            return carry

        return lambda amount: lax.fori_loop(0, amount, body, 0)

    def near_even(turn):
        for k in range(2):
            pl.when(turn == k + 1)(second[k].wait_recv)
        near(-2 * turn)

    loop(near_even, lambda turn: turn)(3)
    for copy in second[2:]:
        copy.wait_recv()
    third_copy = send(
        gathered.at[:, side], gathered.at[:, side], send_three, recv_three, 0, (1 - 2 * side, 0)
    )
    start_halos()
    near(2)
    loop(lambda offset: [far(offset + 2 * k) for k in range(4)], lambda turn: 4 + turn)(1)
    third_copy.wait_recv()
    loop(lambda offset: [far(offset + 2 * k) for k in range(3)], lambda turn: 6 * turn + 1)(2)
    loop(near, lambda turn: 2 * turn - 3)(2)

    answers = None
    for part in range(8):
        slot_rows = lax.broadcasted_iota(jnp.int32, (256, 1024), 0) + part * 256
        chosen = jnp.where(slot_rows == slot, 1.0, 0.0).astype(BF)
        gained = jnp.concatenate(
            [
                jnp.where(
                    slot_eight < before[block : block + 1],
                    node_total[128 * block : 128 * (block + 1), :],
                    0.0,
                )
                for block in (2 * part, 2 * part + 1)
            ],
            axis=0,
        )
        high, mid, low = split_three(gained)
        stacked = jnp.concatenate([high, mid, low, jnp.zeros_like(low)], axis=1).astype(BF)
        added = lax.dot_general(stacked, chosen, (((0,), (0,)), ((), ())), preferred_element_type=F32)
        answers = added if answers is None else answers + added
    found = answers[0:8] + answers[8:16] + answers[16:24]
    moved = cross_rows(spots, [found[c : c + 1] for c in range(3)])
    for c in range(3):
        result = (moved[c] - found[3 + c : 4 + c]) * SCALE
        even = jnp.concatenate([result[:, 128 * k : 128 * (k + 1)] for k in range(8)], axis=0)
        odd = pltpu.roll(even, 64, 1)
        own_nodes[c] = jnp.concatenate(
            [(even, odd)[r % 2][r // 2 : r // 2 + 1] for r in range(16)], axis=0
        )
    shared = [
        send(own_nodes, far_nodes.at[k], send_node, recv_node, k, peer)
        for k, peer in enumerate([(0, -1), (-1, 0), (1, 0), (-1, -1), (1, -1)])
    ]

    loop(lambda offset: near(offset, False), lambda turn: 2 * turn + 1)(2)

    spin = [own[c : c + 1] for c in range(3)]
    sums = jnp.transpose(total[...])
    sums = sums[0:40] + sums[40:80] + sums[80:120]
    plain = [sums[k : k + 1] for k in range(6)]
    turned = [[sums[8 + 8 * c + k : 9 + 8 * c + k] for k in range(6)] for c in range(3)]
    heavy = [sums[32 + k : 33 + k] for k in range(6)]
    mixed = [
        weight * plain[k]
        + heavy[k]
        - 2.0 * (place[0] * turned[0][k] + place[1] * turned[1][k] + place[2] * turned[2][k])
        for k in range(6)
    ]
    live = grid * 256 + lax.broadcasted_iota(jnp.int32, (1, 256), 1) < counts[wake]
    factor = jnp.where(live, SCALE, 0.0)
    swept = cross_rows(place, mixed[0:3])
    bent_own = cross_rows(place, plain[0:3])
    along = spin[0] * place[0] + spin[1] * place[1] + spin[2] * place[2]
    pulled = [spin[0] * turned[0][k] + spin[1] * turned[1][k] + spin[2] * turned[2][k] for k in range(6)]
    bent_far = cross_rows(place, pulled[0:3])
    lifted = cross_rows(spin, mixed[0:3])
    for c in range(3):
        velocity_out[c : c + 1, :] = (swept[c] - mixed[3 + c]) * factor
        bent = along * (bent_own[c] - plain[3 + c]) - (bent_far[c] - pulled[3 + c])
        stretch_out[c : c + 1, :] = (lifted[c] - 3.0 * bent) * factor

    for copy in shared:
        copy.wait()
    finish_halos()
    for copy in first + second + [third_copy]:
        copy.wait_send()


ANY = pl.BlockSpec(memory_space=pltpu.HBM)
SCALAR = pl.BlockSpec(memory_space=pltpu.SMEM)


def gather_and_sum(counts, place, spin, core, node_place, node_block, flow, sections):
    dma = pltpu.SemaphoreType.DMA
    return pl.pallas_call(
        gather_kernel,
        out_shape=[
            jax.ShapeDtypeStruct((3, 256), F32),
            jax.ShapeDtypeStruct((3, 256), F32),
            jax.ShapeDtypeStruct((3, 16, 128), F32),
            jax.ShapeDtypeStruct((5, 3, 16, 128), F32),
            jax.ShapeDtypeStruct((5, 8, BUFFER), F32),
            jax.ShapeDtypeStruct((5, 16, 128), F32),
            jax.ShapeDtypeStruct((5, 16, 128), F32),
            jax.ShapeDtypeStruct((8, BUFFER), jnp.int32),
            jax.ShapeDtypeStruct((16, 128), jnp.int32),
            jax.ShapeDtypeStruct((16, 128), jnp.int32),
        ],
        in_specs=[SCALAR] + [ANY] * 7,
        out_specs=[WHOLE] * 4 + [ANY] * 6,
        scratch_shapes=[
            pltpu.VMEM((NW // 2, 2, 8, PB), F32),
            pltpu.VMEM((3, 3, 256), F32),
            pltpu.VMEM((3, 1024), F32),
            pltpu.VMEM((1, 1024), jnp.int32),
            pltpu.VMEM((NW * 128, 48), BF),
            pltpu.VMEM((256, 48), BF),
            pltpu.VMEM((256, 128), F32),
            pltpu.VMEM((NW * 128, 8), F32),
            dma((5,)),
            dma((NG - 1,)),
            dma((NG - 1,)),
            dma((NG - 1,)),
            dma((NG - 1,)),
            dma((1,)),
            dma((1,)),
            dma((16,)),
            dma((16,)),
            dma((5,)),
            dma((5,)),
        ],
        compiler_params=pltpu.CompilerParams(
            collective_id=0, has_side_effects=True, vmem_limit_bytes=LIMIT
        ),
    )(counts, place, spin, core, node_place, node_block, flow, sections)


TILES = 130
BUFFER = 16640 + 256


def sweep_kernel(
    flow, sections, viscosity, rows_halo, left_halo, right_halo, kind_rows, kind_left, kind_right,
    own_nodes, far_nodes, velocity, stretch, out, velocity_out, stretch_out,
    rows_in, kind, first, second, rates, rows_out, nodes, sem_in, sem_out,
):
    fields = 5
    wake = lax.axis_index("wake")
    grid = lax.axis_index("grid")
    own_rows, halo_rows = pl.ds(0, 16), pl.ds(16, 8)
    middle, before, after = pl.ds(256, 16384), pl.ds(128, 128), pl.ds(16640, 128)
    kinds = [
        pltpu.make_async_copy(source, target, sem_in.at[4 * fields + k])
        for k, (source, target) in enumerate(
            [
                (sections, kind.at[own_rows, middle]),
                (kind_rows, kind.at[halo_rows, :]),
                (kind_left, kind.at[own_rows, before]),
                (kind_right, kind.at[own_rows, after]),
            ]
        )
    ]
    def incoming(f):
        return [
            pltpu.make_async_copy(source, target, sem_in.at[4 * f + k])
            for k, (source, target) in enumerate(
                [
                    (flow.at[f], rows_in.at[f, own_rows, middle]),
                    (rows_halo.at[f], rows_in.at[f, halo_rows, :]),
                    (left_halo.at[f], rows_in.at[f, own_rows, before]),
                    (right_halo.at[f], rows_in.at[f, own_rows, after]),
                ]
            )
        ]

    def outgoing(f, half):
        return pltpu.make_async_copy(
            rows_out.at[f, :, pl.ds(256 + 8192 * half, 8192)],
            out.at[f, :, pl.ds(8192 * half, 8192)],
            sem_out.at[2 * f + half],
        )

    for copy in kinds + incoming(0):
        copy.start()
    velocity_out[...] = velocity[...]
    stretch_out[...] = stretch[...]

    lane = lax.broadcasted_iota(jnp.int32, (24, 128), 1)
    row = lax.broadcasted_iota(jnp.int32, (24, 128), 0)
    is_first, is_last = lane == 0, lane == 127
    inside_rows = ((row < 20) | (wake > 0)) & ((row < 16) | (row >= 20) | (wake < NW - 1))
    lane8 = lax.broadcasted_iota(jnp.int32, (8, 128), 1)
    row8 = lax.broadcasted_iota(jnp.int32, (8, 128), 0)

    for c in range(3):
        def with_next(rows, column):
            return jnp.where(lane8 == 64, jnp.broadcast_to(column, (8, 128)), rows)

        halo = jnp.where(row8 < 4, far_nodes[1, c, 0:8], far_nodes[2, c, 8:16])
        halo_next = jnp.where(row8 < 4, far_nodes[3, c, 0:8], far_nodes[4, c, 8:16])
        parts = [
            with_next(own_nodes[c, 0:8], far_nodes[0, c, 0:8, 0:1]),
            with_next(own_nodes[c, 8:16], far_nodes[0, c, 8:16, 0:1]),
            with_next(halo, halo_next[:, 0:1]),
        ]
        nodes[c] = jnp.where(inside_rows, jnp.concatenate(parts, axis=0), 0.0)

    for copy in kinds:
        copy.wait()

    tile_lanes = lambda t: pl.ds(t * 128, 128)

    def field(f, done):
        for copy in incoming(f):
            copy.wait()

        @pl.when(f + 1 < fields)
        def _():
            for copy in incoming(f + 1):
                copy.start()

        rows_in[f, 16:24, 256:16640] = jnp.where(
            inside_rows[16:24, 0:1], rows_in[f, 16:24, 256:16640], 0.0
        )
        for start, edge in ((128, grid == 0), (16640, grid == NG - 1)):
            keep = inside_rows & jnp.logical_not(edge)
            rows_in[f, :, start : start + 128] = jnp.where(keep, rows_in[f, :, start : start + 128], 0.0)
        @pl.when((f >= 1) & (f <= 3))
        def _():
            given = nodes[jnp.clip(f - 1, 0, 2)]
            for k in range(65):
                start = 256 + 256 * k
                column = jnp.broadcast_to(given[:, k : k + 1], (24, 128))
                if k == 64:
                    column = jnp.where(grid == NG - 1, 0.0, column)
                rows_in[f, :, start : start + 128] = jnp.where(
                    is_first, column, rows_in[f, :, start : start + 128]
                )

        def sweep(load, finish):
            here = load(1)
            last_right, right, left = pltpu.roll(load(0), 1, 1), pltpu.roll(here, 1, 1), pltpu.roll(here, 127, 1)
            for t in range(1, TILES + 1):
                following = load(t + 1)
                next_right = pltpu.roll(following, 1, 1)
                next_left = pltpu.roll(following, 127, 1)
                across = jnp.where(is_first, last_right, right) + jnp.where(is_last, next_left, left)
                along = pltpu.roll(here, 1, 0) + pltpu.roll(here, 23, 0)
                finish(t, here, across + along)
                last_right, here, right, left = right, following, next_right, next_left

        def finish_first(t, here, beside):
            name = kind[:, tile_lanes(t)]
            rate = jnp.where(
                name == 0, viscosity[0, f], jnp.where(name == 1, viscosity[1, f], viscosity[2, f])
            )
            keep = inside_rows
            if t == 1:
                keep = keep & (grid > 0)
            if t == TILES:
                keep = keep & (grid < NG - 1)
            rate = jnp.where(keep, rate, 0.0)
            rates[:, tile_lanes(t)] = rate
            first[:, tile_lanes(t)] = here + rate * (beside - 4.0 * here)

        def finish_second(t, here, beside):
            second[:, tile_lanes(t)] = here + rates[:, tile_lanes(t)] * (beside - 4.0 * here)

        def finish_third(t, here, beside):
            rows_out[f, :, tile_lanes(t)] = (here + rates[:, tile_lanes(t)] * (beside - 4.0 * here))[0:16]
            if t == 65:
                outgoing(f, 0).start()

        sweep(lambda t: rows_in[f, :, tile_lanes(t)], finish_first)
        sweep(lambda t: first[:, tile_lanes(t)], finish_second)
        sweep(lambda t: second[:, tile_lanes(t)], finish_third)
        outgoing(f, 1).start()
        return done

    lax.fori_loop(0, fields, field, 0)
    for f in range(fields):
        outgoing(f, 0).wait()
        outgoing(f, 1).wait()


def sweep_fields(*arrays):
    dma = pltpu.SemaphoreType.DMA
    return pl.pallas_call(
        sweep_kernel,
        out_shape=[
            jax.ShapeDtypeStruct((5, 16, 16384), F32),
            jax.ShapeDtypeStruct((3, 256), F32),
            jax.ShapeDtypeStruct((3, 256), F32),
        ],
        in_specs=[ANY, ANY, SCALAR] + [ANY] * 6 + [WHOLE] * 4,
        out_specs=[ANY, WHOLE, WHOLE],
        scratch_shapes=[
            pltpu.VMEM((5, 24, BUFFER), F32),
            pltpu.VMEM((24, BUFFER), jnp.int32),
            pltpu.VMEM((24, BUFFER), F32),
            pltpu.VMEM((24, BUFFER), F32),
            pltpu.VMEM((24, BUFFER), F32),
            pltpu.VMEM((5, 16, BUFFER), F32),
            pltpu.VMEM((3, 24, 128), F32),
            dma((24,)),
            dma((10,)),
        ],
        compiler_params=pltpu.CompilerParams(vmem_limit_bytes=LIMIT),
    )(*arrays)


def on_device(
    flow,
    section_map,
    viscosity,
    particle_position,
    particle_strength,
    particle_core,
    shed_counts,
    node_position,
    node_block,
):
    (
        velocity, stretch, own_nodes, far_nodes, rows_halo, left_halo, right_halo, kind_rows, kind_left, kind_right,
    ) = gather_and_sum(
        shed_counts,
        particle_position,
        particle_strength,
        particle_core.reshape(1, 256),
        node_position,
        node_block.reshape(1, 1024),
        flow,
        section_map,
    )
    field, velocity, stretch = sweep_fields(
        flow, section_map, viscosity, rows_halo, left_halo, right_halo, kind_rows, kind_left, kind_right,
        own_nodes, far_nodes, velocity, stretch,
    )
    return (field, velocity, stretch)


def solution(mesh):
    return jax.shard_map(
        on_device,
        mesh=mesh,
        in_specs=(
            P(None, "wake", "grid"),
            P("wake", "grid"),
            P(),
            P(None, ("wake", "grid")),
            P(None, ("wake", "grid")),
            P(("wake", "grid")),
            P(),
            P(None, ("wake", "grid")),
            P(("wake", "grid"), None),
        ),
        out_specs=(P(None, "wake", "grid"), P(None, ("wake", "grid")), P(None, ("wake", "grid"))),
        check_vma=False,
    )
```

```python
import math

import jax
import jax.numpy as jnp
from jax import lax
from jax.experimental import pallas as pl
from jax.experimental.pallas import tpu as pltpu
from jax.sharding import PartitionSpec as P

PB = 2048
NW = 16
NG = 8
CHUNK = 512
LIMIT = 64 << 20
BF = jnp.bfloat16
F32 = jnp.float32
MESH = pl.DeviceIdType.MESH
SCALE = -1.0 / (4.0 * math.pi)
WHOLE = pl.BlockSpec(memory_space=pltpu.VMEM)


def split_three(value):
    high = value.astype(BF).astype(F32)
    rest = value - high
    middle = rest.astype(BF).astype(F32)
    return high, middle, rest - middle


def dot_nt(first, second):
    return lax.dot_general(first, second, (((1,), (1,)), ((), ())), preferred_element_type=F32)


def cross_rows(first, second):
    return [
        first[1] * second[2] - first[2] * second[1],
        first[2] * second[0] - first[0] * second[2],
        first[0] * second[1] - first[1] * second[0],
    ]


def target_rows(place, weight, halved):
    ones = jnp.ones_like(weight)
    none = jnp.zeros_like(weight)
    parts = split_three(jnp.concatenate([weight, none, none] + [-2.0 * row for row in place] + [none, none], axis=0))
    unit = jnp.concatenate([none] * 6 + [none if halved else ones, ones if halved else none], axis=0)
    high, middle, low = parts
    return jnp.concatenate([high + unit, middle, low, high + unit, middle, high + unit], axis=0).astype(BF)


def source_columns(moment, factors):
    parts = [split_three(moment)] + [split_three(moment * factor) for factor in factors]
    columns = [part[level] for level in range(3) for part in parts]
    return columns


def centred(rows, centre):
    return [rows[c : c + 1] - centre[c][:, 0 : rows.shape[1]] for c in range(3)]


def square_sum(place):
    return place[0] * place[0] + place[1] * place[1] + place[2] * place[2]


def gather_kernel(
    counts, place_in, spin_in, core_in, node_place_in, node_block_in, flow, sections,
    velocity_to, stretch_to, own_nodes_to, far_nodes, rows_halo, left_halo, right_halo,
    kind_rows, kind_left, kind_right,
    velocity_out, stretch_out, own_nodes, gathered, share, node_place, node_block, points, targets_ref, total, node_total,
    sem_in, send_one, recv_one, send_two, recv_two, send_three, recv_three,
    send_halo, recv_halo, send_node, recv_node, sem_out,
):
    wake = lax.axis_index("wake")
    grid = lax.axis_index("grid")
    side = lax.rem(wake, 2)
    pair = wake // 2
    lanes = pl.ds(pl.multiple_of(grid * 256, 256), 256)
    mine = gathered.at[pair, side, :, lanes]

    def device(wake_by, grid_by):
        return {"wake": lax.rem(wake + wake_by + NW, NW), "grid": lax.rem(grid + grid_by + NG, NG)}

    loads = [
        pltpu.make_async_copy(source, target, sem_in.at[k])
        for k, (source, target) in enumerate(
            [
                (place_in, share.at[0]),
                (spin_in, share.at[1]),
                (core_in, share.at[2, pl.ds(0, 1)]),
                (node_place_in, node_place),
                (node_block_in, node_block),
            ]
        )
    ]
    for load in loads:
        load.start()

    peers = [(0, turn) for turn in range(1, NG)] + [(2 * turn, 0) for turn in range(1, NG)]
    peers += [(1, 0), (-1, 0), (1, 1), (1, -1), (-1, 1), (-1, -1)]
    barrier = pltpu.get_barrier_semaphore()
    for peer in peers:
        pl.semaphore_signal(barrier, inc=1, device_id=device(*peer), device_id_type=MESH)
    for load in loads:
        load.wait()
    own_live = grid * 256 + lax.broadcasted_iota(jnp.int32, (1, 256), 1) < counts[wake]
    squared_core = share[2, 0:1] * share[2, 0:1]
    mine[...] = jnp.concatenate(
        [jnp.where(own_live, share[1], 0.0), share[0], squared_core, 0.5 * squared_core], axis=0
    )
    pl.semaphore_wait(barrier, len(peers))

    def describe(source, target, sends, recvs, slot, peer):
        return pltpu.make_async_remote_copy(
            src_ref=source,
            dst_ref=target,
            send_sem=sends.at[slot],
            recv_sem=recvs.at[slot],
            device_id=device(*peer),
            device_id_type=MESH,
        )

    def send(*arguments):
        copy = describe(*arguments)
        copy.start()
        return copy

    own = mine[...]
    centre = [
        jnp.broadcast_to(jnp.sum(own[3 + c : 4 + c], axis=1, keepdims=True) * (1.0 / 256.0), (1, 1024))
        for c in range(3)
    ]
    first = [send(mine, mine, send_one, recv_one, turn - 1, (0, turn)) for turn in range(1, NG)]

    names = node_block[...]
    spots = centred(node_place, centre)
    rows = target_rows(spots, square_sum(spots), False)
    members = jnp.where(lax.broadcasted_iota(jnp.int32, (NW, 1024), 0) == names, 1.0, 0.0)
    triangle = jnp.where(
        lax.broadcasted_iota(jnp.int32, (128, 128), 0) <= lax.broadcasted_iota(jnp.int32, (128, 128), 1),
        1.0,
        0.0,
    ).astype(BF)
    pieces = jnp.concatenate([members[:, 128 * k : 128 * (k + 1)] for k in range(8)], axis=0)
    running = jnp.dot(pieces.astype(BF), triangle, preferred_element_type=F32)
    before = jnp.zeros((NW, 1), F32)
    ranks = []
    for k in range(8):
        part = running[NW * k : NW * (k + 1)]
        ranks.append(part + before)
        before = before + part[:, 127:128]
    rank = jnp.sum(members * jnp.concatenate(ranks, axis=1), axis=0, keepdims=True) - 1.0
    slot = names * 128 + rank.astype(jnp.int32)
    slot_eight = lax.broadcasted_iota(jnp.int32, (128, 8), 0).astype(F32)

    place = centred(own[3:6], centre)
    weight = square_sum(place) + own[7:8]
    identity = jnp.where(
        lax.broadcasted_iota(jnp.int32, (256, 256), 0) == lax.broadcasted_iota(jnp.int32, (256, 256), 1),
        1.0,
        0.0,
    ).astype(BF)
    targets_ref[...] = dot_nt(identity, target_rows(place, weight, True)).astype(BF)
    total[...] = jnp.zeros_like(total)

    for copy in first:
        copy.wait_recv()
    block_here = gathered.at[pair, side]
    second = [
        send(block_here, block_here, send_two, recv_two, turn - 1, (2 * turn, 0)) for turn in (1, 2, 7, 3, 4, 5, 6)
    ]

    top, bottom = pl.ds(0, 3), pl.ds(13, 3)
    low_rows, high_rows = pl.ds(0, 3), pl.ds(5, 3)
    begin, finish = pl.ds(0, 128), pl.ds(16256, 128)
    middle, before_lanes, after_lanes = pl.ds(256, 16384), pl.ds(128, 128), pl.ds(16640, 128)
    everything, every = pl.ds(0, 16384), pl.ds(0, 16)
    plan = [
        ((-1, 0), top, everything, 0, low_rows, middle),
        ((1, 0), bottom, everything, 0, high_rows, middle),
        ((0, -1), every, begin, 2, every, begin),
        ((0, 1), every, finish, 1, every, begin),
        ((-1, -1), top, begin, 0, low_rows, after_lanes),
        ((-1, 1), top, finish, 0, low_rows, before_lanes),
        ((1, -1), bottom, begin, 0, high_rows, after_lanes),
        ((1, 1), bottom, finish, 0, high_rows, before_lanes),
    ]
    halos = []
    for k, (peer, from_rows, from_lanes, which, to_rows, to_lanes) in enumerate(plan):
        for part, (source, targets) in enumerate(
            [
                (flow.at[:, from_rows, from_lanes], (rows_halo, left_halo, right_halo)),
                (sections.at[from_rows, from_lanes], (kind_rows, kind_left, kind_right)),
            ]
        ):
            target = targets[which].at[:, to_rows, to_lanes] if part == 0 else targets[which].at[to_rows, to_lanes]
            halos.append((peer, describe(source, target, send_halo, recv_halo, 2 * k + part, peer)))

    def within(wake_by, grid_by):
        to_wake, to_grid = wake + wake_by, grid + grid_by
        return (to_wake >= 0) & (to_wake < NW) & (to_grid >= 0) & (to_grid < NG)

    def start_halos():
        for peer, copy in halos:
            pl.when(within(*peer))(copy.start)

    def finish_halos():
        for peer, copy in halos:
            pl.when(within(*peer))(copy.wait_send)
            pl.when(within(-peer[0], -peer[1]))(copy.wait_recv)

    for part in range(8):
        chosen = jnp.where(
            lax.broadcasted_iota(jnp.int32, (256, 1024), 0) + part * 256 == slot, 1.0, 0.0
        ).astype(BF)
        points[256 * part : 256 * (part + 1), :] = dot_nt(chosen, rows).astype(BF)

    line = lax.broadcasted_iota(jnp.int32, (8, CHUNK), 0)
    is_place = (line >= 3) & (line < 6)
    shift = jnp.zeros((8, CHUNK), F32)
    for c in range(3):
        shift = jnp.where(line == 3 + c, jnp.broadcast_to(centre[c][:, 0:CHUNK], (8, CHUNK)), shift)

    def load_source(block, start):
        tile = gathered[block // 2, lax.rem(block, 2), :, pl.ds(start, CHUNK)] - shift
        summed = jnp.where(is_place, tile * tile, 0.0)
        for step in (4, 2, 1):
            summed = summed + pltpu.roll(summed, step, 0)
        full = tile + jnp.where(line >= 6, summed, 0.0)
        high, middle, low = split_three(jnp.where(line == 0, 1.0, full))
        distance = jnp.concatenate([high, high, high, middle, middle, low], axis=0).astype(BF)
        down_one, down_two = pltpu.roll(tile, 1, 0), pltpu.roll(tile, 2, 0)
        place_next = jnp.where(line == 5, down_two, pltpu.roll(tile, 7, 0))
        place_last = jnp.where(line == 3, pltpu.roll(tile, 6, 0), down_one)
        spin_next = jnp.where(line == 5, pltpu.roll(tile, 5, 0), down_two)
        spin_last = jnp.where(line == 3, down_one, pltpu.roll(tile, 4, 0))
        crossed = place_next * spin_last - place_last * spin_next
        moment = jnp.where(line < 3, tile, jnp.where(line < 6, crossed, 0.0))
        return distance, moment, [full[k : k + 1] for k in (3, 4, 5, 7)]

    def node_slots(block):
        return pl.ds(pl.multiple_of(block * 128, 128), 128)

    def split_two(value):
        high = value.astype(BF)
        return high, (value - high.astype(F32)).astype(BF)

    def near(offset, with_nodes=True):
        block = lax.rem(wake + offset + NW, NW)
        looking = targets_ref[...]
        if with_nodes:
            looking = jnp.concatenate([looking, points[node_slots(block), :]], axis=0)

        def run(step, gained):
            distance, moment, factors = load_source(block, pl.multiple_of(step * CHUNK, CHUNK))
            columns = source_columns(moment, factors)
            columns = jnp.concatenate(columns + [jnp.zeros_like(moment)], axis=0).astype(BF)
            for cut in range(0, CHUNK, CHUNK):
                root = lax.rsqrt(
                    jnp.dot(looking, distance[:, cut : cut + CHUNK], preferred_element_type=F32)
                )
                second_power = root * root
                third = second_power * root
                fifth = third[0:256] * second_power[0:256]
                weights = split_two(fifth)
                if with_nodes:
                    weights += split_two(third[256:384])
                added = dot_nt(jnp.concatenate(weights, axis=0), columns[:, cut : cut + CHUNK])
                gained = added if gained is None else gained + added
            return gained

        gained = None
        for step in range(PB // CHUNK):
            gained = run(step, gained)
        total[...] += gained[0:256] + gained[256:512]
        if not with_nodes:
            return
        sums = gained[512:640] + gained[640:768]
        node_total[node_slots(block), :] = sums[:, 0:8] + sums[:, 40:48] + sums[:, 80:88]

    def far(offset):
        block = lax.rem(wake + offset + NW, NW)
        looking = points[node_slots(block), :]
        gained = None
        for step in range(PB // CHUNK):
            distance, moment, _ = load_source(block, pl.multiple_of(step * CHUNK, CHUNK))
            columns = source_columns(moment, [])
            columns = jnp.concatenate(columns + [jnp.zeros_like(moment)], axis=0).astype(BF)
            root = lax.rsqrt(jnp.dot(looking, distance, preferred_element_type=F32))
            high, low = split_two(root * root * root)
            added = dot_nt(jnp.concatenate([high, low], axis=0), columns)
            gained = added if gained is None else gained + added
        sums = gained[0:128] + gained[128:256]
        node_total[node_slots(block), :] = sums[:, 0:8] + sums[:, 8:16] + sums[:, 16:24]

    def loop(function, offsets):
        def body(turn, carry):
            function(offsets(turn))
            return carry

        return lambda amount: lax.fori_loop(0, amount, body, 0)

    def near_even(turn):
        for k in range(2):
            pl.when(turn == k + 1)(second[k].wait_recv)
        near(-2 * turn)

    loop(near_even, lambda turn: turn)(3)
    for copy in second[2:]:
        copy.wait_recv()
    third_copy = send(
        gathered.at[:, side], gathered.at[:, side], send_three, recv_three, 0, (1 - 2 * side, 0)
    )
    start_halos()
    near(2)
    loop(lambda offset: [far(offset + 2 * k) for k in range(4)], lambda turn: 4 + turn)(1)
    third_copy.wait_recv()
    loop(lambda offset: [far(offset + 2 * k) for k in range(3)], lambda turn: 6 * turn + 1)(2)
    loop(near, lambda turn: 2 * turn - 3)(2)

    answers = None
    for part in range(8):
        slot_rows = lax.broadcasted_iota(jnp.int32, (256, 1024), 0) + part * 256
        chosen = jnp.where(slot_rows == slot, 1.0, 0.0).astype(BF)
        gained = jnp.concatenate(
            [
                jnp.where(
                    slot_eight < before[block : block + 1],
                    node_total[128 * block : 128 * (block + 1), :],
                    0.0,
                )
                for block in (2 * part, 2 * part + 1)
            ],
            axis=0,
        )
        high, mid, low = split_three(gained)
        stacked = jnp.concatenate([high, mid, low, jnp.zeros_like(low)], axis=1).astype(BF)
        added = lax.dot_general(stacked, chosen, (((0,), (0,)), ((), ())), preferred_element_type=F32)
        answers = added if answers is None else answers + added
    found = answers[0:8] + answers[8:16] + answers[16:24]
    moved = cross_rows(spots, [found[c : c + 1] for c in range(3)])
    for c in range(3):
        result = (moved[c] - found[3 + c : 4 + c]) * SCALE
        even = jnp.concatenate([result[:, 128 * k : 128 * (k + 1)] for k in range(8)], axis=0)
        odd = pltpu.roll(even, 64, 1)
        own_nodes[c] = jnp.concatenate(
            [(even, odd)[r % 2][r // 2 : r // 2 + 1] for r in range(16)], axis=0
        )
    shared = [
        send(own_nodes, far_nodes.at[k], send_node, recv_node, k, peer)
        for k, peer in enumerate([(0, -1), (-1, 0), (1, 0), (-1, -1), (1, -1)])
    ]

    results = [
        pltpu.make_async_copy(source, target, sem_out.at[k])
        for k, (source, target) in enumerate(
            [(own_nodes, own_nodes_to), (velocity_out, velocity_to), (stretch_out, stretch_to)]
        )
    ]
    results[0].start()
    loop(lambda offset: near(offset, False), lambda turn: 2 * turn + 1)(2)

    spin = [own[c : c + 1] for c in range(3)]
    sums = jnp.transpose(total[...])
    sums = sums[0:40] + sums[40:80] + sums[80:120]
    plain = [sums[k : k + 1] for k in range(6)]
    turned = [[sums[8 + 8 * c + k : 9 + 8 * c + k] for k in range(6)] for c in range(3)]
    heavy = [sums[32 + k : 33 + k] for k in range(6)]
    mixed = [
        weight * plain[k]
        + heavy[k]
        - 2.0 * (place[0] * turned[0][k] + place[1] * turned[1][k] + place[2] * turned[2][k])
        for k in range(6)
    ]
    live = grid * 256 + lax.broadcasted_iota(jnp.int32, (1, 256), 1) < counts[wake]
    factor = jnp.where(live, SCALE, 0.0)
    swept = cross_rows(place, mixed[0:3])
    bent_own = cross_rows(place, plain[0:3])
    along = spin[0] * place[0] + spin[1] * place[1] + spin[2] * place[2]
    pulled = [spin[0] * turned[0][k] + spin[1] * turned[1][k] + spin[2] * turned[2][k] for k in range(6)]
    bent_far = cross_rows(place, pulled[0:3])
    lifted = cross_rows(spin, mixed[0:3])
    for c in range(3):
        velocity_out[c : c + 1, :] = (swept[c] - mixed[3 + c]) * factor
        bent = along * (bent_own[c] - plain[3 + c]) - (bent_far[c] - pulled[3 + c])
        stretch_out[c : c + 1, :] = (lifted[c] - 3.0 * bent) * factor

    results[1].start()
    results[2].start()
    for copy in shared:
        copy.wait()
    finish_halos()
    for copy in results:
        copy.wait()
    for copy in first + second + [third_copy]:
        copy.wait_send()


ANY = pl.BlockSpec(memory_space=pltpu.HBM)
SCALAR = pl.BlockSpec(memory_space=pltpu.SMEM)


def gather_and_sum(counts, place, spin, core, node_place, node_block, flow, sections):
    dma = pltpu.SemaphoreType.DMA
    return pl.pallas_call(
        gather_kernel,
        out_shape=[
            jax.ShapeDtypeStruct((3, 256), F32),
            jax.ShapeDtypeStruct((3, 256), F32),
            jax.ShapeDtypeStruct((3, 16, 128), F32),
            jax.ShapeDtypeStruct((5, 3, 16, 128), F32),
            jax.ShapeDtypeStruct((5, 8, BUFFER), F32),
            jax.ShapeDtypeStruct((5, 16, 128), F32),
            jax.ShapeDtypeStruct((5, 16, 128), F32),
            jax.ShapeDtypeStruct((8, BUFFER), jnp.int32),
            jax.ShapeDtypeStruct((16, 128), jnp.int32),
            jax.ShapeDtypeStruct((16, 128), jnp.int32),
        ],
        in_specs=[SCALAR] + [ANY] * 7,
        out_specs=[ANY] * 10,
        scratch_shapes=[
            pltpu.VMEM((3, 256), F32),
            pltpu.VMEM((3, 256), F32),
            pltpu.VMEM((3, 16, 128), F32),
            pltpu.VMEM((NW // 2, 2, 8, PB), F32),
            pltpu.VMEM((3, 3, 256), F32),
            pltpu.VMEM((3, 1024), F32),
            pltpu.VMEM((1, 1024), jnp.int32),
            pltpu.VMEM((NW * 128, 48), BF),
            pltpu.VMEM((256, 48), BF),
            pltpu.VMEM((256, 128), F32),
            pltpu.VMEM((NW * 128, 8), F32),
            dma((5,)),
            dma((NG - 1,)),
            dma((NG - 1,)),
            dma((NG - 1,)),
            dma((NG - 1,)),
            dma((1,)),
            dma((1,)),
            dma((16,)),
            dma((16,)),
            dma((5,)),
            dma((5,)),
            dma((3,)),
        ],
        compiler_params=pltpu.CompilerParams(
            collective_id=0, has_side_effects=True, vmem_limit_bytes=LIMIT
        ),
    )(counts, place, spin, core, node_place, node_block, flow, sections)


TILES = 130
BUFFER = 16640 + 256


def sweep_kernel(
    flow, sections, viscosity, rows_halo, left_halo, right_halo, kind_rows, kind_left, kind_right,
    own_nodes_in, far_nodes_in, velocity, stretch, out, velocity_out, stretch_out,
    own_nodes, far_nodes, rows_in, kind, first, second, rates, rows_out, nodes, sem_in, sem_out, sem_small,
):
    fields = 5
    wake = lax.axis_index("wake")
    grid = lax.axis_index("grid")
    own_rows, halo_rows = pl.ds(0, 16), pl.ds(16, 8)
    middle, before, after = pl.ds(256, 16384), pl.ds(128, 128), pl.ds(16640, 128)
    kinds = [
        pltpu.make_async_copy(source, target, sem_in.at[4 * fields + k])
        for k, (source, target) in enumerate(
            [
                (sections, kind.at[own_rows, middle]),
                (kind_rows, kind.at[halo_rows, :]),
                (kind_left, kind.at[own_rows, before]),
                (kind_right, kind.at[own_rows, after]),
            ]
        )
    ]
    def incoming(f):
        return [
            pltpu.make_async_copy(source, target, sem_in.at[4 * f + k])
            for k, (source, target) in enumerate(
                [
                    (flow.at[f], rows_in.at[f, own_rows, middle]),
                    (rows_halo.at[f], rows_in.at[f, halo_rows, :]),
                    (left_halo.at[f], rows_in.at[f, own_rows, before]),
                    (right_halo.at[f], rows_in.at[f, own_rows, after]),
                ]
            )
        ]

    def outgoing(f, half):
        return pltpu.make_async_copy(
            rows_out.at[f, :, pl.ds(256 + 8192 * half, 8192)],
            out.at[f, :, pl.ds(8192 * half, 8192)],
            sem_out.at[2 * f + half],
        )

    for copy in kinds + incoming(0):
        copy.start()
    small = [
        pltpu.make_async_copy(source, target, sem_small.at[k])
        for k, (source, target) in enumerate(
            [
                (own_nodes_in, own_nodes),
                (far_nodes_in, far_nodes),
                (velocity, velocity_out),
                (stretch, stretch_out),
            ]
        )
    ]
    for copy in small:
        copy.start()
    for copy in small[0:2]:
        copy.wait()

    lane = lax.broadcasted_iota(jnp.int32, (24, 128), 1)
    row = lax.broadcasted_iota(jnp.int32, (24, 128), 0)
    is_first, is_last = lane == 0, lane == 127
    inside_rows = ((row < 20) | (wake > 0)) & ((row < 16) | (row >= 20) | (wake < NW - 1))
    lane8 = lax.broadcasted_iota(jnp.int32, (8, 128), 1)
    row8 = lax.broadcasted_iota(jnp.int32, (8, 128), 0)

    for c in range(3):
        def with_next(rows, column):
            return jnp.where(lane8 == 64, jnp.broadcast_to(column, (8, 128)), rows)

        halo = jnp.where(row8 < 4, far_nodes[1, c, 0:8], far_nodes[2, c, 8:16])
        halo_next = jnp.where(row8 < 4, far_nodes[3, c, 0:8], far_nodes[4, c, 8:16])
        parts = [
            with_next(own_nodes[c, 0:8], far_nodes[0, c, 0:8, 0:1]),
            with_next(own_nodes[c, 8:16], far_nodes[0, c, 8:16, 0:1]),
            with_next(halo, halo_next[:, 0:1]),
        ]
        nodes[c] = jnp.where(inside_rows, jnp.concatenate(parts, axis=0), 0.0)

    for copy in kinds:
        copy.wait()

    tile_lanes = lambda t: pl.ds(t * 128, 128)

    def field(f, done):
        for copy in incoming(f):
            copy.wait()

        @pl.when(f + 1 < fields)
        def _():
            for copy in incoming(f + 1):
                copy.start()

        rows_in[f, 16:24, 256:16640] = jnp.where(
            inside_rows[16:24, 0:1], rows_in[f, 16:24, 256:16640], 0.0
        )
        for start, edge in ((128, grid == 0), (16640, grid == NG - 1)):
            keep = inside_rows & jnp.logical_not(edge)
            rows_in[f, :, start : start + 128] = jnp.where(keep, rows_in[f, :, start : start + 128], 0.0)
        @pl.when((f >= 1) & (f <= 3))
        def _():
            given = nodes[jnp.clip(f - 1, 0, 2)]
            for k in range(65):
                start = 256 + 256 * k
                column = jnp.broadcast_to(given[:, k : k + 1], (24, 128))
                if k == 64:
                    column = jnp.where(grid == NG - 1, 0.0, column)
                rows_in[f, :, start : start + 128] = jnp.where(
                    is_first, column, rows_in[f, :, start : start + 128]
                )

        def sweep(load, finish):
            here = load(1)
            last_right, right, left = pltpu.roll(load(0), 1, 1), pltpu.roll(here, 1, 1), pltpu.roll(here, 127, 1)
            for t in range(1, TILES + 1):
                following = load(t + 1)
                next_right = pltpu.roll(following, 1, 1)
                next_left = pltpu.roll(following, 127, 1)
                across = jnp.where(is_first, last_right, right) + jnp.where(is_last, next_left, left)
                along = pltpu.roll(here, 1, 0) + pltpu.roll(here, 23, 0)
                finish(t, here, across + along)
                last_right, here, right, left = right, following, next_right, next_left

        def finish_first(t, here, beside):
            name = kind[:, tile_lanes(t)]
            rate = jnp.where(
                name == 0, viscosity[0, f], jnp.where(name == 1, viscosity[1, f], viscosity[2, f])
            )
            keep = inside_rows
            if t == 1:
                keep = keep & (grid > 0)
            if t == TILES:
                keep = keep & (grid < NG - 1)
            rate = jnp.where(keep, rate, 0.0)
            rates[:, tile_lanes(t)] = rate
            first[:, tile_lanes(t)] = here + rate * (beside - 4.0 * here)

        def finish_second(t, here, beside):
            second[:, tile_lanes(t)] = here + rates[:, tile_lanes(t)] * (beside - 4.0 * here)

        def finish_third(t, here, beside):
            rows_out[f, :, tile_lanes(t)] = (here + rates[:, tile_lanes(t)] * (beside - 4.0 * here))[0:16]
            if t == 65:
                outgoing(f, 0).start()

        sweep(lambda t: rows_in[f, :, tile_lanes(t)], finish_first)
        sweep(lambda t: first[:, tile_lanes(t)], finish_second)
        sweep(lambda t: second[:, tile_lanes(t)], finish_third)
        outgoing(f, 1).start()
        return done

    lax.fori_loop(0, fields, field, 0)
    for f in range(fields):
        outgoing(f, 0).wait()
        outgoing(f, 1).wait()
    for copy in small[2:4]:
        copy.wait()


def sweep_fields(*arrays):
    dma = pltpu.SemaphoreType.DMA
    return pl.pallas_call(
        sweep_kernel,
        out_shape=[
            jax.ShapeDtypeStruct((5, 16, 16384), F32),
            jax.ShapeDtypeStruct((3, 256), F32),
            jax.ShapeDtypeStruct((3, 256), F32),
        ],
        in_specs=[ANY, ANY, SCALAR] + [ANY] * 10,
        out_specs=[ANY] * 3,
        scratch_shapes=[
            pltpu.VMEM((3, 16, 128), F32),
            pltpu.VMEM((5, 3, 16, 128), F32),
            pltpu.VMEM((5, 24, BUFFER), F32),
            pltpu.VMEM((24, BUFFER), jnp.int32),
            pltpu.VMEM((24, BUFFER), F32),
            pltpu.VMEM((24, BUFFER), F32),
            pltpu.VMEM((24, BUFFER), F32),
            pltpu.VMEM((5, 16, BUFFER), F32),
            pltpu.VMEM((3, 24, 128), F32),
            dma((24,)),
            dma((10,)),
            dma((4,)),
        ],
        compiler_params=pltpu.CompilerParams(vmem_limit_bytes=LIMIT),
    )(*arrays)


def on_device(
    flow,
    section_map,
    viscosity,
    particle_position,
    particle_strength,
    particle_core,
    shed_counts,
    node_position,
    node_block,
):
    (
        velocity, stretch, own_nodes, far_nodes, rows_halo, left_halo, right_halo, kind_rows, kind_left, kind_right,
    ) = gather_and_sum(
        shed_counts,
        particle_position,
        particle_strength,
        particle_core.reshape(1, 256),
        node_position,
        node_block.reshape(1, 1024),
        flow,
        section_map,
    )
    field, velocity, stretch = sweep_fields(
        flow, section_map, viscosity, rows_halo, left_halo, right_halo, kind_rows, kind_left, kind_right,
        own_nodes, far_nodes, velocity, stretch,
    )
    return (field, velocity, stretch)


def solution(mesh):
    return jax.shard_map(
        on_device,
        mesh=mesh,
        in_specs=(
            P(None, "wake", "grid"),
            P("wake", "grid"),
            P(),
            P(None, ("wake", "grid")),
            P(None, ("wake", "grid")),
            P(("wake", "grid")),
            P(),
            P(None, ("wake", "grid")),
            P(("wake", "grid"), None),
        ),
        out_specs=(P(None, "wake", "grid"), P(None, ("wake", "grid")), P(None, ("wake", "grid"))),
        check_vma=False,
    )
```

```python
import math

import jax
import jax.numpy as jnp
from jax import lax
from jax.experimental import pallas as pl
from jax.experimental.pallas import tpu as pltpu
from jax.sharding import PartitionSpec as P

PB = 2048
NW = 16
NG = 8
CHUNK = 512
LIMIT = 64 << 20
BF = jnp.bfloat16
F32 = jnp.float32
MESH = pl.DeviceIdType.MESH
SCALE = -1.0 / (4.0 * math.pi)
WHOLE = pl.BlockSpec(memory_space=pltpu.VMEM)


def split_three(value):
    high = value.astype(BF).astype(F32)
    rest = value - high
    middle = rest.astype(BF).astype(F32)
    return high, middle, rest - middle


def dot_nt(first, second):
    return lax.dot_general(first, second, (((1,), (1,)), ((), ())), preferred_element_type=F32)


def cross_rows(first, second):
    return [
        first[1] * second[2] - first[2] * second[1],
        first[2] * second[0] - first[0] * second[2],
        first[0] * second[1] - first[1] * second[0],
    ]


def target_rows(place, weight, halved):
    ones = jnp.ones_like(weight)
    none = jnp.zeros_like(weight)
    parts = split_three(jnp.concatenate([weight, none, none] + [-2.0 * row for row in place] + [none, none], axis=0))
    unit = jnp.concatenate([none] * 6 + [none if halved else ones, ones if halved else none], axis=0)
    high, middle, low = parts
    return jnp.concatenate([high + unit, middle, low, high + unit, middle, high + unit], axis=0).astype(BF)


def source_columns(moment, factors):
    parts = [split_three(moment)] + [split_three(moment * factor) for factor in factors]
    columns = [part[level] for level in range(3) for part in parts]
    return columns


def centred(rows, centre):
    return [rows[c : c + 1] - centre[c][:, 0 : rows.shape[1]] for c in range(3)]


def square_sum(place):
    return place[0] * place[0] + place[1] * place[1] + place[2] * place[2]


def gather_kernel(
    counts, place_in, spin_in, core_in, node_place_in, node_block_in, flow, sections,
    velocity_to, stretch_to, own_nodes_to, far_nodes, rows_halo, left_halo, right_halo,
    kind_rows, kind_left, kind_right,
    velocity_out, stretch_out, own_nodes, gathered, share, node_place, node_block, points, targets_ref, total, node_total,
    sem_in, send_one, recv_one, send_two, recv_two, send_three, recv_three,
    send_halo, recv_halo, send_node, recv_node, sem_out,
):
    wake = lax.axis_index("wake")
    grid = lax.axis_index("grid")
    side = lax.rem(wake, 2)
    pair = wake // 2
    lanes = pl.ds(pl.multiple_of(grid * 256, 256), 256)
    mine = gathered.at[pair, side, :, lanes]

    def device(wake_by, grid_by):
        return {"wake": lax.rem(wake + wake_by + NW, NW), "grid": lax.rem(grid + grid_by + NG, NG)}

    loads = [
        pltpu.make_async_copy(source, target, sem_in.at[k])
        for k, (source, target) in enumerate(
            [
                (place_in, share.at[0]),
                (spin_in, share.at[1]),
                (core_in, share.at[2, pl.ds(0, 1)]),
                (node_place_in, node_place),
                (node_block_in, node_block),
            ]
        )
    ]
    for load in loads:
        load.start()

    peers = [(0, turn) for turn in range(1, NG)] + [(2 * turn, 0) for turn in range(1, NG)]
    peers += [(1, 0), (-1, 0), (1, 1), (1, -1), (-1, 1), (-1, -1)]
    barrier = pltpu.get_barrier_semaphore()
    for peer in peers:
        pl.semaphore_signal(barrier, inc=1, device_id=device(*peer), device_id_type=MESH)
    for load in loads:
        load.wait()
    own_live = grid * 256 + lax.broadcasted_iota(jnp.int32, (1, 256), 1) < counts[wake]
    squared_core = share[2, 0:1] * share[2, 0:1]
    mine[...] = jnp.concatenate(
        [jnp.where(own_live, share[1], 0.0), share[0], squared_core, 0.5 * squared_core], axis=0
    )
    pl.semaphore_wait(barrier, len(peers))

    def describe(source, target, sends, recvs, slot, peer):
        return pltpu.make_async_remote_copy(
            src_ref=source,
            dst_ref=target,
            send_sem=sends.at[slot],
            recv_sem=recvs.at[slot],
            device_id=device(*peer),
            device_id_type=MESH,
        )

    def send(*arguments):
        copy = describe(*arguments)
        copy.start()
        return copy

    own = mine[...]
    centre = [
        jnp.broadcast_to(jnp.sum(own[3 + c : 4 + c], axis=1, keepdims=True) * (1.0 / 256.0), (1, 1024))
        for c in range(3)
    ]
    first = [send(mine, mine, send_one, recv_one, turn - 1, (0, turn)) for turn in range(1, NG)]

    names = node_block[...]
    spots = centred(node_place, centre)
    rows = target_rows(spots, square_sum(spots), False)
    members = jnp.where(lax.broadcasted_iota(jnp.int32, (NW, 1024), 0) == names, 1.0, 0.0)
    triangle = jnp.where(
        lax.broadcasted_iota(jnp.int32, (128, 128), 0) <= lax.broadcasted_iota(jnp.int32, (128, 128), 1),
        1.0,
        0.0,
    ).astype(BF)
    pieces = jnp.concatenate([members[:, 128 * k : 128 * (k + 1)] for k in range(8)], axis=0)
    running = jnp.dot(pieces.astype(BF), triangle, preferred_element_type=F32)
    before = jnp.zeros((NW, 1), F32)
    ranks = []
    for k in range(8):
        part = running[NW * k : NW * (k + 1)]
        ranks.append(part + before)
        before = before + part[:, 127:128]
    rank = jnp.sum(members * jnp.concatenate(ranks, axis=1), axis=0, keepdims=True) - 1.0
    slot = names * 128 + rank.astype(jnp.int32)
    slot_eight = lax.broadcasted_iota(jnp.int32, (128, 8), 0).astype(F32)

    place = centred(own[3:6], centre)
    weight = square_sum(place) + own[7:8]
    identity = jnp.where(
        lax.broadcasted_iota(jnp.int32, (256, 256), 0) == lax.broadcasted_iota(jnp.int32, (256, 256), 1),
        1.0,
        0.0,
    ).astype(BF)
    targets_ref[...] = dot_nt(identity, target_rows(place, weight, True)).astype(BF)
    total[...] = jnp.zeros_like(total)

    for copy in first:
        copy.wait_recv()
    block_here = gathered.at[pair, side]
    second = [
        send(block_here, block_here, send_two, recv_two, turn - 1, (2 * turn, 0)) for turn in (1, 2, 7, 3, 4, 5, 6)
    ]

    top, bottom = pl.ds(0, 3), pl.ds(13, 3)
    low_rows, high_rows = pl.ds(0, 3), pl.ds(5, 3)
    begin, finish = pl.ds(0, 128), pl.ds(16256, 128)
    middle, before_lanes, after_lanes = pl.ds(256, 16384), pl.ds(128, 128), pl.ds(16640, 128)
    everything, every = pl.ds(0, 16384), pl.ds(0, 16)
    plan = [
        ((-1, 0), top, everything, 0, low_rows, middle),
        ((1, 0), bottom, everything, 0, high_rows, middle),
        ((0, -1), every, begin, 2, every, begin),
        ((0, 1), every, finish, 1, every, begin),
        ((-1, -1), top, begin, 0, low_rows, after_lanes),
        ((-1, 1), top, finish, 0, low_rows, before_lanes),
        ((1, -1), bottom, begin, 0, high_rows, after_lanes),
        ((1, 1), bottom, finish, 0, high_rows, before_lanes),
    ]
    halos = []
    for k, (peer, from_rows, from_lanes, which, to_rows, to_lanes) in enumerate(plan):
        for part, (source, targets) in enumerate(
            [
                (flow.at[:, from_rows, from_lanes], (rows_halo, left_halo, right_halo)),
                (sections.at[from_rows, from_lanes], (kind_rows, kind_left, kind_right)),
            ]
        ):
            target = targets[which].at[:, to_rows, to_lanes] if part == 0 else targets[which].at[to_rows, to_lanes]
            halos.append((peer, describe(source, target, send_halo, recv_halo, 2 * k + part, peer)))

    def within(wake_by, grid_by):
        to_wake, to_grid = wake + wake_by, grid + grid_by
        return (to_wake >= 0) & (to_wake < NW) & (to_grid >= 0) & (to_grid < NG)

    def start_halos():
        for peer, copy in halos:
            pl.when(within(*peer))(copy.start)

    def finish_halos():
        for peer, copy in halos:
            pl.when(within(*peer))(copy.wait_send)
            pl.when(within(-peer[0], -peer[1]))(copy.wait_recv)

    for part in range(8):
        chosen = jnp.where(
            lax.broadcasted_iota(jnp.int32, (256, 1024), 0) + part * 256 == slot, 1.0, 0.0
        ).astype(BF)
        points[256 * part : 256 * (part + 1), :] = dot_nt(chosen, rows).astype(BF)

    line = lax.broadcasted_iota(jnp.int32, (8, CHUNK), 0)
    is_place = (line >= 3) & (line < 6)
    shift = jnp.zeros((8, CHUNK), F32)
    for c in range(3):
        shift = jnp.where(line == 3 + c, jnp.broadcast_to(centre[c][:, 0:CHUNK], (8, CHUNK)), shift)

    def load_source(block, start):
        tile = gathered[block // 2, lax.rem(block, 2), :, pl.ds(start, CHUNK)] - shift
        summed = jnp.where(is_place, tile * tile, 0.0)
        for step in (4, 2, 1):
            summed = summed + pltpu.roll(summed, step, 0)
        full = tile + jnp.where(line >= 6, summed, 0.0)
        high, middle, low = split_three(jnp.where(line == 0, 1.0, full))
        distance = jnp.concatenate([high, high, high, middle, middle, low], axis=0).astype(BF)
        down_one, down_two = pltpu.roll(tile, 1, 0), pltpu.roll(tile, 2, 0)
        place_next = jnp.where(line == 5, down_two, pltpu.roll(tile, 7, 0))
        place_last = jnp.where(line == 3, pltpu.roll(tile, 6, 0), down_one)
        spin_next = jnp.where(line == 5, pltpu.roll(tile, 5, 0), down_two)
        spin_last = jnp.where(line == 3, down_one, pltpu.roll(tile, 4, 0))
        crossed = place_next * spin_last - place_last * spin_next
        moment = jnp.where(line < 3, tile, jnp.where(line < 6, crossed, 0.0))
        return distance, moment, [full[k : k + 1] for k in (3, 4, 5, 7)]

    def node_slots(block):
        return pl.ds(pl.multiple_of(block * 128, 128), 128)

    def split_two(value):
        high = value.astype(BF)
        return high, (value - high.astype(F32)).astype(BF)

    def near(offset, with_nodes=True):
        block = lax.rem(wake + offset + NW, NW)
        looking = targets_ref[...]
        if with_nodes:
            looking = jnp.concatenate([looking, points[node_slots(block), :]], axis=0)

        def run(step, gained):
            distance, moment, factors = load_source(block, pl.multiple_of(step * CHUNK, CHUNK))
            columns = source_columns(moment, factors)
            columns = jnp.concatenate(columns + [jnp.zeros_like(moment)], axis=0).astype(BF)
            for cut in range(0, CHUNK, CHUNK):
                root = lax.rsqrt(
                    jnp.dot(looking, distance[:, cut : cut + CHUNK], preferred_element_type=F32)
                )
                second_power = root * root
                third = second_power * root
                fifth = third[0:256] * second_power[0:256]
                weights = split_two(fifth)
                if with_nodes:
                    weights += split_two(third[256:384])
                added = dot_nt(jnp.concatenate(weights, axis=0), columns[:, cut : cut + CHUNK])
                gained = added if gained is None else gained + added
            return gained

        gained = None
        for step in range(PB // CHUNK):
            gained = run(step, gained)
        total[...] += gained[0:256] + gained[256:512]
        if not with_nodes:
            return
        sums = gained[512:640] + gained[640:768]
        node_total[node_slots(block), :] = sums[:, 0:8] + sums[:, 40:48] + sums[:, 80:88]

    def far(offset):
        block = lax.rem(wake + offset + NW, NW)
        looking = points[node_slots(block), :]
        gained = None
        for step in range(PB // CHUNK):
            distance, moment, _ = load_source(block, pl.multiple_of(step * CHUNK, CHUNK))
            columns = source_columns(moment, [])
            columns = jnp.concatenate(columns + [jnp.zeros_like(moment)], axis=0).astype(BF)
            root = lax.rsqrt(jnp.dot(looking, distance, preferred_element_type=F32))
            high, low = split_two(root * root * root)
            added = dot_nt(jnp.concatenate([high, low], axis=0), columns)
            gained = added if gained is None else gained + added
        sums = gained[0:128] + gained[128:256]
        node_total[node_slots(block), :] = sums[:, 0:8] + sums[:, 8:16] + sums[:, 16:24]

    def loop(function, offsets):
        def body(turn, carry):
            function(offsets(turn))
            return carry

        return lambda amount: lax.fori_loop(0, amount, body, 0)

    def near_even(turn):
        for k in range(2):
            pl.when(turn == k + 1)(second[k].wait_recv)
        near(-2 * turn)

    loop(near_even, lambda turn: turn)(3)
    for copy in second[2:]:
        copy.wait_recv()
    third_copy = send(
        gathered.at[:, side], gathered.at[:, side], send_three, recv_three, 0, (1 - 2 * side, 0)
    )
    start_halos()
    near(2)
    loop(lambda offset: [far(offset + 2 * k) for k in range(4)], lambda turn: 4 + turn)(1)
    third_copy.wait_recv()
    loop(lambda offset: [far(offset + 2 * k) for k in range(7)], lambda turn: turn - 1)(1)
    near(-3)

    answers = None
    for part in range(8):
        slot_rows = lax.broadcasted_iota(jnp.int32, (256, 1024), 0) + part * 256
        chosen = jnp.where(slot_rows == slot, 1.0, 0.0).astype(BF)
        gained = jnp.concatenate(
            [
                jnp.where(
                    slot_eight < before[block : block + 1],
                    node_total[128 * block : 128 * (block + 1), :],
                    0.0,
                )
                for block in (2 * part, 2 * part + 1)
            ],
            axis=0,
        )
        high, mid, low = split_three(gained)
        stacked = jnp.concatenate([high, mid, low, jnp.zeros_like(low)], axis=1).astype(BF)
        added = lax.dot_general(stacked, chosen, (((0,), (0,)), ((), ())), preferred_element_type=F32)
        answers = added if answers is None else answers + added
    found = answers[0:8] + answers[8:16] + answers[16:24]
    moved = cross_rows(spots, [found[c : c + 1] for c in range(3)])
    for c in range(3):
        result = (moved[c] - found[3 + c : 4 + c]) * SCALE
        even = jnp.concatenate([result[:, 128 * k : 128 * (k + 1)] for k in range(8)], axis=0)
        odd = pltpu.roll(even, 64, 1)
        own_nodes[c] = jnp.concatenate(
            [(even, odd)[r % 2][r // 2 : r // 2 + 1] for r in range(16)], axis=0
        )
    shared = [
        send(own_nodes, far_nodes.at[k], send_node, recv_node, k, peer)
        for k, peer in enumerate([(0, -1), (-1, 0), (1, 0), (-1, -1), (1, -1)])
    ]

    results = [
        pltpu.make_async_copy(source, target, sem_out.at[k])
        for k, (source, target) in enumerate(
            [(own_nodes, own_nodes_to), (velocity_out, velocity_to), (stretch_out, stretch_to)]
        )
    ]
    results[0].start()
    loop(lambda offset: near(offset, False), lambda turn: 2 * turn - 1)(3)

    spin = [own[c : c + 1] for c in range(3)]
    sums = jnp.transpose(total[...])
    sums = sums[0:40] + sums[40:80] + sums[80:120]
    plain = [sums[k : k + 1] for k in range(6)]
    turned = [[sums[8 + 8 * c + k : 9 + 8 * c + k] for k in range(6)] for c in range(3)]
    heavy = [sums[32 + k : 33 + k] for k in range(6)]
    mixed = [
        weight * plain[k]
        + heavy[k]
        - 2.0 * (place[0] * turned[0][k] + place[1] * turned[1][k] + place[2] * turned[2][k])
        for k in range(6)
    ]
    live = grid * 256 + lax.broadcasted_iota(jnp.int32, (1, 256), 1) < counts[wake]
    factor = jnp.where(live, SCALE, 0.0)
    swept = cross_rows(place, mixed[0:3])
    bent_own = cross_rows(place, plain[0:3])
    along = spin[0] * place[0] + spin[1] * place[1] + spin[2] * place[2]
    pulled = [spin[0] * turned[0][k] + spin[1] * turned[1][k] + spin[2] * turned[2][k] for k in range(6)]
    bent_far = cross_rows(place, pulled[0:3])
    lifted = cross_rows(spin, mixed[0:3])
    for c in range(3):
        velocity_out[c : c + 1, :] = (swept[c] - mixed[3 + c]) * factor
        bent = along * (bent_own[c] - plain[3 + c]) - (bent_far[c] - pulled[3 + c])
        stretch_out[c : c + 1, :] = (lifted[c] - 3.0 * bent) * factor

    results[1].start()
    results[2].start()
    for copy in shared:
        copy.wait()
    finish_halos()
    for copy in results:
        copy.wait()
    for copy in first + second + [third_copy]:
        copy.wait_send()


ANY = pl.BlockSpec(memory_space=pltpu.HBM)
SCALAR = pl.BlockSpec(memory_space=pltpu.SMEM)


def gather_and_sum(counts, place, spin, core, node_place, node_block, flow, sections):
    dma = pltpu.SemaphoreType.DMA
    return pl.pallas_call(
        gather_kernel,
        out_shape=[
            jax.ShapeDtypeStruct((3, 256), F32),
            jax.ShapeDtypeStruct((3, 256), F32),
            jax.ShapeDtypeStruct((3, 16, 128), F32),
            jax.ShapeDtypeStruct((5, 3, 16, 128), F32),
            jax.ShapeDtypeStruct((5, 8, BUFFER), F32),
            jax.ShapeDtypeStruct((5, 16, 128), F32),
            jax.ShapeDtypeStruct((5, 16, 128), F32),
            jax.ShapeDtypeStruct((8, BUFFER), jnp.int32),
            jax.ShapeDtypeStruct((16, 128), jnp.int32),
            jax.ShapeDtypeStruct((16, 128), jnp.int32),
        ],
        in_specs=[SCALAR] + [ANY] * 7,
        out_specs=[ANY] * 10,
        scratch_shapes=[
            pltpu.VMEM((3, 256), F32),
            pltpu.VMEM((3, 256), F32),
            pltpu.VMEM((3, 16, 128), F32),
            pltpu.VMEM((NW // 2, 2, 8, PB), F32),
            pltpu.VMEM((3, 3, 256), F32),
            pltpu.VMEM((3, 1024), F32),
            pltpu.VMEM((1, 1024), jnp.int32),
            pltpu.VMEM((NW * 128, 48), BF),
            pltpu.VMEM((256, 48), BF),
            pltpu.VMEM((256, 128), F32),
            pltpu.VMEM((NW * 128, 8), F32),
            dma((5,)),
            dma((NG - 1,)),
            dma((NG - 1,)),
            dma((NG - 1,)),
            dma((NG - 1,)),
            dma((1,)),
            dma((1,)),
            dma((16,)),
            dma((16,)),
            dma((5,)),
            dma((5,)),
            dma((3,)),
        ],
        compiler_params=pltpu.CompilerParams(
            collective_id=0, has_side_effects=True, vmem_limit_bytes=LIMIT
        ),
    )(counts, place, spin, core, node_place, node_block, flow, sections)


TILES = 130
BUFFER = 16640 + 256


def sweep_kernel(
    flow, sections, viscosity, rows_halo, left_halo, right_halo, kind_rows, kind_left, kind_right,
    own_nodes_in, far_nodes_in, velocity, stretch, out, velocity_out, stretch_out,
    own_nodes, far_nodes, rows_in, kind, first, second, rates, rows_out, nodes, sem_in, sem_out, sem_small,
):
    fields = 5
    wake = lax.axis_index("wake")
    grid = lax.axis_index("grid")
    own_rows, halo_rows = pl.ds(0, 16), pl.ds(16, 8)
    middle, before, after = pl.ds(256, 16384), pl.ds(128, 128), pl.ds(16640, 128)
    kinds = [
        pltpu.make_async_copy(source, target, sem_in.at[4 * fields + k])
        for k, (source, target) in enumerate(
            [
                (sections, kind.at[own_rows, middle]),
                (kind_rows, kind.at[halo_rows, :]),
                (kind_left, kind.at[own_rows, before]),
                (kind_right, kind.at[own_rows, after]),
            ]
        )
    ]
    def incoming(f):
        return [
            pltpu.make_async_copy(source, target, sem_in.at[4 * f + k])
            for k, (source, target) in enumerate(
                [
                    (flow.at[f], rows_in.at[f, own_rows, middle]),
                    (rows_halo.at[f], rows_in.at[f, halo_rows, :]),
                    (left_halo.at[f], rows_in.at[f, own_rows, before]),
                    (right_halo.at[f], rows_in.at[f, own_rows, after]),
                ]
            )
        ]

    def outgoing(f, half):
        return pltpu.make_async_copy(
            rows_out.at[f, :, pl.ds(256 + 8192 * half, 8192)],
            out.at[f, :, pl.ds(8192 * half, 8192)],
            sem_out.at[2 * f + half],
        )

    for copy in kinds + incoming(0):
        copy.start()
    small = [
        pltpu.make_async_copy(source, target, sem_small.at[k])
        for k, (source, target) in enumerate(
            [
                (own_nodes_in, own_nodes),
                (far_nodes_in, far_nodes),
                (velocity, velocity_out),
                (stretch, stretch_out),
            ]
        )
    ]
    for copy in small:
        copy.start()
    for copy in small[0:2]:
        copy.wait()

    lane = lax.broadcasted_iota(jnp.int32, (24, 128), 1)
    row = lax.broadcasted_iota(jnp.int32, (24, 128), 0)
    is_first, is_last = lane == 0, lane == 127
    inside_rows = ((row < 20) | (wake > 0)) & ((row < 16) | (row >= 20) | (wake < NW - 1))
    lane8 = lax.broadcasted_iota(jnp.int32, (8, 128), 1)
    row8 = lax.broadcasted_iota(jnp.int32, (8, 128), 0)

    for c in range(3):
        def with_next(rows, column):
            return jnp.where(lane8 == 64, jnp.broadcast_to(column, (8, 128)), rows)

        halo = jnp.where(row8 < 4, far_nodes[1, c, 0:8], far_nodes[2, c, 8:16])
        halo_next = jnp.where(row8 < 4, far_nodes[3, c, 0:8], far_nodes[4, c, 8:16])
        parts = [
            with_next(own_nodes[c, 0:8], far_nodes[0, c, 0:8, 0:1]),
            with_next(own_nodes[c, 8:16], far_nodes[0, c, 8:16, 0:1]),
            with_next(halo, halo_next[:, 0:1]),
        ]
        nodes[c] = jnp.where(inside_rows, jnp.concatenate(parts, axis=0), 0.0)

    for copy in kinds:
        copy.wait()

    tile_lanes = lambda t: pl.ds(t * 128, 128)

    def field(f, done):
        for copy in incoming(f):
            copy.wait()

        @pl.when(f + 1 < fields)
        def _():
            for copy in incoming(f + 1):
                copy.start()

        rows_in[f, 16:24, 256:16640] = jnp.where(
            inside_rows[16:24, 0:1], rows_in[f, 16:24, 256:16640], 0.0
        )
        for start, edge in ((128, grid == 0), (16640, grid == NG - 1)):
            keep = inside_rows & jnp.logical_not(edge)
            rows_in[f, :, start : start + 128] = jnp.where(keep, rows_in[f, :, start : start + 128], 0.0)
        @pl.when((f >= 1) & (f <= 3))
        def _():
            given = nodes[jnp.clip(f - 1, 0, 2)]
            for k in range(65):
                start = 256 + 256 * k
                column = jnp.broadcast_to(given[:, k : k + 1], (24, 128))
                if k == 64:
                    column = jnp.where(grid == NG - 1, 0.0, column)
                rows_in[f, :, start : start + 128] = jnp.where(
                    is_first, column, rows_in[f, :, start : start + 128]
                )

        def sweep(load, finish):
            here = load(1)
            last_right, right, left = pltpu.roll(load(0), 1, 1), pltpu.roll(here, 1, 1), pltpu.roll(here, 127, 1)
            for t in range(1, TILES + 1):
                following = load(t + 1)
                next_right = pltpu.roll(following, 1, 1)
                next_left = pltpu.roll(following, 127, 1)
                across = jnp.where(is_first, last_right, right) + jnp.where(is_last, next_left, left)
                along = pltpu.roll(here, 1, 0) + pltpu.roll(here, 23, 0)
                finish(t, here, across + along)
                last_right, here, right, left = right, following, next_right, next_left

        def finish_first(t, here, beside):
            name = kind[:, tile_lanes(t)]
            rate = jnp.where(
                name == 0, viscosity[0, f], jnp.where(name == 1, viscosity[1, f], viscosity[2, f])
            )
            if t == 1:
                rate = jnp.where(grid > 0, rate, 0.0)
            if t == TILES:
                rate = jnp.where(grid < NG - 1, rate, 0.0)
            rate = jnp.concatenate([rate[0:16], jnp.where(inside_rows[16:24], rate[16:24], 0.0)], axis=0)
            rates[:, tile_lanes(t)] = rate
            first[:, tile_lanes(t)] = here + rate * (beside - 4.0 * here)

        def finish_second(t, here, beside):
            second[:, tile_lanes(t)] = here + rates[:, tile_lanes(t)] * (beside - 4.0 * here)

        def finish_third(t, here, beside):
            rows_out[f, :, tile_lanes(t)] = (here + rates[:, tile_lanes(t)] * (beside - 4.0 * here))[0:16]
            if t == 65:
                outgoing(f, 0).start()

        sweep(lambda t: rows_in[f, :, tile_lanes(t)], finish_first)
        sweep(lambda t: first[:, tile_lanes(t)], finish_second)
        sweep(lambda t: second[:, tile_lanes(t)], finish_third)
        outgoing(f, 1).start()
        return done

    lax.fori_loop(0, fields, field, 0)
    for f in range(fields):
        outgoing(f, 0).wait()
        outgoing(f, 1).wait()
    for copy in small[2:4]:
        copy.wait()


def sweep_fields(*arrays):
    dma = pltpu.SemaphoreType.DMA
    return pl.pallas_call(
        sweep_kernel,
        out_shape=[
            jax.ShapeDtypeStruct((5, 16, 16384), F32),
            jax.ShapeDtypeStruct((3, 256), F32),
            jax.ShapeDtypeStruct((3, 256), F32),
        ],
        in_specs=[ANY, ANY, SCALAR] + [ANY] * 10,
        out_specs=[ANY] * 3,
        scratch_shapes=[
            pltpu.VMEM((3, 16, 128), F32),
            pltpu.VMEM((5, 3, 16, 128), F32),
            pltpu.VMEM((5, 24, BUFFER), F32),
            pltpu.VMEM((24, BUFFER), jnp.int32),
            pltpu.VMEM((24, BUFFER), F32),
            pltpu.VMEM((24, BUFFER), F32),
            pltpu.VMEM((24, BUFFER), F32),
            pltpu.VMEM((5, 16, BUFFER), F32),
            pltpu.VMEM((3, 24, 128), F32),
            dma((24,)),
            dma((10,)),
            dma((4,)),
        ],
        compiler_params=pltpu.CompilerParams(vmem_limit_bytes=LIMIT),
    )(*arrays)


def on_device(
    flow,
    section_map,
    viscosity,
    particle_position,
    particle_strength,
    particle_core,
    shed_counts,
    node_position,
    node_block,
):
    (
        velocity, stretch, own_nodes, far_nodes, rows_halo, left_halo, right_halo, kind_rows, kind_left, kind_right,
    ) = gather_and_sum(
        shed_counts,
        particle_position,
        particle_strength,
        particle_core.reshape(1, 256),
        node_position,
        node_block.reshape(1, 1024),
        flow,
        section_map,
    )
    field, velocity, stretch = sweep_fields(
        flow, section_map, viscosity, rows_halo, left_halo, right_halo, kind_rows, kind_left, kind_right,
        own_nodes, far_nodes, velocity, stretch,
    )
    return (field, velocity, stretch)


def solution(mesh):
    return jax.shard_map(
        on_device,
        mesh=mesh,
        in_specs=(
            P(None, "wake", "grid"),
            P("wake", "grid"),
            P(),
            P(None, ("wake", "grid")),
            P(None, ("wake", "grid")),
            P(("wake", "grid")),
            P(),
            P(None, ("wake", "grid")),
            P(("wake", "grid"), None),
        ),
        out_specs=(P(None, "wake", "grid"), P(None, ("wake", "grid")), P(None, ("wake", "grid"))),
        check_vma=False,
    )
```

```python
import math

import jax
import jax.numpy as jnp
from jax import lax
from jax.experimental import pallas as pl
from jax.experimental.pallas import tpu as pltpu
from jax.sharding import PartitionSpec as P

PB = 2048
NW = 16
NG = 8
CHUNK = 1024
LIMIT = 64 << 20
BF = jnp.bfloat16
F32 = jnp.float32
MESH = pl.DeviceIdType.MESH
SCALE = -1.0 / (4.0 * math.pi)
WHOLE = pl.BlockSpec(memory_space=pltpu.VMEM)


def split_three(value):
    high = value.astype(BF).astype(F32)
    rest = value - high
    middle = rest.astype(BF).astype(F32)
    return high, middle, rest - middle


def dot_nt(first, second):
    return lax.dot_general(first, second, (((1,), (1,)), ((), ())), preferred_element_type=F32)


def cross_rows(first, second):
    return [
        first[1] * second[2] - first[2] * second[1],
        first[2] * second[0] - first[0] * second[2],
        first[0] * second[1] - first[1] * second[0],
    ]


def target_rows(place, weight, halved):
    ones = jnp.ones_like(weight)
    none = jnp.zeros_like(weight)
    parts = split_three(jnp.concatenate([weight, none, none] + [-2.0 * row for row in place] + [none, none], axis=0))
    unit = jnp.concatenate([none] * 6 + [none if halved else ones, ones if halved else none], axis=0)
    high, middle, low = parts
    return jnp.concatenate([high + unit, middle, low, high + unit, middle, high + unit], axis=0).astype(BF)


def source_columns(moment, factors):
    parts = [split_three(moment)] + [split_three(moment * factor) for factor in factors]
    columns = [part[level] for level in range(3) for part in parts]
    return columns


def centred(rows, centre):
    return [rows[c : c + 1] - centre[c][:, 0 : rows.shape[1]] for c in range(3)]


def square_sum(place):
    return place[0] * place[0] + place[1] * place[1] + place[2] * place[2]


def gather_kernel(
    counts, place_in, spin_in, core_in, node_place_in, node_block_in, flow, sections,
    velocity_to, stretch_to, own_nodes_to, far_nodes, rows_halo, left_halo, right_halo,
    kind_rows, kind_left, kind_right,
    velocity_out, stretch_out, own_nodes, gathered, share, node_place, node_block, points, targets_ref, total, node_total,
    sem_in, send_one, recv_one, send_two, recv_two, send_three, recv_three,
    send_halo, recv_halo, send_node, recv_node, sem_out,
):
    wake = lax.axis_index("wake")
    grid = lax.axis_index("grid")
    side = lax.rem(wake, 2)
    pair = wake // 2
    lanes = pl.ds(pl.multiple_of(grid * 256, 256), 256)
    mine = gathered.at[pair, side, :, lanes]

    def device(wake_by, grid_by):
        return {"wake": lax.rem(wake + wake_by + NW, NW), "grid": lax.rem(grid + grid_by + NG, NG)}

    loads = [
        pltpu.make_async_copy(source, target, sem_in.at[k])
        for k, (source, target) in enumerate(
            [
                (place_in, share.at[0]),
                (spin_in, share.at[1]),
                (core_in, share.at[2, pl.ds(0, 1)]),
                (node_place_in, node_place),
                (node_block_in, node_block),
            ]
        )
    ]
    for load in loads:
        load.start()

    peers = [(0, turn) for turn in range(1, NG)] + [(2 * turn, 0) for turn in range(1, NG)]
    peers += [(1, 0), (-1, 0), (1, 1), (1, -1), (-1, 1), (-1, -1)]
    barrier = pltpu.get_barrier_semaphore()
    for peer in peers:
        pl.semaphore_signal(barrier, inc=1, device_id=device(*peer), device_id_type=MESH)
    for load in loads:
        load.wait()
    own_live = grid * 256 + lax.broadcasted_iota(jnp.int32, (1, 256), 1) < counts[wake]
    squared_core = share[2, 0:1] * share[2, 0:1]
    mine[...] = jnp.concatenate(
        [jnp.where(own_live, share[1], 0.0), share[0], squared_core, 0.5 * squared_core], axis=0
    )
    pl.semaphore_wait(barrier, len(peers))

    def describe(source, target, sends, recvs, slot, peer):
        return pltpu.make_async_remote_copy(
            src_ref=source,
            dst_ref=target,
            send_sem=sends.at[slot],
            recv_sem=recvs.at[slot],
            device_id=device(*peer),
            device_id_type=MESH,
        )

    def send(*arguments):
        copy = describe(*arguments)
        copy.start()
        return copy

    own = mine[...]
    centre = [
        jnp.broadcast_to(jnp.sum(own[3 + c : 4 + c], axis=1, keepdims=True) * (1.0 / 256.0), (1, 1024))
        for c in range(3)
    ]
    first = [send(mine, mine, send_one, recv_one, turn - 1, (0, turn)) for turn in range(1, NG)]

    names = node_block[...]
    spots = centred(node_place, centre)
    rows = target_rows(spots, square_sum(spots), False)
    members = jnp.where(lax.broadcasted_iota(jnp.int32, (NW, 1024), 0) == names, 1.0, 0.0)
    triangle = jnp.where(
        lax.broadcasted_iota(jnp.int32, (128, 128), 0) <= lax.broadcasted_iota(jnp.int32, (128, 128), 1),
        1.0,
        0.0,
    ).astype(BF)
    pieces = jnp.concatenate([members[:, 128 * k : 128 * (k + 1)] for k in range(8)], axis=0)
    running = jnp.dot(pieces.astype(BF), triangle, preferred_element_type=F32)
    before = jnp.zeros((NW, 1), F32)
    ranks = []
    for k in range(8):
        part = running[NW * k : NW * (k + 1)]
        ranks.append(part + before)
        before = before + part[:, 127:128]
    rank = jnp.sum(members * jnp.concatenate(ranks, axis=1), axis=0, keepdims=True) - 1.0
    slot = names * 128 + rank.astype(jnp.int32)
    slot_eight = lax.broadcasted_iota(jnp.int32, (128, 8), 0).astype(F32)

    place = centred(own[3:6], centre)
    weight = square_sum(place) + own[7:8]
    identity = jnp.where(
        lax.broadcasted_iota(jnp.int32, (256, 256), 0) == lax.broadcasted_iota(jnp.int32, (256, 256), 1),
        1.0,
        0.0,
    ).astype(BF)
    targets_ref[...] = dot_nt(identity, target_rows(place, weight, True)).astype(BF)
    total[...] = jnp.zeros_like(total)

    for copy in first:
        copy.wait_recv()
    block_here = gathered.at[pair, side]
    second = [
        send(block_here, block_here, send_two, recv_two, turn - 1, (2 * turn, 0)) for turn in (1, 2, 7, 3, 4, 5, 6)
    ]

    top, bottom = pl.ds(0, 3), pl.ds(13, 3)
    low_rows, high_rows = pl.ds(0, 3), pl.ds(5, 3)
    begin, finish = pl.ds(0, 128), pl.ds(16256, 128)
    middle, before_lanes, after_lanes = pl.ds(256, 16384), pl.ds(128, 128), pl.ds(16640, 128)
    everything, every = pl.ds(0, 16384), pl.ds(0, 16)
    plan = [
        ((-1, 0), top, everything, 0, low_rows, middle),
        ((1, 0), bottom, everything, 0, high_rows, middle),
        ((0, -1), every, begin, 2, every, begin),
        ((0, 1), every, finish, 1, every, begin),
        ((-1, -1), top, begin, 0, low_rows, after_lanes),
        ((-1, 1), top, finish, 0, low_rows, before_lanes),
        ((1, -1), bottom, begin, 0, high_rows, after_lanes),
        ((1, 1), bottom, finish, 0, high_rows, before_lanes),
    ]
    halos = []
    for k, (peer, from_rows, from_lanes, which, to_rows, to_lanes) in enumerate(plan):
        for part, (source, targets) in enumerate(
            [
                (flow.at[:, from_rows, from_lanes], (rows_halo, left_halo, right_halo)),
                (sections.at[from_rows, from_lanes], (kind_rows, kind_left, kind_right)),
            ]
        ):
            target = targets[which].at[:, to_rows, to_lanes] if part == 0 else targets[which].at[to_rows, to_lanes]
            halos.append((peer, describe(source, target, send_halo, recv_halo, 2 * k + part, peer)))

    def within(wake_by, grid_by):
        to_wake, to_grid = wake + wake_by, grid + grid_by
        return (to_wake >= 0) & (to_wake < NW) & (to_grid >= 0) & (to_grid < NG)

    def start_halos():
        for peer, copy in halos:
            pl.when(within(*peer))(copy.start)

    def finish_halos():
        for peer, copy in halos:
            pl.when(within(*peer))(copy.wait_send)
            pl.when(within(-peer[0], -peer[1]))(copy.wait_recv)

    for part in range(8):
        chosen = jnp.where(
            lax.broadcasted_iota(jnp.int32, (256, 1024), 0) + part * 256 == slot, 1.0, 0.0
        ).astype(BF)
        points[256 * part : 256 * (part + 1), :] = dot_nt(chosen, rows).astype(BF)

    line = lax.broadcasted_iota(jnp.int32, (8, CHUNK), 0)
    is_place = (line >= 3) & (line < 6)
    shift = jnp.zeros((8, CHUNK), F32)
    for c in range(3):
        shift = jnp.where(line == 3 + c, jnp.broadcast_to(centre[c][:, 0:CHUNK], (8, CHUNK)), shift)

    def load_source(block, start):
        tile = gathered[block // 2, lax.rem(block, 2), :, pl.ds(start, CHUNK)] - shift
        summed = jnp.where(is_place, tile * tile, 0.0)
        for step in (4, 2, 1):
            summed = summed + pltpu.roll(summed, step, 0)
        full = tile + jnp.where(line >= 6, summed, 0.0)
        high, middle, low = split_three(jnp.where(line == 0, 1.0, full))
        distance = jnp.concatenate([high, high, high, middle, middle, low], axis=0).astype(BF)
        down_one, down_two = pltpu.roll(tile, 1, 0), pltpu.roll(tile, 2, 0)
        place_next = jnp.where(line == 5, down_two, pltpu.roll(tile, 7, 0))
        place_last = jnp.where(line == 3, pltpu.roll(tile, 6, 0), down_one)
        spin_next = jnp.where(line == 5, pltpu.roll(tile, 5, 0), down_two)
        spin_last = jnp.where(line == 3, down_one, pltpu.roll(tile, 4, 0))
        crossed = place_next * spin_last - place_last * spin_next
        moment = jnp.where(line < 3, tile, jnp.where(line < 6, crossed, 0.0))
        return distance, moment, [full[k : k + 1] for k in (3, 4, 5, 7)]

    def node_slots(block):
        return pl.ds(pl.multiple_of(block * 128, 128), 128)

    def split_two(value):
        high = value.astype(BF)
        return high, (value - high.astype(F32)).astype(BF)

    def near(offset, with_nodes=True):
        block = lax.rem(wake + offset + NW, NW)
        looking = targets_ref[...]
        if with_nodes:
            looking = jnp.concatenate([looking, points[node_slots(block), :]], axis=0)

        def run(step, gained):
            distance, moment, factors = load_source(block, pl.multiple_of(step * CHUNK, CHUNK))
            columns = source_columns(moment, factors)
            columns = jnp.concatenate(columns + [jnp.zeros_like(moment)], axis=0).astype(BF)
            for cut in range(0, CHUNK, CHUNK):
                root = lax.rsqrt(
                    jnp.dot(looking, distance[:, cut : cut + CHUNK], preferred_element_type=F32)
                )
                second_power = root * root
                third = second_power * root
                fifth = third[0:256] * second_power[0:256]
                weights = split_two(fifth)
                if with_nodes:
                    weights += split_two(third[256:384])
                added = dot_nt(jnp.concatenate(weights, axis=0), columns[:, cut : cut + CHUNK])
                gained = added if gained is None else gained + added
            return gained

        gained = None
        for step in range(PB // CHUNK):
            gained = run(step, gained)
        total[...] += gained[0:256] + gained[256:512]
        if not with_nodes:
            return
        sums = gained[512:640] + gained[640:768]
        node_total[node_slots(block), :] = sums[:, 0:8] + sums[:, 40:48] + sums[:, 80:88]

    def far(offset):
        block = lax.rem(wake + offset + NW, NW)
        looking = points[node_slots(block), :]
        gained = None
        for step in range(PB // CHUNK):
            distance, moment, _ = load_source(block, pl.multiple_of(step * CHUNK, CHUNK))
            columns = source_columns(moment, [])
            columns = jnp.concatenate(columns + [jnp.zeros_like(moment)], axis=0).astype(BF)
            root = lax.rsqrt(jnp.dot(looking, distance, preferred_element_type=F32))
            high, low = split_two(root * root * root)
            added = dot_nt(jnp.concatenate([high, low], axis=0), columns)
            gained = added if gained is None else gained + added
        sums = gained[0:128] + gained[128:256]
        node_total[node_slots(block), :] = sums[:, 0:8] + sums[:, 8:16] + sums[:, 16:24]

    def loop(function, offsets):
        def body(turn, carry):
            function(offsets(turn))
            return carry

        return lambda amount: lax.fori_loop(0, amount, body, 0)

    def near_even(turn):
        for k in range(2):
            pl.when(turn == k + 1)(second[k].wait_recv)
        near(-2 * turn)

    loop(near_even, lambda turn: turn)(3)
    for copy in second[2:]:
        copy.wait_recv()
    third_copy = send(
        gathered.at[:, side], gathered.at[:, side], send_three, recv_three, 0, (1 - 2 * side, 0)
    )
    start_halos()
    near(2)
    loop(lambda offset: [far(offset + 2 * k) for k in range(4)], lambda turn: 4 + turn)(1)
    third_copy.wait_recv()
    loop(lambda offset: [far(offset + 2 * k) for k in range(7)], lambda turn: turn - 1)(1)
    near(-3)

    answers = None
    for part in range(8):
        slot_rows = lax.broadcasted_iota(jnp.int32, (256, 1024), 0) + part * 256
        chosen = jnp.where(slot_rows == slot, 1.0, 0.0).astype(BF)
        gained = jnp.concatenate(
            [
                jnp.where(
                    slot_eight < before[block : block + 1],
                    node_total[128 * block : 128 * (block + 1), :],
                    0.0,
                )
                for block in (2 * part, 2 * part + 1)
            ],
            axis=0,
        )
        high, mid, low = split_three(gained)
        stacked = jnp.concatenate([high, mid, low, jnp.zeros_like(low)], axis=1).astype(BF)
        added = lax.dot_general(stacked, chosen, (((0,), (0,)), ((), ())), preferred_element_type=F32)
        answers = added if answers is None else answers + added
    found = answers[0:8] + answers[8:16] + answers[16:24]
    moved = cross_rows(spots, [found[c : c + 1] for c in range(3)])
    for c in range(3):
        result = (moved[c] - found[3 + c : 4 + c]) * SCALE
        even = jnp.concatenate([result[:, 128 * k : 128 * (k + 1)] for k in range(8)], axis=0)
        odd = pltpu.roll(even, 64, 1)
        own_nodes[c] = jnp.concatenate(
            [(even, odd)[r % 2][r // 2 : r // 2 + 1] for r in range(16)], axis=0
        )
    shared = [
        send(own_nodes, far_nodes.at[k], send_node, recv_node, k, peer)
        for k, peer in enumerate([(0, -1), (-1, 0), (1, 0), (-1, -1), (1, -1)])
    ]

    results = [
        pltpu.make_async_copy(source, target, sem_out.at[k])
        for k, (source, target) in enumerate(
            [(own_nodes, own_nodes_to), (velocity_out, velocity_to), (stretch_out, stretch_to)]
        )
    ]
    results[0].start()
    loop(lambda offset: near(offset, False), lambda turn: 2 * turn - 1)(3)

    spin = [own[c : c + 1] for c in range(3)]
    sums = jnp.transpose(total[...])
    sums = sums[0:40] + sums[40:80] + sums[80:120]
    plain = [sums[k : k + 1] for k in range(6)]
    turned = [[sums[8 + 8 * c + k : 9 + 8 * c + k] for k in range(6)] for c in range(3)]
    heavy = [sums[32 + k : 33 + k] for k in range(6)]
    mixed = [
        weight * plain[k]
        + heavy[k]
        - 2.0 * (place[0] * turned[0][k] + place[1] * turned[1][k] + place[2] * turned[2][k])
        for k in range(6)
    ]
    live = grid * 256 + lax.broadcasted_iota(jnp.int32, (1, 256), 1) < counts[wake]
    factor = jnp.where(live, SCALE, 0.0)
    swept = cross_rows(place, mixed[0:3])
    bent_own = cross_rows(place, plain[0:3])
    along = spin[0] * place[0] + spin[1] * place[1] + spin[2] * place[2]
    pulled = [spin[0] * turned[0][k] + spin[1] * turned[1][k] + spin[2] * turned[2][k] for k in range(6)]
    bent_far = cross_rows(place, pulled[0:3])
    lifted = cross_rows(spin, mixed[0:3])
    for c in range(3):
        velocity_out[c : c + 1, :] = (swept[c] - mixed[3 + c]) * factor
        bent = along * (bent_own[c] - plain[3 + c]) - (bent_far[c] - pulled[3 + c])
        stretch_out[c : c + 1, :] = (lifted[c] - 3.0 * bent) * factor

    results[1].start()
    results[2].start()
    for copy in shared:
        copy.wait()
    finish_halos()
    for copy in results:
        copy.wait()
    for copy in first + second + [third_copy]:
        copy.wait_send()


ANY = pl.BlockSpec(memory_space=pltpu.HBM)
SCALAR = pl.BlockSpec(memory_space=pltpu.SMEM)


def gather_and_sum(counts, place, spin, core, node_place, node_block, flow, sections):
    dma = pltpu.SemaphoreType.DMA
    return pl.pallas_call(
        gather_kernel,
        out_shape=[
            jax.ShapeDtypeStruct((3, 256), F32),
            jax.ShapeDtypeStruct((3, 256), F32),
            jax.ShapeDtypeStruct((3, 16, 128), F32),
            jax.ShapeDtypeStruct((5, 3, 16, 128), F32),
            jax.ShapeDtypeStruct((5, 8, BUFFER), F32),
            jax.ShapeDtypeStruct((5, 16, 128), F32),
            jax.ShapeDtypeStruct((5, 16, 128), F32),
            jax.ShapeDtypeStruct((8, BUFFER), jnp.int32),
            jax.ShapeDtypeStruct((16, 128), jnp.int32),
            jax.ShapeDtypeStruct((16, 128), jnp.int32),
        ],
        in_specs=[SCALAR] + [ANY] * 7,
        out_specs=[ANY] * 10,
        scratch_shapes=[
            pltpu.VMEM((3, 256), F32),
            pltpu.VMEM((3, 256), F32),
            pltpu.VMEM((3, 16, 128), F32),
            pltpu.VMEM((NW // 2, 2, 8, PB), F32),
            pltpu.VMEM((3, 3, 256), F32),
            pltpu.VMEM((3, 1024), F32),
            pltpu.VMEM((1, 1024), jnp.int32),
            pltpu.VMEM((NW * 128, 48), BF),
            pltpu.VMEM((256, 48), BF),
            pltpu.VMEM((256, 128), F32),
            pltpu.VMEM((NW * 128, 8), F32),
            dma((5,)),
            dma((NG - 1,)),
            dma((NG - 1,)),
            dma((NG - 1,)),
            dma((NG - 1,)),
            dma((1,)),
            dma((1,)),
            dma((16,)),
            dma((16,)),
            dma((5,)),
            dma((5,)),
            dma((3,)),
        ],
        compiler_params=pltpu.CompilerParams(
            collective_id=0, has_side_effects=True, vmem_limit_bytes=LIMIT
        ),
    )(counts, place, spin, core, node_place, node_block, flow, sections)


TILES = 130
BUFFER = 16640 + 256


def sweep_kernel(
    flow, sections, viscosity, rows_halo, left_halo, right_halo, kind_rows, kind_left, kind_right,
    own_nodes_in, far_nodes_in, velocity, stretch, out, velocity_out, stretch_out,
    own_nodes, far_nodes, rows_in, kind, first, second, rates, rows_out, nodes, sem_in, sem_out, sem_small,
):
    fields = 5
    wake = lax.axis_index("wake")
    grid = lax.axis_index("grid")
    own_rows, halo_rows = pl.ds(0, 16), pl.ds(16, 8)
    middle, before, after = pl.ds(256, 16384), pl.ds(128, 128), pl.ds(16640, 128)
    kinds = [
        pltpu.make_async_copy(source, target, sem_in.at[4 * fields + k])
        for k, (source, target) in enumerate(
            [
                (sections, kind.at[own_rows, middle]),
                (kind_rows, kind.at[halo_rows, :]),
                (kind_left, kind.at[own_rows, before]),
                (kind_right, kind.at[own_rows, after]),
            ]
        )
    ]
    def incoming(f):
        return [
            pltpu.make_async_copy(source, target, sem_in.at[4 * f + k])
            for k, (source, target) in enumerate(
                [
                    (flow.at[f], rows_in.at[f, own_rows, middle]),
                    (rows_halo.at[f], rows_in.at[f, halo_rows, :]),
                    (left_halo.at[f], rows_in.at[f, own_rows, before]),
                    (right_halo.at[f], rows_in.at[f, own_rows, after]),
                ]
            )
        ]

    def outgoing(f, half):
        return pltpu.make_async_copy(
            rows_out.at[f, :, pl.ds(256 + 8192 * half, 8192)],
            out.at[f, :, pl.ds(8192 * half, 8192)],
            sem_out.at[2 * f + half],
        )

    for copy in kinds + incoming(0):
        copy.start()
    small = [
        pltpu.make_async_copy(source, target, sem_small.at[k])
        for k, (source, target) in enumerate(
            [
                (own_nodes_in, own_nodes),
                (far_nodes_in, far_nodes),
                (velocity, velocity_out),
                (stretch, stretch_out),
            ]
        )
    ]
    for copy in small:
        copy.start()
    for copy in small[0:2]:
        copy.wait()

    lane = lax.broadcasted_iota(jnp.int32, (24, 128), 1)
    row = lax.broadcasted_iota(jnp.int32, (24, 128), 0)
    is_first, is_last = lane == 0, lane == 127
    inside_rows = ((row < 20) | (wake > 0)) & ((row < 16) | (row >= 20) | (wake < NW - 1))
    lane8 = lax.broadcasted_iota(jnp.int32, (8, 128), 1)
    row8 = lax.broadcasted_iota(jnp.int32, (8, 128), 0)

    for c in range(3):
        def with_next(rows, column):
            return jnp.where(lane8 == 64, jnp.broadcast_to(column, (8, 128)), rows)

        halo = jnp.where(row8 < 4, far_nodes[1, c, 0:8], far_nodes[2, c, 8:16])
        halo_next = jnp.where(row8 < 4, far_nodes[3, c, 0:8], far_nodes[4, c, 8:16])
        parts = [
            with_next(own_nodes[c, 0:8], far_nodes[0, c, 0:8, 0:1]),
            with_next(own_nodes[c, 8:16], far_nodes[0, c, 8:16, 0:1]),
            with_next(halo, halo_next[:, 0:1]),
        ]
        nodes[c] = jnp.where(inside_rows, jnp.concatenate(parts, axis=0), 0.0)

    for copy in kinds:
        copy.wait()

    tile_lanes = lambda t: pl.ds(t * 128, 128)

    def field(f, done):
        for copy in incoming(f):
            copy.wait()

        @pl.when(f + 1 < fields)
        def _():
            for copy in incoming(f + 1):
                copy.start()

        rows_in[f, 16:24, 256:16640] = jnp.where(
            inside_rows[16:24, 0:1], rows_in[f, 16:24, 256:16640], 0.0
        )
        for start, edge in ((128, grid == 0), (16640, grid == NG - 1)):
            keep = inside_rows & jnp.logical_not(edge)
            rows_in[f, :, start : start + 128] = jnp.where(keep, rows_in[f, :, start : start + 128], 0.0)
        @pl.when((f >= 1) & (f <= 3))
        def _():
            given = nodes[jnp.clip(f - 1, 0, 2)]
            for k in range(65):
                start = 256 + 256 * k
                column = jnp.broadcast_to(given[:, k : k + 1], (24, 128))
                if k == 64:
                    column = jnp.where(grid == NG - 1, 0.0, column)
                rows_in[f, :, start : start + 128] = jnp.where(
                    is_first, column, rows_in[f, :, start : start + 128]
                )

        def sweep(load, finish):
            here = load(1)
            last_right, right, left = pltpu.roll(load(0), 1, 1), pltpu.roll(here, 1, 1), pltpu.roll(here, 127, 1)
            for t in range(1, TILES + 1):
                following = load(t + 1)
                next_right = pltpu.roll(following, 1, 1)
                next_left = pltpu.roll(following, 127, 1)
                across = jnp.where(is_first, last_right, right) + jnp.where(is_last, next_left, left)
                along = pltpu.roll(here, 1, 0) + pltpu.roll(here, 23, 0)
                finish(t, here, across + along)
                last_right, here, right, left = right, following, next_right, next_left

        def finish_first(t, here, beside):
            name = kind[:, tile_lanes(t)]
            rate = jnp.where(
                name == 0, viscosity[0, f], jnp.where(name == 1, viscosity[1, f], viscosity[2, f])
            )
            if t == 1:
                rate = jnp.where(grid > 0, rate, 0.0)
            if t == TILES:
                rate = jnp.where(grid < NG - 1, rate, 0.0)
            rate = jnp.concatenate([rate[0:16], jnp.where(inside_rows[16:24], rate[16:24], 0.0)], axis=0)
            rates[:, tile_lanes(t)] = rate
            first[:, tile_lanes(t)] = here + rate * (beside - 4.0 * here)

        def finish_second(t, here, beside):
            second[:, tile_lanes(t)] = here + rates[:, tile_lanes(t)] * (beside - 4.0 * here)

        def finish_third(t, here, beside):
            rows_out[f, :, tile_lanes(t)] = (here + rates[:, tile_lanes(t)] * (beside - 4.0 * here))[0:16]
            if t == 65:
                outgoing(f, 0).start()

        sweep(lambda t: rows_in[f, :, tile_lanes(t)], finish_first)
        sweep(lambda t: first[:, tile_lanes(t)], finish_second)
        sweep(lambda t: second[:, tile_lanes(t)], finish_third)
        outgoing(f, 1).start()
        return done

    lax.fori_loop(0, fields, field, 0)
    for f in range(fields):
        outgoing(f, 0).wait()
        outgoing(f, 1).wait()
    for copy in small[2:4]:
        copy.wait()


def sweep_fields(*arrays):
    dma = pltpu.SemaphoreType.DMA
    return pl.pallas_call(
        sweep_kernel,
        out_shape=[
            jax.ShapeDtypeStruct((5, 16, 16384), F32),
            jax.ShapeDtypeStruct((3, 256), F32),
            jax.ShapeDtypeStruct((3, 256), F32),
        ],
        in_specs=[ANY, ANY, SCALAR] + [ANY] * 10,
        out_specs=[ANY] * 3,
        scratch_shapes=[
            pltpu.VMEM((3, 16, 128), F32),
            pltpu.VMEM((5, 3, 16, 128), F32),
            pltpu.VMEM((5, 24, BUFFER), F32),
            pltpu.VMEM((24, BUFFER), jnp.int32),
            pltpu.VMEM((24, BUFFER), F32),
            pltpu.VMEM((24, BUFFER), F32),
            pltpu.VMEM((24, BUFFER), F32),
            pltpu.VMEM((5, 16, BUFFER), F32),
            pltpu.VMEM((3, 24, 128), F32),
            dma((24,)),
            dma((10,)),
            dma((4,)),
        ],
        compiler_params=pltpu.CompilerParams(vmem_limit_bytes=LIMIT),
    )(*arrays)


def on_device(
    flow,
    section_map,
    viscosity,
    particle_position,
    particle_strength,
    particle_core,
    shed_counts,
    node_position,
    node_block,
):
    (
        velocity, stretch, own_nodes, far_nodes, rows_halo, left_halo, right_halo, kind_rows, kind_left, kind_right,
    ) = gather_and_sum(
        shed_counts,
        particle_position,
        particle_strength,
        particle_core.reshape(1, 256),
        node_position,
        node_block.reshape(1, 1024),
        flow,
        section_map,
    )
    field, velocity, stretch = sweep_fields(
        flow, section_map, viscosity, rows_halo, left_halo, right_halo, kind_rows, kind_left, kind_right,
        own_nodes, far_nodes, velocity, stretch,
    )
    return (field, velocity, stretch)


def solution(mesh):
    return jax.shard_map(
        on_device,
        mesh=mesh,
        in_specs=(
            P(None, "wake", "grid"),
            P("wake", "grid"),
            P(),
            P(None, ("wake", "grid")),
            P(None, ("wake", "grid")),
            P(("wake", "grid")),
            P(),
            P(None, ("wake", "grid")),
            P(("wake", "grid"), None),
        ),
        out_specs=(P(None, "wake", "grid"), P(None, ("wake", "grid")), P(None, ("wake", "grid"))),
        check_vma=False,
    )
```
